32 devices in a mesh: gx: 4 (over x, core), gy: 8 (over z, y).
Axes of the slice: x: 2, y: 2, z: 4, core: 2. Of those that a mesh axis runs over, the one named last changes fastest.
Arguments:
- fields: float32 [4, 64, 128, 128], P(None, 'gx', 'gy'), may hold values from -6 to 6
- lift: float32 [32, 4], replicated, may hold values from -3 to 3
- lift_bias: float32 [32], replicated, may hold values from -3 to 3
- spectral_in: float32 [256, 2, 8, 32, 64], P(('gx', 'gy')), may hold values from -0.03125 to 0.03125
- bypass_in: float32 [64, 32], replicated, may hold values from -1 to 1
- bias_in: float32 [64], replicated, may hold values from -3 to 3
- spectral_out: float32 [256, 2, 8, 64, 32], P(('gx', 'gy')), may hold values from -0.046875 to 0.046875
- bypass_out: float32 [32, 64], replicated, may hold values from -0.75 to 0.75
- bias_out: float32 [32], replicated, may hold values from -3 to 3
- project: float32 [4, 32], replicated, may hold values from -1 to 1
- project_bias: float32 [4], replicated, may hold values from -3 to 3
Outputs:
- result: float32 [4, 64, 128, 128], P(None, 'gx', 'gy')
The draws below stay inside these ranges and needn't reach their ends.
All inputs are finite; a program needn't handle non-finite values.
Results may differ from the reference program's by a relative error of at most 0.000058.
Values sent between devices are 32-bit elements; how exact they have to be, the bound alone decides.
A program may use at most 64 MiB of HBM per device.

```python
import math
import jax
import jax.numpy as jnp
from jax import lax

CIN = 4
C1 = 32
C2 = 64
KX = 16
KY = 16
KZ = 8
NZ = 128
NX = 64
NY = 128


def wave_table(length, count, offset):
    places = jnp.arange(length, dtype=jnp.int32)
    frequency = jnp.arange(count, dtype=jnp.int32) - offset
    turns = places[:, None] * frequency[None, :] % length
    angle = turns.astype(jnp.float32) * (2.0 * math.pi / length)
    return (jnp.cos(angle), jnp.sin(angle), frequency.astype(jnp.float32))


def draw_fields(key, part):
    key_real = jax.random.fold_in(key, 101)
    key_imag = jax.random.fold_in(key, 202)
    key_rough = jax.random.fold_in(key, 303)
    x_cos, x_sin, freq_x = wave_table(NX, 2 * KX, KX)
    y_cos, y_sin, freq_y = wave_table(NY, 2 * KY, KY)
    z_cos, z_sin, freq_z = wave_table(NZ, 2 * KZ, 0)
    ratio = (freq_x[:, None, None] / KX) ** 2 + (freq_y[None, :, None] / KY) ** 2 + (freq_z[None, None, :] / KZ) ** 2
    amplitude = 1.0 / (1.0 + 2.0 * ratio)
    real_coef = jax.random.normal(key_real, (CIN, 2 * KX, 2 * KY, 2 * KZ), jnp.float32) * amplitude[None]
    imag_coef = jax.random.normal(key_imag, (CIN, 2 * KX, 2 * KY, 2 * KZ), jnp.float32) * amplitude[None]
    highest = lax.Precision.HIGHEST
    real_x = jnp.einsum('cijk,xi->cxjk', real_coef, x_cos, precision=highest) - jnp.einsum('cijk,xi->cxjk', imag_coef, x_sin, precision=highest)
    imag_x = jnp.einsum('cijk,xi->cxjk', real_coef, x_sin, precision=highest) + jnp.einsum('cijk,xi->cxjk', imag_coef, x_cos, precision=highest)
    real_y = jnp.einsum('cxjk,yj->cxyk', real_x, y_cos, precision=highest) - jnp.einsum('cxjk,yj->cxyk', imag_x, y_sin, precision=highest)
    imag_y = jnp.einsum('cxjk,yj->cxyk', real_x, y_sin, precision=highest) + jnp.einsum('cxjk,yj->cxyk', imag_x, y_cos, precision=highest)
    smooth = jnp.einsum('cxyk,zk->cxyz', real_y, z_cos, precision=highest) - jnp.einsum('cxyk,zk->cxyz', imag_y, z_sin, precision=highest)
    smooth = smooth / jnp.sqrt(jnp.sum(amplitude * amplitude))
    rough = jax.random.normal(key_rough, (CIN, NX, NY, NZ), jnp.float32)
    value = smooth + 0.5 * rough
    return jnp.clip(value, -6.0, 6.0)


def levels(rng, dims, pieces, least, top_value):
    level = 1.0
    for position, blocks in pieces:
        draws = jax.random.uniform(jax.random.fold_in(jax.random.fold_in(rng, 6), position), (blocks,), jnp.float32, least / len(pieces), top_value / len(pieces))
        level = level * jnp.repeat(jnp.exp(draws), dims[position] // blocks).reshape((-1,) + (1,) * (len(dims) - 1 - position))
    return level


def gaussian(own_key, extent, deviation, limit, split=(), held_as=jnp.bfloat16):
    values = jax.random.normal(own_key, extent, jnp.float32) * deviation
    if len(split) > 0:
        values = levels(own_key, extent, split, -0.22, 0.18) * values
    return jnp.clip(values, min=-limit, max=limit).astype(held_as)


def setup_inputs(seed: int = 0) -> dict:
    seeds = jax.random.split(jax.random.key(seed), 12)
    return {
        "fields": draw_fields(jax.random.fold_in(seeds[11], 71), 0),
        "lift": gaussian(seeds[1], (C1, CIN), CIN ** -0.5, 3.0, (), jnp.float32),
        "lift_bias": gaussian(seeds[2], (C1,), 0.5, 3.0, (), jnp.float32),
        "spectral_in": gaussian(seeds[3], (KX * KY, 2, KZ, C1, C2), (2 * C1 * NX * NY * NZ // (KX * KY * KZ)) ** -0.5, 0.03125, ((0, 32),), jnp.float32),
        "bypass_in": gaussian(seeds[4], (C2, C1), C1 ** -0.5, 1.0, (), jnp.float32),
        "bias_in": gaussian(seeds[5], (C2,), 0.5, 3.0, (), jnp.float32),
        "spectral_out": gaussian(seeds[6], (KX * KY, 2, KZ, C2, C1), (2 * C2 * NX * NY * NZ // (4 * KX * KY * KZ)) ** -0.5, 0.046875, ((0, 32),), jnp.float32),
        "bypass_out": gaussian(seeds[7], (C1, C2), C2 ** -0.5, 0.75, (), jnp.float32),
        "bias_out": gaussian(seeds[8], (C1,), 0.5, 3.0, (), jnp.float32),
        "project": gaussian(seeds[9], (CIN, C1), C1 ** -0.5, 1.0, (), jnp.float32),
        "project_bias": gaussian(seeds[10], (CIN,), 0.5, 3.0, (), jnp.float32),
    }


def product(formula, left, right):
    return jnp.einsum(formula, left, right, precision=lax.Precision.HIGHEST)

def tables(places, length, count, centered):
    frequency = jnp.arange(count, dtype=jnp.int32)
    if centered:
        frequency = jnp.where(frequency < count // 2, frequency, frequency - count)
    turns = places.astype(jnp.int32)[:, None] * frequency[None, :] % length
    angle = turns.astype(jnp.float32) * (2.0 * math.pi / length)
    return (jnp.cos(angle), jnp.sin(angle))

def forward(field, x_places, y_places, x_length, y_length, scale):
    z_length = field.shape[3]
    z_cos, z_sin = tables(jnp.arange(z_length, dtype=jnp.int32), z_length, KZ, False)
    real_part = product('cxyz,zk->cxyk', field, z_cos)
    imag_part = -product('cxyz,zk->cxyk', field, z_sin)
    y_cos, y_sin = tables(y_places, y_length, KY, True)
    real_next = product('cxyk,yj->cxjk', real_part, y_cos) + product('cxyk,yj->cxjk', imag_part, y_sin)
    imag_next = product('cxyk,yj->cxjk', imag_part, y_cos) - product('cxyk,yj->cxjk', real_part, y_sin)
    x_cos, x_sin = tables(x_places, x_length, KX, True)
    real_last = product('cxjk,xi->ijkc', real_next, x_cos) + product('cxjk,xi->ijkc', imag_next, x_sin)
    imag_last = product('cxjk,xi->ijkc', imag_next, x_cos) - product('cxjk,xi->ijkc', real_next, x_sin)
    stacked = jnp.stack([real_last, imag_last], axis=2)
    return stacked.reshape((KX * KY, 2, KZ, stacked.shape[4])) * scale

def mix_modes(spectrum, weights):
    real_in = spectrum[:, 0]
    imag_in = spectrum[:, 1]
    real_weight = weights[:, 0]
    imag_weight = weights[:, 1]
    real_out = product('mkc,mkcd->mkd', real_in, real_weight) - product('mkc,mkcd->mkd', imag_in, imag_weight)
    imag_out = product('mkc,mkcd->mkd', real_in, imag_weight) + product('mkc,mkcd->mkd', imag_in, real_weight)
    return jnp.stack([real_out, imag_out], axis=1)

def inverse(spectrum, x_places, y_places, x_length, y_length, z_length, scale):
    grid = spectrum.reshape((KX, KY, 2, KZ, spectrum.shape[3]))
    real_part = grid[:, :, 0]
    imag_part = grid[:, :, 1]
    x_cos, x_sin = tables(x_places, x_length, KX, True)
    real_next = product('ijkc,xi->xjkc', real_part, x_cos) - product('ijkc,xi->xjkc', imag_part, x_sin)
    imag_next = product('ijkc,xi->xjkc', real_part, x_sin) + product('ijkc,xi->xjkc', imag_part, x_cos)
    y_cos, y_sin = tables(y_places, y_length, KY, True)
    real_last = product('xjkc,yj->xykc', real_next, y_cos) - product('xjkc,yj->xykc', imag_next, y_sin)
    imag_last = product('xjkc,yj->xykc', real_next, y_sin) + product('xjkc,yj->xykc', imag_next, y_cos)
    z_cos, z_sin = tables(jnp.arange(z_length, dtype=jnp.int32), z_length, KZ, False)
    return (product('xykc,zk->cxyz', real_last, z_cos) - product('xykc,zk->cxyz', imag_last, z_sin)) * scale

def reference(fields, lift, lift_bias, spectral_in, bypass_in, bias_in, spectral_out, bypass_out, bias_out, project, project_bias):
    back = math.sqrt(2.0 / (KX * KY * KZ))
    lifted = product('dc,cxyz->dxyz', lift, fields) + lift_bias[:, None, None, None]
    full_x = jnp.arange(NX, dtype=jnp.int32)
    full_y = jnp.arange(NY, dtype=jnp.int32)
    half_x = jnp.arange(NX // 2, dtype=jnp.int32)
    half_y = jnp.arange(NY // 2, dtype=jnp.int32)
    spectrum = forward(lifted, full_x, full_y, NX, NY, 1.0 / math.sqrt(NX * NY * NZ))
    mixed = mix_modes(spectrum, spectral_in)
    pooled = lifted.reshape((C1, NX // 2, 2, NY // 2, 2, NZ)).mean(axis=(2, 4))
    coarse = jax.nn.gelu(inverse(mixed, 2 * half_x, 2 * half_y, NX, NY, NZ, back) + product('ec,cxyz->exyz', bypass_in, pooled) + bias_in[:, None, None, None], approximate=False)
    spectrum = forward(coarse, half_x, half_y, NX // 2, NY // 2, 1.0 / math.sqrt(NX * NY * NZ / 4.0))
    mixed = mix_modes(spectrum, spectral_out)
    narrow = product('dc,cxyz->dxyz', bypass_out, coarse)
    widened = jnp.repeat(jnp.repeat(narrow, 2, axis=1), 2, axis=2)
    fine = jax.nn.gelu(inverse(mixed, full_x, full_y, NX, NY, NZ, back) + widened + bias_out[:, None, None, None], approximate=False)
    return product('oc,cxyz->oxyz', project, fine + lifted) + project_bias[:, None, None, None]
```

```python
import functools
import math

import jax
import jax.numpy as jnp
import numpy as np
from jax import lax
from jax.experimental import pallas as pl
from jax.experimental.pallas import tpu as pltpu
from jax.sharding import PartitionSpec as P

KX = 16
KY = 16
KZ = 8
YB = 8
LB = 128
GROUP = 4
F32 = jnp.float32
BF16 = jnp.bfloat16
MESH = pl.DeviceIdType.MESH


def freq(count):
    f = np.arange(count)
    return np.where(f < count // 2, f, f - count)


def halves(table):
    high = table.astype(np.float32).astype(jnp.bfloat16)
    low = (table - high.astype(np.float64)).astype(np.float32).astype(jnp.bfloat16)
    return np.stack([high, low])


def stacked(table):
    high, low = halves(table)
    return np.concatenate([high, high, low], axis=0)


def angles(places, frequency, length):
    turns = np.mod(places[:, None] * frequency[None, :], length)
    return turns * (2.0 * math.pi / length)


def z_table(z_length):
    ang = angles(np.arange(z_length), np.arange(KZ), z_length)
    table = np.zeros((YB, z_length, 2, YB, KZ))
    for y in range(YB):
        table[y, :, 0, y] = np.cos(ang)
        table[y, :, 1, y] = -np.sin(ang)
    return table.reshape(YB * z_length, LB)


def y_table(blocks, cells, length, groups):
    per = KY // groups
    frequency = freq(KY)
    out = np.zeros((blocks, cells // YB, 2, YB, KZ, groups, LB))
    for b in range(blocks):
        ang = angles(b * cells + np.arange(cells), frequency, length)
        for y in range(cells):
            for j in range(KY):
                c, s = np.cos(ang[y, j]), np.sin(ang[y, j])
                for k in range(KZ):
                    re = (j % per) * KZ + k
                    im = per * KZ + re
                    at = (b, y // YB)
                    out[at + (0, y % YB, k, j // per, re)] = c
                    out[at + (1, y % YB, k, j // per, re)] = s
                    out[at + (0, y % YB, k, j // per, im)] = -s
                    out[at + (1, y % YB, k, j // per, im)] = c
    return out.reshape(blocks, cells // YB * LB, groups * LB)


def x_angles(blocks, cells, length):
    return angles(np.arange(blocks * cells), freq(KX), length).reshape(blocks, cells, KX)


def split(value):
    high = value.astype(BF16)
    return high, (value - high.astype(F32)).astype(BF16)


def mul(a, b):
    return jnp.dot(a, b, preferred_element_type=F32)


def tall(a):
    return jnp.concatenate([a[0], a[1], a[0]], axis=1)


def deep(a):
    return jnp.concatenate([a[0], a[1], a[0]], axis=0)


def wide(a):
    return jnp.concatenate([a[0], a[0], a[1]], axis=1)


def mul3(a, b):
    return mul(a[0], b[0]) + (mul(a[1], b[0]) + mul(a[0], b[1]))


def gelu(v):
    return (0.5 * v) * (1.0 + lax.erf(v * math.sqrt(0.5)))


def kernel(
    A, B, cells_x, scale1, scale2, gain,
    f_ref, lift_ref, lbias_ref, byp_ref, bi_ref, wo_ref, bo_ref, pr_ref, pb_ref,
    tzf_ref, tzi_hbm, w1_hbm, w2_hbm, tx_hbm, yf1_hbm, yfc_hbm, yic_hbm, yi2_hbm, xf_hbm, xi_hbm, xo_hbm,
    o_ref,
    tzi_ref, w1, w2, tx, yf1, yfc, yic, yi2, xf, xi, xo,
    buf1, r1, mx, mt1, g1, yall, pg, pk_ref, vx, zc, vn, buf2, r3, ag2, vf, nar, fk_ref, t16, bd, bpq,
    csem, ssem, rsem,
):
    a = lax.axis_index("gx")
    b = lax.axis_index("gy")
    me = a * B + b
    IL = KX // A
    H = B // IL
    J = KY // H
    N = A * B
    X = A // 2
    CIN, C1 = lift_ref.shape
    C2 = wo_ref.shape[1]
    CQ = C2 // A
    CG = CQ // 8
    hx = cells_x // 2
    HX = hx * A
    G1 = GROUP * C2 // CQ
    own_g = b // H
    own_h = lax.rem(b, H)
    core = lax.rem(a, 2)
    sib = a + 1 - 2 * core
    mates = [lax.rem(a + 2 * s, A) for s in range(1, X)]

    pairs = [
        (tx_hbm.at[a], tx), (yf1_hbm.at[b], yf1), (w1_hbm, w1), (yic_hbm.at[b], yic), (xi_hbm, xi), (tzi_hbm, tzi_ref),
        (xf_hbm, xf), (yfc_hbm.at[b], yfc), (w2_hbm, w2), (yi2_hbm.at[b], yi2), (xo_hbm.at[a], xo),
    ]
    loads = [pltpu.make_async_copy(src, dst, csem.at[k]) for k, (src, dst) in enumerate(pairs)]
    l_tx, l_yf1, l_w1, l_yic, l_xi, l_tzi, l_xf, l_yfc, l_w2, l_yi2, l_xo = loads
    for load in loads:
        load.start()

    barrier = pltpu.get_barrier_semaphore()
    for step in range(1, N):
        peer = lax.rem(me + step, N)
        pl.semaphore_signal(
            barrier, inc=1, device_id=(peer // B, lax.rem(peer, B)), device_id_type=MESH
        )

    lane = lax.broadcasted_iota(jnp.int32, (1, LB), 1)
    sign_f = jnp.where(lane < LB // 2, 1.0, -1.0).astype(F32)

    def rot_f(v):
        return pltpu.roll(v, LB // 2, 1) * sign_f

    def rot_i(v):
        return pltpu.roll(v, LB // 2, 1) * -sign_f

    sends = []
    used = [0]

    def remote(source, target, slot, device):
        copy = pltpu.make_async_remote_copy(
            src_ref=source, dst_ref=target, send_sem=ssem.at[used[0]], recv_sem=rsem.at[slot],
            device_id=device, device_id_type=MESH,
        )
        used[0] += 1
        copy.start()
        sends.append(copy)

    def arrive(target, slot):
        pltpu.make_async_remote_copy(
            src_ref=target, dst_ref=target, send_sem=ssem.at[0], recv_sem=rsem.at[slot],
            device_id=(sib, b), device_id_type=MESH,
        ).wait_recv()

    def at(index):
        return (index // B, lax.rem(index, B))

    S_EXP1, S_RED, S_EXP2, S_POOL, S_Y = N, 2 * N, 3 * N, 4 * N, 4 * N + A

    width = tzi_ref.shape[1]
    zs = []
    for ch in range(2):
        zs.append(mul(tall(split(f_ref[:, ch * width:(ch + 1) * width])), tzf_ref[...]))
    l_tx.wait()
    us = []
    for z in zs:
        us.append(mul3((tx[0], tx[1]), split(jnp.concatenate([z, rot_f(z)], axis=0))))
    l_yf1.wait()
    part = mul3(split(jnp.concatenate(us, axis=1)), (yf1[0], yf1[1]))
    for i in range(KX):
        for h in range(H):
            buf1[i * H + h] = part[i * CIN:(i + 1) * CIN, h * LB:(h + 1) * LB]
    r1[me] = buf1[me]
    pl.semaphore_wait(barrier, N - 1)

    for step in range(1, N):
        peer = lax.rem(me + step, N)
        remote(buf1.at[peer], r1.at[me], me, at(peer))

    zn = width // YB
    for x in range(hx):
        both = f_ref[2 * x * CIN:(2 * x + 1) * CIN] + f_ref[(2 * x + 1) * CIN:(2 * x + 2) * CIN]
        pieces = [
            both[:, 2 * y * zn:(2 * y + 1) * zn] + both[:, (2 * y + 1) * zn:(2 * y + 2) * zn]
            for y in range(YB)
        ]
        pg[a, x * CIN:(x + 1) * CIN] = jnp.concatenate(pieces, axis=1) * 0.25

    def near_send(buffer, slot):
        for peer in mates + [sib]:
            remote(buffer.at[a], buffer.at[a], slot + a, (peer, b))

    def near_forward(buffer, slot):
        for peer in mates:
            arrive(buffer.at[peer], slot + peer)
            remote(buffer.at[peer], buffer.at[peer], slot + peer, (sib, b))

    def near_finish(buffer, slot):
        arrive(buffer.at[sib], slot + sib)
        for peer in mates:
            other = peer + 1 - 2 * core
            arrive(buffer.at[other], slot + other)

    near_send(pg, S_POOL)

    l_w1.wait()
    mx[...] = jnp.zeros_like(mx)
    mx[0:CIN, :C1] = lift_ref[...]
    mx[CIN:CIN + 1, :C1] = lbias_ref[...]
    mx[CIN + 1:CIN + 2, :C1] = bo_ref[...]
    lift8 = jnp.concatenate([mx[0:8, :C1]], axis=0)
    columns = mx[...].T[:C1]
    bo_col = columns[:, CIN + 1:CIN + 2]

    def left16(matrix, bias):
        n = matrix.shape[1]
        high, low = split(matrix[0:CIN])
        b0 = bias.astype(BF16)
        rest = bias - b0.astype(F32)
        b1 = rest.astype(BF16)
        b2 = (rest - b1.astype(F32)).astype(BF16)
        mx[...] = jnp.zeros_like(mx)
        mx[0:CIN, :n] = high.astype(F32)
        mx[CIN:2 * CIN, :n] = high.astype(F32)
        mx[2 * CIN:3 * CIN, :n] = low.astype(F32)
        for row, value in enumerate((b0, b1, b2)):
            mx[3 * CIN + row:3 * CIN + row + 1, :n] = value.astype(F32)
        return mx[...].T[:n, :16].astype(BF16)

    highest = lax.Precision.HIGHEST
    m = jnp.dot(lift8, byp_ref[...], precision=highest, preferred_element_type=F32)
    bp16 = left16(m, m[CIN:CIN + 1] + bi_ref[...])
    m = lax.dot_general(
        lift8, pr_ref[...], (((1,), (1,)), ((), ())), precision=highest, preferred_element_type=F32
    )
    pl16 = left16(m, m[CIN:CIN + 1] + pb_ref[...])
    t16[...] = jnp.ones_like(t16)

    def diagonal(value, count):
        rows, cols = value.shape
        bd[...] = jnp.zeros_like(bd)
        for g in range(count):
            bd[g * rows:(g + 1) * rows, g * cols:(g + 1) * cols] = value
        return bd[0:count * rows, 0:count * cols]

    bp_all = bp16.astype(F32)
    for q in range(A):
        bpq[q] = bp_all[q * CQ:(q + 1) * CQ]
    bq_bd = diagonal(bpq[a], G1).astype(BF16)
    bp_bd = diagonal(bp_all, GROUP).astype(BF16)
    pl_bd = diagonal(pl16.astype(F32), GROUP).astype(BF16)
    wo_bd = wide(split(diagonal(wo_ref[...], GROUP)))
    pr_bd = wide(split(diagonal(pr_ref[...], GROUP)))
    for step in range(1, N):
        peer = lax.rem(me + step, N)
        arrive(r1.at[peer], peer)

    def mix(st, w, width_out):
        mx[...] = jnp.zeros_like(mx)
        for j in range(J):
            for k in range(KZ):
                q = j * KZ + k
                p = J * KZ + q
                re = st[:, q:q + 1]
                im = st[:, p:p + 1]
                wr = w[j, 0, k]
                wi = w[j, 1, k]
                mx[q:q + 1, :width_out] = jnp.sum(re * wr - im * wi, axis=0, keepdims=True)
                mx[p:p + 1, :width_out] = jnp.sum(re * wi + im * wr, axis=0, keepdims=True)
        return mx[...].T[:width_out]

    s4 = jnp.sum(r1[...], axis=0) * scale1
    st = columns[:, 0:1] * s4[0:1]
    for c in range(1, CIN):
        st = st + columns[:, c:c + 1] * s4[c:c + 1]
    first = jnp.where((lane == 0) & (me == 0), gain, 0.0).astype(F32)
    st = st + columns[:, CIN:CIN + 1] * first
    mixed = mix(st, w1, C2)
    for q in range(A):
        mt1[q] = mixed[q * CQ:(q + 1) * CQ]
    g1[me] = mt1[a]

    def group_member(step):
        return own_g * H + lax.rem(own_h + step, H)

    def column(ia, ig):
        return lax.rem(a + ia, A), lax.rem(own_g + ig, IL) * H + own_h

    order = [(ia, ig) for ig in range(IL) for ia in range(A) if ia or ig]
    for ia, ig in reversed(order):
        pa, pb = column(ia, ig)
        remote(mt1.at[pa], g1.at[me], S_EXP1 + me, (pa, pb))
    for t in range(1, H):
        remote(mt1.at[a], g1.at[me], S_EXP1 + me, (a, group_member(t)))

    def fill(value):
        n = value.shape[1]
        high, low = split(value)
        t16[0:CIN, :n] = high.astype(F32)
        t16[CIN:2 * CIN, :n] = low.astype(F32)
        t16[2 * CIN:3 * CIN, :n] = high.astype(F32)
        return t16[:, :n].astype(BF16)

    near_forward(pg, S_POOL)
    for x in range(cells_x):
        fk_ref[x] = fill(f_ref[x * CIN:(x + 1) * CIN])
    near_finish(pg, S_POOL)
    for q in range(A):
        for x in range(hx):
            pk_ref[q * hx + x] = fill(pg[q, x * CIN:(x + 1) * CIN])

    for ia, ig in order:
        pa, pb = column(ia, ig)
        source = pa * B + pb
        arrive(g1.at[source], S_EXP1 + source)
        for t in range(1, H):
            remote(g1.at[source], g1.at[source], S_EXP1 + source, (a, group_member(t)))
    for t in range(1, H):
        for ia, ig in [(0, 0)] + order:
            source = lax.rem(a + ia, A) * B + lax.rem(own_g + ig, IL) * H + lax.rem(own_h + t, H)
            arrive(g1.at[source], S_EXP1 + source)

    l_yic.wait()
    rows = jnp.concatenate(
        [jnp.concatenate([g1[i * H + h] for h in range(H)], axis=1) for i in range(KX)], axis=0
    )
    y = mul3(split(rows), (yic[0], yic[1]))
    for i in range(KX):
        yall[a, i] = y[i * CQ:(i + 1) * CQ]
    near_send(yall, S_Y)

    def modes(value, rows_each):
        groups = rows_each // 8
        turned = rot_i(value)
        parts = []
        for g in range(groups):
            parts.append(jnp.concatenate([
                v[i * rows_each + g * 8:i * rows_each + g * 8 + 8] for v in (value, turned) for i in range(KX)
            ], axis=0))
        return parts

    l_xi.wait()
    table = wide((
        jnp.concatenate([xi[q, 0] for q in range(A)], axis=0),
        jnp.concatenate([xi[q, 1] for q in range(A)], axis=0),
    ))
    v = mul(table, deep(split(jnp.concatenate(modes(y, CQ), axis=1))))
    for s in range(HX // G1):
        vx[s] = jnp.concatenate([
            v[(s * G1 + xx) * 8:(s * G1 + xx) * 8 + 8, g * LB:(g + 1) * LB]
            for xx in range(G1) for g in range(CG)
        ], axis=0)

    def coarse_step(s, carry):
        v = mul(tall(split(vx[s])), tzi_ref[...])
        near = jnp.concatenate([pk_ref[s * G1 + xx] for xx in range(G1)], axis=0)
        g = split(gelu(v + mul(bq_bd, near)))
        zc[s] = mul(tall(g), tzf_ref[...])
        return carry

    l_tzi.wait()
    lax.fori_loop(0, HX // G1, coarse_step, 0)
    near_forward(yall, S_Y)

    l_xf.wait()
    l_yfc.wait()
    z = jnp.concatenate([
        jnp.concatenate([
            zc[s, xx * CQ + g * 8:xx * CQ + g * 8 + 8] for s in range(HX // G1) for xx in range(G1)
        ], axis=0) for g in range(CG)
    ], axis=1)
    z = mul(wide((xf[0], xf[1])), deep(split(z)))
    value = jnp.concatenate([
        z[i * 8:(i + 1) * 8, g * LB:(g + 1) * LB] for i in range(KX) for g in range(CG)
    ], axis=0) + rot_f(jnp.concatenate([
        z[(KX + i) * 8:(KX + i + 1) * 8, g * LB:(g + 1) * LB] for i in range(KX) for g in range(CG)
    ], axis=0))
    out = mul3(split(value), (yfc[0], yfc[1]))
    for i in range(KX):
        for h in range(H):
            buf2[i * H + h] = out[i * CQ:(i + 1) * CQ, h * LB:(h + 1) * LB]
    for step in range(1, N):
        peer = lax.rem(me + step, N)
        remote(buf2.at[peer], r3.at[me], S_RED + me, at(peer))
    r3[me] = buf2[me]

    near_finish(yall, S_Y)
    parts = []
    for q in range(A):
        parts += modes(jnp.concatenate([yall[q, i] for i in range(KX)], axis=0), CQ)
    v = mul(wide((xi[a, 0], xi[a, 1])), deep(split(jnp.concatenate(parts, axis=1))))
    for s in range(hx // GROUP):
        vn[s] = jnp.concatenate([
            v[(s * GROUP + xx) * 8:(s * GROUP + xx) * 8 + 8, g * LB:(g + 1) * LB]
            for xx in range(GROUP) for g in range(C2 // 8)
        ], axis=0)

    def narrow_step(s, carry):
        v = mul(tall(split(vn[s])), tzi_ref[...])
        near = jnp.concatenate([pk_ref[a * hx + s * GROUP + xx] for xx in range(GROUP)], axis=0)
        g = split(gelu(v + mul(bp_bd, near)))
        narrow = mul(wo_bd, deep(g))
        for xx in range(GROUP):
            nar[s * GROUP + xx] = narrow[xx * C1:(xx + 1) * C1]
        return carry

    lax.fori_loop(0, hx // GROUP, narrow_step, 0)

    l_w2.wait()
    for step in range(1, N):
        peer = lax.rem(me + step, N)
        arrive(r3.at[peer], S_RED + peer)
    sums = []
    for q in range(A):
        total = r3[q * B]
        for t in range(1, B):
            total = total + r3[q * B + t]
        sums.append(total)
    st = (jnp.concatenate(sums, axis=0) * scale2).T
    mixed = jnp.zeros((C1, LB), F32)
    for j in range(J):
        for k in range(KZ):
            q = j * KZ + k
            p = J * KZ + q
            re = st[q:q + 1]
            im = st[p:p + 1]
            wr = w2[j, 0, k]
            wi = w2[j, 1, k]
            real = jnp.sum(re * wr - im * wi, axis=1, keepdims=True)
            imag = jnp.sum(re * wi + im * wr, axis=1, keepdims=True)
            mixed = jnp.where(lane == q, real, jnp.where(lane == p, imag, mixed))
    ag2[me] = mixed

    def flip(t):
        value = b
        bit = 1
        while bit < B:
            if t & bit:
                value = value + bit - 2 * bit * lax.rem(b // bit, 2)
            bit *= 2
        return value

    def spread(source):
        for peer in mates + [sib]:
            remote(ag2.at[source], ag2.at[source], S_EXP2 + source, (peer, b))

    for t in range(B - 1, 0, -1):
        remote(ag2.at[me], ag2.at[me], S_EXP2 + me, (a, flip(t)))
    spread(me)
    for t in range(1, B):
        source = a * B + flip(t)
        arrive(ag2.at[source], S_EXP2 + source)
        spread(source)
    for t in range(B):
        for peer in mates:
            source = peer * B + flip(t)
            arrive(ag2.at[source], S_EXP2 + source)
            remote(ag2.at[source], ag2.at[source], S_EXP2 + source, (sib, b))
    for t in range(B):
        for peer in [a] + mates:
            source = (peer + 1 - 2 * core) * B + flip(t)
            arrive(ag2.at[source], S_EXP2 + source)

    l_yi2.wait()
    l_xo.wait()
    rows = jnp.concatenate(
        [jnp.concatenate([ag2[i * H + h] for h in range(H)], axis=1) for i in range(KX)], axis=0
    )
    y = mul3(split(rows), (yi2[0], yi2[1]))
    halves_y = [modes(y[:, ch * LB:(ch + 1) * LB], C1) for ch in range(2)]
    v = mul(wide((xo[0], xo[1])), deep(split(jnp.concatenate(halves_y[0] + halves_y[1], axis=1))))
    CF = C1 // 8
    for s in range(cells_x // GROUP):
        for ch in range(2):
            vf[s, ch] = jnp.concatenate([
                v[(s * GROUP + xx) * 8:(s * GROUP + xx) * 8 + 8, (ch * CF + g) * LB:(ch * CF + g + 1) * LB]
                for xx in range(GROUP) for g in range(CF)
            ], axis=0)

    def fine_step(group, carry):
        near = jnp.concatenate([fk_ref[group * GROUP + xx] for xx in range(GROUP)], axis=0)
        for ch in range(2):
            v = mul(tall(split(vf[group, ch])), tzi_ref[...])
            rows = []
            for xx in range(0, GROUP, 2):
                half = nar.at[group * (GROUP // 2) + xx // 2]
                pieces = []
                for yy in range(YB):
                    at_y = (ch * YB + yy) // 2 * zn
                    pieces.append(half[:, at_y:at_y + zn])
                rows += [jnp.concatenate(pieces, axis=1) + bo_col] * 2
            g = split(gelu(v + jnp.concatenate(rows, axis=0)))
            cols = slice(ch * width, (ch + 1) * width)
            res = mul(pr_bd, deep(g)) + mul(pl_bd, near[:, cols])
            for xx in range(GROUP):
                o_ref[group * GROUP + xx, :, cols] = res[xx * CIN:(xx + 1) * CIN]
        return carry

    lax.fori_loop(0, cells_x // GROUP, fine_step, 0)
    for copy in sends:
        copy.wait_send()


def on_device(
    A, B, fields, lift, lift_bias, spectral_in, bypass_in, bias_in, spectral_out, bypass_out,
    bias_out, proj, proj_bias,
):
    cin, xc, yc, zc = fields.shape
    C1 = lift.shape[0]
    C2 = bypass_in.shape[0]
    NX = xc * A
    NY = yc * B
    IL = KX // A
    H = B // IL
    J = KY // H
    N = A * B
    width = YB * zc
    CQ = C2 // A
    hx = xc // 2
    HX = hx * A
    G1 = GROUP * C2 // CQ
    cells = float(NX * NY * zc)
    back = math.sqrt(2.0 / (KX * KY * KZ))

    tz = z_table(zc)
    tzf = stacked(tz)
    tzi = stacked(np.ascontiguousarray(tz.T) * back)
    fine_x = x_angles(A, xc, NX)
    half_x = x_angles(A, xc // 2, NX // 2)
    eye = np.eye(cin)
    tx = np.stack([
        np.concatenate([np.kron(np.cos(fine_x[i].T), eye), np.kron(np.sin(fine_x[i].T), eye)], axis=1)
        for i in range(A)
    ])
    eye8 = np.eye(8)

    def lines(ang):
        return np.concatenate([np.kron(np.cos(ang), eye8), np.kron(np.sin(ang), eye8)], axis=1)

    xi = np.stack([lines(half_x[i]) for i in range(A)])
    xf = np.ascontiguousarray(xi.reshape(-1, xi.shape[2]).T)
    xo = np.stack([lines(fine_x[i]) for i in range(A)])
    yf1 = y_table(B, yc, NY, H)
    yfc = y_table(B, yc // 2, NY // 2, H)

    def per_device(table):
        return jnp.asarray(np.ascontiguousarray(np.swapaxes(halves(table), 0, 1)))

    tx_t = per_device(tx)
    yf1_t = per_device(yf1)
    yfc_t = per_device(yfc)
    yic_t = per_device(np.swapaxes(yfc, 1, 2))
    yi2_t = per_device(np.swapaxes(yf1, 1, 2))
    xi_t = per_device(xi)
    xo_t = per_device(xo)
    xf_t = jnp.asarray(halves(xf))

    rows = jnp.transpose(fields, (1, 0, 2, 3)).reshape(xc * cin, yc * zc)
    weights2 = jnp.swapaxes(spectral_out, 3, 4)

    vmem = pl.BlockSpec(memory_space=pltpu.VMEM)
    anywhere = pl.BlockSpec(memory_space=pl.ANY)
    V = pltpu.VMEM
    out = pl.pallas_call(
        functools.partial(
            kernel, A, B, xc, 1.0 / math.sqrt(cells), 1.0 / math.sqrt(cells / 4.0), math.sqrt(cells)
        ),
        out_shape=jax.ShapeDtypeStruct((xc, cin, yc * zc), F32),
        in_specs=[vmem] * 10 + [anywhere] * 11,
        out_specs=vmem,
        scratch_shapes=[
            V(tzi.shape, BF16), V(spectral_in.shape, F32), V(weights2.shape, F32),
            V(tx_t.shape[1:], BF16), V(yf1_t.shape[1:], BF16), V(yfc_t.shape[1:], BF16),
            V(yic_t.shape[1:], BF16), V(yi2_t.shape[1:], BF16), V(xf_t.shape, BF16), V(xi_t.shape, BF16),
            V(xo_t.shape[1:], BF16),
            V((N, cin, LB), F32), V((N, cin, LB), F32), V((LB, LB), F32),
            V((A, CQ, LB), F32), V((N, CQ, LB), F32), V((A, KX, CQ, LB), F32),
            V((A, hx * cin, width), F32), V((hx * A, 16, width), BF16),
            V((HX // G1, G1 * CQ, LB), F32), V((HX // G1, G1 * CQ, LB), F32), V((hx // GROUP, GROUP * C2, LB), F32),
            V((N, CQ, LB), F32), V((N, CQ, LB), F32), V((N, C1, LB), F32),
            V((xc // GROUP, 2, GROUP * C1, LB), F32),
            V((hx, C1, width), F32), V((xc, 16, yc * zc), BF16), V((16, yc * zc), F32),
            V((GROUP * C2, max(GROUP * C2, G1 * 16)), F32), V((A, CQ, 16), F32),
            pltpu.SemaphoreType.DMA((11,)),
            pltpu.SemaphoreType.DMA((4 * N + 2 * A,)), pltpu.SemaphoreType.DMA((4 * N + 2 * A,)),
        ],
        compiler_params=pltpu.CompilerParams(
            collective_id=0, has_side_effects=True, vmem_limit_bytes=60 * 1024 * 1024
        ),
    )(
        rows, lift.T, lift_bias[None], bypass_in.T, bias_in[None], bypass_out, bias_out[None], proj,
        proj_bias[None], jnp.asarray(tzf),
        jnp.asarray(tzi), spectral_in, weights2, tx_t, yf1_t, yfc_t, yic_t, yi2_t, xf_t, xi_t, xo_t,
    )
    return jnp.transpose(out.reshape(xc, cin, yc, zc), (1, 0, 2, 3))


def solution(mesh):
    A = mesh.shape["gx"]
    B = mesh.shape["gy"]
    in_specs = (
        P(None, "gx", "gy", None), P(), P(), P(("gx", "gy"), None, None, None, None), P(), P(),
        P(("gx", "gy"), None, None, None, None), P(), P(), P(), P(),
    )
    return jax.shard_map(
        functools.partial(on_device, A, B), mesh=mesh, in_specs=in_specs,
        out_specs=P(None, "gx", "gy", None), check_vma=False,
    )
```

```python
import functools
import math

import jax
import jax.numpy as jnp
import numpy as np
from jax import lax
from jax.experimental import pallas as pl
from jax.experimental.pallas import tpu as pltpu
from jax.sharding import PartitionSpec as P

KX = 16
KY = 16
KZ = 8
YB = 8
LB = 128
GROUP = 4
F32 = jnp.float32
BF16 = jnp.bfloat16
MESH = pl.DeviceIdType.MESH


def freq(count):
    f = np.arange(count)
    return np.where(f < count // 2, f, f - count)


def halves(table):
    high = table.astype(np.float32).astype(jnp.bfloat16)
    low = (table - high.astype(np.float64)).astype(np.float32).astype(jnp.bfloat16)
    return np.stack([high, low])


def stacked(table):
    high, low = halves(table)
    return np.concatenate([high, high, low], axis=0)


def angles(places, frequency, length):
    turns = np.mod(places[:, None] * frequency[None, :], length)
    return turns * (2.0 * math.pi / length)


def z_table(z_length):
    ang = angles(np.arange(z_length), np.arange(KZ), z_length)
    table = np.zeros((YB, z_length, 2, YB, KZ))
    for y in range(YB):
        table[y, :, 0, y] = np.cos(ang)
        table[y, :, 1, y] = -np.sin(ang)
    return table.reshape(YB * z_length, LB)


def y_table(blocks, cells, length, groups):
    per = KY // groups
    frequency = freq(KY)
    out = np.zeros((blocks, cells // YB, 2, YB, KZ, groups, LB))
    for b in range(blocks):
        ang = angles(b * cells + np.arange(cells), frequency, length)
        for y in range(cells):
            for j in range(KY):
                c, s = np.cos(ang[y, j]), np.sin(ang[y, j])
                for k in range(KZ):
                    re = (j % per) * KZ + k
                    im = per * KZ + re
                    at = (b, y // YB)
                    out[at + (0, y % YB, k, j // per, re)] = c
                    out[at + (1, y % YB, k, j // per, re)] = s
                    out[at + (0, y % YB, k, j // per, im)] = -s
                    out[at + (1, y % YB, k, j // per, im)] = c
    return out.reshape(blocks, cells // YB * LB, groups * LB)


def x_angles(blocks, cells, length):
    return angles(np.arange(blocks * cells), freq(KX), length).reshape(blocks, cells, KX)


def split(value):
    high = value.astype(BF16)
    return high, (value - high.astype(F32)).astype(BF16)


def mul(a, b):
    return jnp.dot(a, b, preferred_element_type=F32)


def tall(a):
    return jnp.concatenate([a[0], a[1], a[0]], axis=1)


def deep(a):
    return jnp.concatenate([a[0], a[1], a[0]], axis=0)


def wide(a):
    return jnp.concatenate([a[0], a[0], a[1]], axis=1)


def mul3(a, b):
    return mul(a[0], b[0]) + (mul(a[1], b[0]) + mul(a[0], b[1]))


def gelu(v):
    return (0.5 * v) * (1.0 + lax.erf(v * math.sqrt(0.5)))


def kernel(
    A, B, cells_x, cells_y, scale1, scale2, gain,
    f_hbm, lift_hbm, lbias_hbm, byp_hbm, bi_hbm, wo_hbm, bo_hbm, pr_hbm, pb_hbm, tzf_hbm, tzi_hbm, w1_hbm, w2_hbm, tx_hbm, yf1_hbm, yfc_hbm, yic_hbm, yi2_hbm, xf_hbm, xi_hbm, xo_hbm,
    o_ref,
    fx, f_ref, lift_ref, lbias_ref, byp_ref, bi_ref, wo_ref, bo_ref, pr_ref, pb_ref, tzf_ref, os_ref,
    tzi_ref, w1, w2, tx, yf1, yfc, yic, yi2, xf, xi, xo,
    buf1, r1, mx, mt1, r5, buf5, yall, pg, pk_ref, vx, zc, vn, buf2, r3, buf4, r4, ag2, vf, nar, fk_ref, t16, bd, bpq,
    fsem, csem, ssem, rsem,
):
    a = lax.axis_index("gx")
    b = lax.axis_index("gy")
    me = a * B + b
    IL = KX // A
    H = B // IL
    J = KY // H
    N = A * B
    X = A // 2
    CIN, C1 = lift_ref.shape
    C2 = wo_ref.shape[1]
    CQ = C2 // A
    CG = CQ // 8
    hx = cells_x // 2
    HX = hx * A
    G1 = GROUP * C2 // CQ
    own_g = b // H
    own_h = lax.rem(b, H)
    core = lax.rem(a, 2)
    sib = a + 1 - 2 * core

    fields = [pltpu.make_async_copy(f_hbm.at[c], fx.at[:, c], fsem.at[c]) for c in range(CIN)]
    pairs = [
        (tzf_hbm, tzf_ref), (tx_hbm.at[a], tx), (yf1_hbm.at[b], yf1), (lift_hbm, lift_ref), (lbias_hbm, lbias_ref),
        (byp_hbm, byp_ref), (bi_hbm, bi_ref), (wo_hbm, wo_ref), (bo_hbm, bo_ref), (pr_hbm, pr_ref), (pb_hbm, pb_ref),
        (w1_hbm, w1), (xi_hbm, xi), (tzi_hbm, tzi_ref), (xf_hbm, xf), (w2_hbm, w2), (yi2_hbm.at[b], yi2), (xo_hbm.at[a], xo),
    ] + [(yic_hbm.at[g * H + own_h], yic.at[g]) for g in range(IL)] + [(yfc_hbm.at[g * H + own_h], yfc.at[g]) for g in range(IL)]
    loads = [pltpu.make_async_copy(src, dst, csem.at[k]) for k, (src, dst) in enumerate(pairs)]
    l_tzf, l_tx, l_yf1 = loads[:3]
    l_w1, l_xi, l_tzi, l_xf, l_w2, l_yi2, l_xo = loads[11:18]
    for load in fields + loads[:3]:
        load.start()

    barrier = pltpu.get_barrier_semaphore()
    for step in range(1, N):
        peer = lax.rem(me + step, N)
        pl.semaphore_signal(
            barrier, inc=1, device_id=(peer // B, lax.rem(peer, B)), device_id_type=MESH
        )
    for load in loads[3:]:
        load.start()

    lane = lax.broadcasted_iota(jnp.int32, (1, LB), 1)
    sign_f = jnp.where(lane < LB // 2, 1.0, -1.0).astype(F32)

    def rot_f(v):
        return pltpu.roll(v, LB // 2, 1) * sign_f

    def rot_i(v):
        return pltpu.roll(v, LB // 2, 1) * -sign_f

    def remote(source, target, phase, slot, device):
        pltpu.make_async_remote_copy(
            src_ref=source, dst_ref=target, send_sem=ssem.at[phase], recv_sem=rsem.at[slot],
            device_id=device, device_id_type=MESH,
        ).start()

    def whole(target, phase, slot):
        return pltpu.make_async_remote_copy(
            src_ref=target, dst_ref=target, send_sem=ssem.at[phase], recv_sem=rsem.at[slot],
            device_id=(sib, b), device_id_type=MESH,
        )

    def arrive(target, slot):
        whole(target, 0, slot).wait_recv()

    def at(index):
        return (index // B, lax.rem(index, B))

    A2A, PAIR1, EXP1, RED, PAIR2, EXP2, POOL, YALL = range(8)
    SPREAD = 8
    NEAR = SPREAD + X * B

    width = tzi_ref.shape[1]
    for load in fields:
        load.wait()
    flat = fx.reshape(f_ref.shape[0] * cells_y, f_ref.shape[1] // cells_y)
    zn = flat.shape[1]
    for y in range(cells_y):
        f_ref[:, y * zn:(y + 1) * zn] = flat[pl.ds(y, f_ref.shape[0], stride=cells_y), :]
    l_tzf.wait()
    zs = []
    for ch in range(2):
        zs.append(mul(tall(split(f_ref[:, ch * width:(ch + 1) * width])), tzf_ref[...]))
    l_tx.wait()
    us = []
    for z in zs:
        us.append(mul3((tx[0], tx[1]), split(jnp.concatenate([z, rot_f(z)], axis=0))))
    l_yf1.wait()
    part = mul3(split(jnp.concatenate(us, axis=1)), (yf1[0], yf1[1]))
    for i in range(KX):
        for h in range(H):
            buf1[i * H + h] = part[i * CIN:(i + 1) * CIN, h * LB:(h + 1) * LB]
    r1[me] = buf1[me]
    pl.semaphore_wait(barrier, N - 1)

    for step in range(1, N):
        peer = lax.rem(me + step, N)
        remote(buf1.at[peer], r1.at[me], A2A, A2A, at(peer))

    for x in range(hx):
        both = f_ref[2 * x * CIN:(2 * x + 1) * CIN] + f_ref[(2 * x + 1) * CIN:(2 * x + 2) * CIN]
        pieces = [
            both[:, 2 * y * zn:(2 * y + 1) * zn] + both[:, (2 * y + 1) * zn:(2 * y + 2) * zn]
            for y in range(YB)
        ]
        pg[a, x * CIN:(x + 1) * CIN] = jnp.concatenate(pieces, axis=1) * 0.25

    def near_slot(phase, step):
        return NEAR + (phase - POOL) * X + step

    def near_send(buffer, phase):
        for step in range(1, X):
            remote(buffer.at[a], buffer.at[a], phase, near_slot(phase, step), (lax.rem(a + 2 * step, A), b))
        remote(buffer.at[a], buffer.at[a], phase, phase, (sib, b))

    def near_forward(buffer, phase):
        for step in range(1, X):
            peer = lax.rem(a + A - 2 * step, A)
            arrive(buffer.at[peer], near_slot(phase, step))
            remote(buffer.at[peer], buffer.at[peer], phase, phase, (sib, b))

    def near_finish(buffer, phase):
        arrive(buffer.at[pl.ds(0, X)], phase)

    near_send(pg, POOL)

    for load in loads[3:12]:
        load.wait()
    mx[...] = jnp.zeros_like(mx)
    mx[0:CIN, :C1] = lift_ref[...]
    mx[CIN:CIN + 1, :C1] = lbias_ref[...]
    mx[CIN + 1:CIN + 2, :C1] = bo_ref[...]
    lift8 = jnp.concatenate([mx[0:8, :C1]], axis=0)
    columns = mx[...].T[:C1]
    bo_col = columns[:, CIN + 1:CIN + 2]

    def left16(matrix, bias):
        n = matrix.shape[1]
        high, low = split(matrix[0:CIN])
        b0 = bias.astype(BF16)
        rest = bias - b0.astype(F32)
        b1 = rest.astype(BF16)
        b2 = (rest - b1.astype(F32)).astype(BF16)
        mx[...] = jnp.zeros_like(mx)
        mx[0:CIN, :n] = high.astype(F32)
        mx[CIN:2 * CIN, :n] = high.astype(F32)
        mx[2 * CIN:3 * CIN, :n] = low.astype(F32)
        for row, value in enumerate((b0, b1, b2)):
            mx[3 * CIN + row:3 * CIN + row + 1, :n] = value.astype(F32)
        return mx[...].T[:n, :16].astype(BF16)

    highest = lax.Precision.HIGHEST
    m = jnp.dot(lift8, byp_ref[...], precision=highest, preferred_element_type=F32)
    bp16 = left16(m, m[CIN:CIN + 1] + bi_ref[...])
    m = lax.dot_general(
        lift8, pr_ref[...], (((1,), (1,)), ((), ())), precision=highest, preferred_element_type=F32
    )
    pl16 = left16(m, m[CIN:CIN + 1] + pb_ref[...])
    t16[...] = jnp.ones_like(t16)

    def diagonal(value, count):
        rows, cols = value.shape
        bd[...] = jnp.zeros_like(bd)
        for g in range(count):
            bd[g * rows:(g + 1) * rows, g * cols:(g + 1) * cols] = value
        return bd[0:count * rows, 0:count * cols]

    bp_all = bp16.astype(F32)
    for q in range(A):
        bpq[q] = bp_all[q * CQ:(q + 1) * CQ]
    bq_bd = diagonal(bpq[a], G1).astype(BF16)
    bp_bd = diagonal(bp_all, GROUP).astype(BF16)
    pl_bd = diagonal(pl16.astype(F32), GROUP).astype(BF16)
    wo_bd = wide(split(diagonal(wo_ref[...], GROUP)))
    pr_bd = wide(split(diagonal(pr_ref[...], GROUP)))
    arrive(r1.at[pl.ds(0, N - 1)], A2A)

    def mix(st, w, width_out):
        mx[...] = jnp.zeros_like(mx)
        for j in range(J):
            for k in range(KZ):
                q = j * KZ + k
                p = J * KZ + q
                re = st[:, q:q + 1]
                im = st[:, p:p + 1]
                wr = w[j, 0, k]
                wi = w[j, 1, k]
                mx[q:q + 1, :width_out] = jnp.sum(re * wr - im * wi, axis=0, keepdims=True)
                mx[p:p + 1, :width_out] = jnp.sum(re * wi + im * wr, axis=0, keepdims=True)
        return mx[...].T[:width_out]

    s4 = jnp.sum(r1[...], axis=0) * scale1
    st = columns[:, 0:1] * s4[0:1]
    for c in range(1, CIN):
        st = st + columns[:, c:c + 1] * s4[c:c + 1]
    first = jnp.where((lane == 0) & (me == 0), gain, 0.0).astype(F32)
    st = st + columns[:, CIN:CIN + 1] * first
    mixed = mix(st, w1, C2)
    mt1[...] = mixed
    r5[own_h] = mixed

    def group_member(step):
        return own_g * H + lax.rem(own_h + step, H)

    def column(ia, ig):
        return lax.rem(a + ia, A), lax.rem(own_g + ig, IL) * H + own_h

    order = [(ia, ig) for ig in range(IL) for ia in range(A) if ia or ig]
    for t in range(1, H):
        remote(mt1, r5.at[own_h], PAIR1, PAIR1, (a, group_member(t)))

    def fill(value):
        n = value.shape[1]
        high, low = split(value)
        t16[0:CIN, :n] = high.astype(F32)
        t16[CIN:2 * CIN, :n] = low.astype(F32)
        t16[2 * CIN:3 * CIN, :n] = high.astype(F32)
        return t16[:, :n].astype(BF16)

    for x in range(cells_x):
        fk_ref[x] = fill(f_ref[x * CIN:(x + 1) * CIN])
    near_forward(pg, POOL)
    for load in loads[18:18 + IL]:
        load.wait()
    arrive(r5.at[pl.ds(0, H - 1)], PAIR1)
    rows = jnp.concatenate([r5[h] for h in range(H)], axis=1)
    tables = tuple(jnp.concatenate([yic[g, n] for g in range(IL)], axis=1) for n in range(2))
    y = mul3(split(rows), tables)
    for q in range(A):
        for g in range(IL):
            buf5[q * IL + g] = y[q * CQ:(q + 1) * CQ, g * LB:(g + 1) * LB]
    mine = a * IL + own_g
    for ia, ig in reversed(order):
        pa, pb = column(ia, ig)
        remote(buf5.at[pa * IL + pb // H], yall.at[pa, mine], EXP1, EXP1, (pa, pb))
    yall[a, mine] = buf5[mine]
    near_finish(pg, POOL)
    for q in range(A):
        for x in range(hx):
            pk_ref[q * hx + x] = fill(pg[q, x * CIN:(x + 1) * CIN])
    arrive(yall.at[a, pl.ds(0, KX - 1)], EXP1)
    near_send(yall, YALL)
    y = jnp.concatenate([yall[a, i] for i in range(KX)], axis=0)

    def modes(value, rows_each):
        groups = rows_each // 8
        turned = rot_i(value)
        parts = []
        for g in range(groups):
            parts.append(jnp.concatenate([
                v[i * rows_each + g * 8:i * rows_each + g * 8 + 8] for v in (value, turned) for i in range(KX)
            ], axis=0))
        return parts

    l_xi.wait()
    table = wide((
        jnp.concatenate([xi[q, 0] for q in range(A)], axis=0),
        jnp.concatenate([xi[q, 1] for q in range(A)], axis=0),
    ))
    v = mul(table, deep(split(jnp.concatenate(modes(y, CQ), axis=1))))
    for s in range(HX // G1):
        vx[s] = jnp.concatenate([
            v[(s * G1 + xx) * 8:(s * G1 + xx) * 8 + 8, g * LB:(g + 1) * LB]
            for xx in range(G1) for g in range(CG)
        ], axis=0)

    def coarse_step(s, carry):
        v = mul(tall(split(vx[s])), tzi_ref[...])
        near = jnp.concatenate([pk_ref[s * G1 + xx] for xx in range(G1)], axis=0)
        g = split(gelu(v + mul(bq_bd, near)))
        zc[s] = mul(tall(g), tzf_ref[...])
        return carry

    l_tzi.wait()
    lax.fori_loop(0, HX // G1, coarse_step, 0)

    l_xf.wait()
    z = jnp.concatenate([
        jnp.concatenate([
            zc[s, xx * CQ + g * 8:xx * CQ + g * 8 + 8] for s in range(HX // G1) for xx in range(G1)
        ], axis=0) for g in range(CG)
    ], axis=1)
    z = mul(wide((xf[0], xf[1])), deep(split(z)))
    value = jnp.concatenate([
        z[i * 8:(i + 1) * 8, g * LB:(g + 1) * LB] for i in range(KX) for g in range(CG)
    ], axis=0) + rot_f(jnp.concatenate([
        z[(KX + i) * 8:(KX + i + 1) * 8, g * LB:(g + 1) * LB] for i in range(KX) for g in range(CG)
    ], axis=0))
    for i in range(KX):
        buf2[i] = value[i * CQ:(i + 1) * CQ]
    for ia, ig in reversed(order):
        pa, pb = column(ia, ig)
        remote(buf2.at[pa * IL + pb // H], r3.at[a * IL + own_g], RED, RED, (pa, pb))
    r3[a * IL + own_g] = buf2[a * IL + own_g]

    near_forward(yall, YALL)
    near_finish(yall, YALL)
    parts = []
    for q in range(A):
        parts += modes(jnp.concatenate([yall[q, i] for i in range(KX)], axis=0), CQ)
    v = mul(wide((xi[a, 0], xi[a, 1])), deep(split(jnp.concatenate(parts, axis=1))))
    for s in range(hx // GROUP):
        vn[s] = jnp.concatenate([
            v[(s * GROUP + xx) * 8:(s * GROUP + xx) * 8 + 8, g * LB:(g + 1) * LB]
            for xx in range(GROUP) for g in range(C2 // 8)
        ], axis=0)

    def narrow_step(s, carry):
        v = mul(tall(split(vn[s])), tzi_ref[...])
        near = jnp.concatenate([pk_ref[a * hx + s * GROUP + xx] for xx in range(GROUP)], axis=0)
        g = split(gelu(v + mul(bp_bd, near)))
        narrow = mul(wo_bd, deep(g))
        for xx in range(GROUP):
            nar[s * GROUP + xx] = narrow[xx * C1:(xx + 1) * C1]
        return carry

    lax.fori_loop(0, hx // GROUP, narrow_step, 0)

    l_w2.wait()
    for load in loads[18 + IL:]:
        load.wait()
    arrive(r3.at[pl.ds(0, KX - 1)], RED)
    value = jnp.concatenate(
        [jnp.concatenate([r3[q * IL + g] for g in range(IL)], axis=1) for q in range(A)], axis=0
    )
    tables = tuple(jnp.concatenate([yfc[g, n] for g in range(IL)], axis=0) for n in range(2))
    out = mul3(split(value), tables)
    for h in range(H):
        buf4[h] = out[:, h * LB:(h + 1) * LB]
    for t in range(1, H):
        peer = lax.rem(own_h + t, H)
        remote(buf4.at[peer], r4.at[own_h], PAIR2, PAIR2, (a, group_member(t)))
    r4[own_h] = buf4[own_h]
    arrive(r4.at[pl.ds(0, H - 1)], PAIR2)
    st = (jnp.sum(r4[...], axis=0) * scale2).T
    mixed = jnp.zeros((C1, LB), F32)
    for j in range(J):
        for k in range(KZ):
            q = j * KZ + k
            p = J * KZ + q
            re = st[q:q + 1]
            im = st[p:p + 1]
            wr = w2[j, 0, k]
            wi = w2[j, 1, k]
            real = jnp.sum(re * wr - im * wi, axis=1, keepdims=True)
            imag = jnp.sum(re * wi + im * wr, axis=1, keepdims=True)
            mixed = jnp.where(lane == q, real, jnp.where(lane == p, imag, mixed))
    ag2[me] = mixed

    def flip(t):
        value = b
        bit = 1
        while bit < B:
            if t & bit:
                value = value + bit - 2 * bit * lax.rem(b // bit, 2)
            bit *= 2
        return value

    def spread(t):
        source = a * B + flip(t)
        for step in range(1, X):
            remote(
                ag2.at[source], ag2.at[source], EXP2, SPREAD + step * B + t, (lax.rem(a + 2 * step, A), b)
            )
        remote(ag2.at[source], ag2.at[source], EXP2, EXP2, (sib, b))

    for t in range(B - 1, 0, -1):
        remote(ag2.at[me], ag2.at[me], EXP2, SPREAD + t, (a, flip(t)))
    spread(0)
    for t in range(1, B):
        source = a * B + flip(t)
        arrive(ag2.at[source], SPREAD + t)
        spread(t)
    for t in range(B):
        for step in range(1, X):
            source = lax.rem(a + A - 2 * step, A) * B + flip(t)
            arrive(ag2.at[source], SPREAD + step * B + t)
            remote(ag2.at[source], ag2.at[source], EXP2, EXP2, (sib, b))
    arrive(ag2.at[pl.ds(0, X * B)], EXP2)

    l_yi2.wait()
    l_xo.wait()
    rows = jnp.concatenate(
        [jnp.concatenate([ag2[i * H + h] for h in range(H)], axis=1) for i in range(KX)], axis=0
    )
    y = mul3(split(rows), (yi2[0], yi2[1]))
    halves_y = [modes(y[:, ch * LB:(ch + 1) * LB], C1) for ch in range(2)]
    v = mul(wide((xo[0], xo[1])), deep(split(jnp.concatenate(halves_y[0] + halves_y[1], axis=1))))
    CF = C1 // 8
    for s in range(cells_x // GROUP):
        for ch in range(2):
            vf[s, ch] = jnp.concatenate([
                v[(s * GROUP + xx) * 8:(s * GROUP + xx) * 8 + 8, (ch * CF + g) * LB:(ch * CF + g + 1) * LB]
                for xx in range(GROUP) for g in range(CF)
            ], axis=0)

    def fine_step(group, carry):
        near = jnp.concatenate([fk_ref[group * GROUP + xx] for xx in range(GROUP)], axis=0)
        for ch in range(2):
            v = mul(tall(split(vf[group, ch])), tzi_ref[...])
            rows = []
            for xx in range(0, GROUP, 2):
                half = nar.at[group * (GROUP // 2) + xx // 2]
                pieces = []
                for yy in range(YB):
                    at_y = (ch * YB + yy) // 2 * zn
                    pieces.append(half[:, at_y:at_y + zn])
                rows += [jnp.concatenate(pieces, axis=1) + bo_col] * 2
            g = split(gelu(v + jnp.concatenate(rows, axis=0)))
            cols = slice(ch * width, (ch + 1) * width)
            res = mul(pr_bd, deep(g)) + mul(pl_bd, near[:, cols])
            for yy in range(YB):
                os_ref[ch, yy * GROUP * CIN:(yy + 1) * GROUP * CIN] = res[:, yy * zn:(yy + 1) * zn]
            for xx in range(GROUP):
                for c in range(CIN):
                    o_ref[c, group * GROUP + xx, ch * YB:(ch + 1) * YB] = os_ref[
                        ch, pl.ds(xx * CIN + c, YB, stride=GROUP * CIN), :
                    ]
        return carry

    lax.fori_loop(0, cells_x // GROUP, fine_step, 0)
    for phase, target in (
        (A2A, buf1.at[pl.ds(0, N - 1)]), (PAIR1, r5.at[pl.ds(0, H - 1)]), (EXP1, buf5.at[pl.ds(0, KX - 1)]),
        (RED, buf2.at[pl.ds(0, KX - 1)]), (PAIR2, buf4.at[pl.ds(0, H - 1)]), (EXP2, ag2.at[pl.ds(0, N - 1)]),
        (POOL, pg.at[pl.ds(0, A - 1)]), (YALL, yall.at[pl.ds(0, A - 1)]),
    ):
        whole(target, phase, phase).wait_send()


def on_device(
    A, B, fields, lift, lift_bias, spectral_in, bypass_in, bias_in, spectral_out, bypass_out,
    bias_out, proj, proj_bias,
):
    cin, xc, yc, zc = fields.shape
    C1 = lift.shape[0]
    C2 = bypass_in.shape[0]
    NX = xc * A
    NY = yc * B
    IL = KX // A
    H = B // IL
    J = KY // H
    N = A * B
    width = YB * zc
    CQ = C2 // A
    hx = xc // 2
    HX = hx * A
    G1 = GROUP * C2 // CQ
    cells = float(NX * NY * zc)
    back = math.sqrt(2.0 / (KX * KY * KZ))

    tz = z_table(zc)
    tzf = stacked(tz)
    tzi = stacked(np.ascontiguousarray(tz.T) * back)
    fine_x = x_angles(A, xc, NX)
    half_x = x_angles(A, xc // 2, NX // 2)
    eye = np.eye(cin)
    tx = np.stack([
        np.concatenate([np.kron(np.cos(fine_x[i].T), eye), np.kron(np.sin(fine_x[i].T), eye)], axis=1)
        for i in range(A)
    ])
    eye8 = np.eye(8)

    def lines(ang):
        return np.concatenate([np.kron(np.cos(ang), eye8), np.kron(np.sin(ang), eye8)], axis=1)

    xi = np.stack([lines(half_x[i]) for i in range(A)])
    xf = np.ascontiguousarray(xi.reshape(-1, xi.shape[2]).T)
    xo = np.stack([lines(fine_x[i]) for i in range(A)])
    yf1 = y_table(B, yc, NY, H)
    yfc = y_table(B, yc // 2, NY // 2, H)

    def per_device(table):
        return jnp.asarray(np.ascontiguousarray(np.swapaxes(halves(table), 0, 1)))

    tx_t = per_device(tx)
    yf1_t = per_device(yf1)
    yfc_t = per_device(yfc)
    yic_t = per_device(np.swapaxes(yfc, 1, 2))
    yi2_t = per_device(np.swapaxes(yf1, 1, 2))
    xi_t = per_device(xi)
    xo_t = per_device(xo)
    xf_t = jnp.asarray(halves(xf))

    weights2 = jnp.swapaxes(spectral_out, 3, 4)

    operands = [
        fields, lift.T, lift_bias[None], bypass_in.T, bias_in[None], bypass_out, bias_out[None], proj,
        proj_bias[None], jnp.asarray(tzf),
        jnp.asarray(tzi), spectral_in, weights2, tx_t, yf1_t, yfc_t, yic_t, yi2_t, xf_t, xi_t, xo_t,
    ]
    anywhere = pl.BlockSpec(memory_space=pl.ANY)
    V = pltpu.VMEM
    return pl.pallas_call(
        functools.partial(
            kernel, A, B, xc, yc, 1.0 / math.sqrt(cells), 1.0 / math.sqrt(cells / 4.0), math.sqrt(cells)
        ),
        out_shape=pltpu.VMEM((cin, xc, yc, zc), F32),
        in_specs=[anywhere] * len(operands),
        out_specs=pl.BlockSpec(memory_space=pltpu.VMEM),
        scratch_shapes=[
            V((xc, cin, yc, zc), F32), V((xc * cin, yc * zc), F32),
        ] + [V(v.shape, v.dtype) for v in operands[1:10]] + [
            V((2, YB * GROUP * cin, zc), F32),
            V(tzi.shape, BF16), V(spectral_in.shape, F32), V(weights2.shape, F32),
            V(tx_t.shape[1:], BF16), V(yf1_t.shape[1:], BF16), V((IL,) + yfc_t.shape[1:], BF16),
            V((IL,) + yic_t.shape[1:], BF16), V(yi2_t.shape[1:], BF16), V(xf_t.shape, BF16), V(xi_t.shape, BF16),
            V(xo_t.shape[1:], BF16),
            V((N, cin, LB), F32), V((N, cin, LB), F32), V((LB, LB), F32),
            V((C2, LB), F32), V((H, C2, LB), F32), V((KX, CQ, LB), F32), V((A, KX, CQ, LB), F32),
            V((A, hx * cin, width), F32), V((hx * A, 16, width), BF16),
            V((HX // G1, G1 * CQ, LB), F32), V((HX // G1, G1 * CQ, LB), F32), V((hx // GROUP, GROUP * C2, LB), F32),
            V((KX, CQ, LB), F32), V((KX, CQ, LB), F32), V((H, C2, LB), F32), V((H, C2, LB), F32), V((N, C1, LB), F32),
            V((xc // GROUP, 2, GROUP * C1, LB), F32),
            V((hx, C1, width), F32), V((xc, 16, yc * zc), BF16), V((16, yc * zc), F32),
            V((GROUP * C2, max(GROUP * C2, G1 * 16)), F32), V((A, CQ, 16), F32),
            pltpu.SemaphoreType.DMA((cin,)),
            pltpu.SemaphoreType.DMA((18 + 2 * IL,)),
            pltpu.SemaphoreType.DMA((8,)), pltpu.SemaphoreType.DMA((8 + A * B // 2 + A,)),
        ],
        compiler_params=pltpu.CompilerParams(
            collective_id=0, has_side_effects=True, vmem_limit_bytes=60 * 1024 * 1024
        ),
    )(*operands)


def solution(mesh):
    A = mesh.shape["gx"]
    B = mesh.shape["gy"]
    in_specs = (
        P(None, "gx", "gy", None), P(), P(), P(("gx", "gy"), None, None, None, None), P(), P(),
        P(("gx", "gy"), None, None, None, None), P(), P(), P(), P(),
    )
    return jax.shard_map(
        functools.partial(on_device, A, B), mesh=mesh, in_specs=in_specs,
        out_specs=P(None, "gx", "gy", None), check_vma=False,
    )
```

```python
import functools
import math

import jax
import jax.numpy as jnp
import numpy as np
from jax import lax
from jax.experimental import pallas as pl
from jax.experimental.pallas import tpu as pltpu
from jax.sharding import PartitionSpec as P

KX = 16
KY = 16
KZ = 8
YB = 8
LB = 128
GROUP = 4
F32 = jnp.float32
BF16 = jnp.bfloat16
MESH = pl.DeviceIdType.MESH


def freq(count):
    f = np.arange(count)
    return np.where(f < count // 2, f, f - count)


def halves(table):
    high = table.astype(np.float32).astype(jnp.bfloat16)
    low = (table - high.astype(np.float64)).astype(np.float32).astype(jnp.bfloat16)
    return np.stack([high, low])


def stacked(table):
    high, low = halves(table)
    return np.concatenate([high, high, low], axis=0)


def angles(places, frequency, length):
    turns = np.mod(places[:, None] * frequency[None, :], length)
    return turns * (2.0 * math.pi / length)


def z_table(z_length):
    ang = angles(np.arange(z_length), np.arange(KZ), z_length)
    table = np.zeros((YB, z_length, 2, YB, KZ))
    for y in range(YB):
        table[y, :, 0, y] = np.cos(ang)
        table[y, :, 1, y] = -np.sin(ang)
    return table.reshape(YB * z_length, LB)


def y_table(blocks, cells, length, groups):
    per = KY // groups
    frequency = freq(KY)
    out = np.zeros((blocks, cells // YB, 2, YB, KZ, groups, LB))
    for b in range(blocks):
        ang = angles(b * cells + np.arange(cells), frequency, length)
        for y in range(cells):
            for j in range(KY):
                c, s = np.cos(ang[y, j]), np.sin(ang[y, j])
                for k in range(KZ):
                    re = (j % per) * KZ + k
                    im = per * KZ + re
                    at = (b, y // YB)
                    out[at + (0, y % YB, k, j // per, re)] = c
                    out[at + (1, y % YB, k, j // per, re)] = s
                    out[at + (0, y % YB, k, j // per, im)] = -s
                    out[at + (1, y % YB, k, j // per, im)] = c
    return out.reshape(blocks, cells // YB * LB, groups * LB)


def x_angles(blocks, cells, length):
    return angles(np.arange(blocks * cells), freq(KX), length).reshape(blocks, cells, KX)


def split(value):
    high = value.astype(BF16)
    return high, (value - high.astype(F32)).astype(BF16)


def mul(a, b):
    return jnp.dot(a, b, preferred_element_type=F32)


def tall(a):
    return jnp.concatenate([a[0], a[1], a[0]], axis=1)


def deep(a):
    return jnp.concatenate([a[0], a[1], a[0]], axis=0)


def wide(a):
    return jnp.concatenate([a[0], a[0], a[1]], axis=1)


def mul3(a, b):
    return mul(a[0], b[0]) + (mul(a[1], b[0]) + mul(a[0], b[1]))


def gelu(v):
    return (0.5 * v) * (1.0 + lax.erf(v * math.sqrt(0.5)))


def parts_of(A, H, channels):
    parts = 1
    while H % (2 * parts) == 0 and channels % (16 * parts * A) == 0:
        parts *= 2
    return parts


def kernel(
    A, B, cells_x, cells_y, scale1, scale2, gain,
    f_hbm, lift_hbm, lbias_hbm, byp_hbm, bi_hbm, wo_hbm, bo_hbm, pr_hbm, pb_hbm, tzf_hbm, tzi_hbm, w1_hbm, w2_hbm, tx_hbm, yf1_hbm, yfc_hbm, yic_hbm, yi2_hbm, xf_hbm, xi_hbm, xo_hbm,
    o_ref,
    fx, f_ref, lift_ref, lbias_ref, byp_ref, bi_ref, wo_ref, bo_ref, pr_ref, pb_ref, tzf_ref, os_ref,
    tzi_ref, w1, w2, tx, yf1, yfc, yic, yi2, xf, xi, xo,
    buf1, r1, mx, mt1, g1, lines, yall, pg, pk_ref, vx, zc, vn, buf2, r3, ag2, vf, nar, fk_ref, t16, bd, bpq,
    fsem, csem, ssem, rsem,
):
    a = lax.axis_index("gx")
    b = lax.axis_index("gy")
    me = a * B + b
    IL = KX // A
    H = B // IL
    J = KY // H
    N = A * B
    X = A // 2
    CIN, C1 = lift_ref.shape
    C2 = wo_ref.shape[1]
    S = parts_of(A, H, C2)
    CQ = C2 // (A * S)
    CG = CQ // 8
    hx = cells_x // 2
    HX = hx * A
    G1 = GROUP * C2 // CQ
    part = lax.rem(b, S)
    base = b - part
    core = lax.rem(a, 2)
    sib = a + 1 - 2 * core

    fields = [pltpu.make_async_copy(f_hbm.at[c], fx.at[:, c], fsem.at[c]) for c in range(CIN)]
    pairs = [
        (tzf_hbm, tzf_ref), (tx_hbm.at[a], tx), (yf1_hbm.at[b], yf1), (lift_hbm, lift_ref), (lbias_hbm, lbias_ref),
        (byp_hbm, byp_ref), (bi_hbm, bi_ref), (wo_hbm, wo_ref), (bo_hbm, bo_ref), (pr_hbm, pr_ref), (pb_hbm, pb_ref),
        (w1_hbm, w1), (xi_hbm, xi), (tzi_hbm, tzi_ref), (xf_hbm, xf), (w2_hbm, w2), (yi2_hbm.at[b], yi2), (xo_hbm.at[a], xo),
    ] + [(yic_hbm.at[base + n], yic.at[n]) for n in range(S)] + [(yfc_hbm.at[base + n], yfc.at[n]) for n in range(S)]
    loads = [pltpu.make_async_copy(src, dst, csem.at[k]) for k, (src, dst) in enumerate(pairs)]
    l_tzf, l_tx, l_yf1 = loads[:3]
    l_w1, l_xi, l_tzi, l_xf, l_w2, l_yi2, l_xo = loads[11:18]
    for load in fields + loads[:3]:
        load.start()

    barrier = pltpu.get_barrier_semaphore()
    for step in range(1, N):
        peer = lax.rem(me + step, N)
        pl.semaphore_signal(
            barrier, inc=1, device_id=(peer // B, lax.rem(peer, B)), device_id_type=MESH
        )
    for load in loads[3:]:
        load.start()

    lane = lax.broadcasted_iota(jnp.int32, (1, LB), 1)
    sign_f = jnp.where(lane < LB // 2, 1.0, -1.0).astype(F32)

    def rot_f(v):
        return pltpu.roll(v, LB // 2, 1) * sign_f

    def rot_i(v):
        return pltpu.roll(v, LB // 2, 1) * -sign_f

    def remote(source, target, phase, slot, device):
        pltpu.make_async_remote_copy(
            src_ref=source, dst_ref=target, send_sem=ssem.at[phase], recv_sem=rsem.at[slot],
            device_id=device, device_id_type=MESH,
        ).start()

    def whole(target, phase, slot):
        return pltpu.make_async_remote_copy(
            src_ref=target, dst_ref=target, send_sem=ssem.at[phase], recv_sem=rsem.at[slot],
            device_id=(sib, b), device_id_type=MESH,
        )

    def arrive(target, slot):
        whole(target, 0, slot).wait_recv()

    def at(index):
        return (index // B, lax.rem(index, B))

    A2A, EXP1, RED, EXP2, LINE_PAIR, POOL, POOL_X, POOL_Y, POOL_XY, LINE = range(10)
    SPREAD = LINE + S
    NEAR = SPREAD + X * B

    width = tzi_ref.shape[1]
    for load in fields:
        load.wait()
    flat = fx.reshape(f_ref.shape[0] * cells_y, f_ref.shape[1] // cells_y)
    zn = flat.shape[1]
    for y in range(cells_y):
        f_ref[:, y * zn:(y + 1) * zn] = flat[pl.ds(y, f_ref.shape[0], stride=cells_y), :]
    l_tzf.wait()
    zs = []
    for ch in range(2):
        zs.append(mul(tall(split(f_ref[:, ch * width:(ch + 1) * width])), tzf_ref[...]))
    l_tx.wait()
    us = []
    for z in zs:
        us.append(mul3((tx[0], tx[1]), split(jnp.concatenate([z, rot_f(z)], axis=0))))
    l_yf1.wait()
    parts = mul3(split(jnp.concatenate(us, axis=1)), (yf1[0], yf1[1]))
    for i in range(KX):
        for h in range(H):
            buf1[i * H + h] = parts[i * CIN:(i + 1) * CIN, h * LB:(h + 1) * LB]
    r1[me] = buf1[me]
    pl.semaphore_wait(barrier, N - 1)

    for step in range(1, N):
        peer = lax.rem(me + step, N)
        remote(buf1.at[peer], r1.at[me], A2A, A2A, at(peer))

    for x in range(hx):
        both = f_ref[2 * x * CIN:(2 * x + 1) * CIN] + f_ref[(2 * x + 1) * CIN:(2 * x + 2) * CIN]
        pieces = [
            both[:, 2 * y * zn:(2 * y + 1) * zn] + both[:, (2 * y + 1) * zn:(2 * y + 2) * zn]
            for y in range(YB)
        ]
        pg[a * S + part, x * CIN:(x + 1) * CIN] = jnp.concatenate(pieces, axis=1) * 0.25

    def near_slot(phase, step):
        return NEAR + (phase - LINE) * X + step

    square = X == 2 and S == 2
    mate = lax.rem(a + 2, A)
    other = S - 1 - part

    def share_send(buffer):
        own = buffer.at[a * S + part]
        if square:
            remote(own, own, POOL, POOL_X, (mate, b))
            remote(own, own, POOL, POOL_Y, (a, base + other))
            remote(own, own, POOL, POOL, (sib, b))
        else:
            for ia in range(A):
                for turn in range(S):
                    if ia or turn:
                        remote(own, own, POOL, POOL, (lax.rem(a + ia, A), base + member(turn)))

    def share_relay(buffer):
        if square:
            left = buffer.at[mate * S + part]
            right = buffer.at[a * S + other]
            arrive(left, POOL_X)
            arrive(right, POOL_Y)
            ia = a * core + mate * (1 - core)
            ip = other * core + part * (1 - core)
            target = (mate * core + a * (1 - core), b * core + (base + other) * (1 - core))
            relayed = buffer.at[ia * S + ip]
            remote(relayed, relayed, POOL, POOL_XY, target)
            remote(left, left, POOL, POOL, (sib, b))
            remote(right, right, POOL, POOL, (sib, b))

    def share_last(buffer):
        if square:
            corner = buffer.at[mate * S + other]
            arrive(corner, POOL_XY)
            remote(corner, corner, POOL, POOL, (sib, b))

    def share_finish(buffer):
        arrive(buffer.at[pl.ds(0, A * S // 2 if square else A * S - 1)], POOL)

    def member(turn):
        return lax.rem(part + turn, S)

    def pair_finish(buffer, phase):
        if S > 1:
            arrive(buffer.at[0, pl.ds(0, S - 1)], phase)

    def near_send(buffer, phase, turn):
        own = buffer.at[a, member(turn)]
        for step in range(1, X):
            remote(own, own, phase + turn, near_slot(phase + turn, step), (lax.rem(a + 2 * step, A), b))
        remote(own, own, phase + turn, phase + turn, (sib, b))

    def near_forward(buffer, phase, turn):
        for step in range(1, X):
            other = buffer.at[lax.rem(a + A - 2 * step, A), member(turn)]
            arrive(other, near_slot(phase + turn, step))
            remote(other, other, phase + turn, phase + turn, (sib, b))

    def near_finish(buffer, phase, turn):
        arrive(buffer.at[pl.ds(0, X), 0], phase + turn)

    share_send(pg)

    for load in loads[3:12]:
        load.wait()
    mx[...] = jnp.zeros_like(mx)
    mx[0:CIN, :C1] = lift_ref[...]
    mx[CIN:CIN + 1, :C1] = lbias_ref[...]
    mx[CIN + 1:CIN + 2, :C1] = bo_ref[...]
    lift8 = jnp.concatenate([mx[0:8, :C1]], axis=0)
    columns = mx[...].T[:C1]
    bo_col = columns[:, CIN + 1:CIN + 2]

    def left16(matrix, bias):
        n = matrix.shape[1]
        high, low = split(matrix[0:CIN])
        b0 = bias.astype(BF16)
        rest = bias - b0.astype(F32)
        b1 = rest.astype(BF16)
        b2 = (rest - b1.astype(F32)).astype(BF16)
        mx[...] = jnp.zeros_like(mx)
        mx[0:CIN, :n] = high.astype(F32)
        mx[CIN:2 * CIN, :n] = high.astype(F32)
        mx[2 * CIN:3 * CIN, :n] = low.astype(F32)
        for row, value in enumerate((b0, b1, b2)):
            mx[3 * CIN + row:3 * CIN + row + 1, :n] = value.astype(F32)
        return mx[...].T[:n, :16].astype(BF16)

    highest = lax.Precision.HIGHEST
    m = jnp.dot(lift8, byp_ref[...], precision=highest, preferred_element_type=F32)
    bp16 = left16(m, m[CIN:CIN + 1] + bi_ref[...])
    m = lax.dot_general(
        lift8, pr_ref[...], (((1,), (1,)), ((), ())), precision=highest, preferred_element_type=F32
    )
    pl16 = left16(m, m[CIN:CIN + 1] + pb_ref[...])
    t16[...] = jnp.ones_like(t16)

    def diagonal(value, count):
        rows, cols = value.shape
        bd[...] = jnp.zeros_like(bd)
        for g in range(count):
            bd[g * rows:(g + 1) * rows, g * cols:(g + 1) * cols] = value
        return bd[0:count * rows, 0:count * cols]

    bp_all = bp16.astype(F32)
    for q in range(A * S):
        bpq[q] = bp_all[q * CQ:(q + 1) * CQ]
    bq_bd = diagonal(bpq[a * S + part], G1).astype(BF16)
    bp_bd = diagonal(bp_all, GROUP).astype(BF16)
    pl_bd = diagonal(pl16.astype(F32), GROUP).astype(BF16)
    wo_bd = wide(split(diagonal(wo_ref[...], GROUP)))
    pr_bd = wide(split(diagonal(pr_ref[...], GROUP)))
    arrive(r1.at[pl.ds(0, N - 1)], A2A)

    def mix(st, w, width_out):
        mx[...] = jnp.zeros_like(mx)
        for j in range(J):
            for k in range(KZ):
                q = j * KZ + k
                p = J * KZ + q
                re = st[:, q:q + 1]
                im = st[:, p:p + 1]
                wr = w[j, 0, k]
                wi = w[j, 1, k]
                mx[q:q + 1, :width_out] = jnp.sum(re * wr - im * wi, axis=0, keepdims=True)
                mx[p:p + 1, :width_out] = jnp.sum(re * wi + im * wr, axis=0, keepdims=True)
        return mx[...].T[:width_out]

    s4 = jnp.sum(r1[...], axis=0) * scale1
    st = columns[:, 0:1] * s4[0:1]
    for c in range(1, CIN):
        st = st + columns[:, c:c + 1] * s4[c:c + 1]
    first = jnp.where((lane == 0) & (me == 0), gain, 0.0).astype(F32)
    st = st + columns[:, CIN:CIN + 1] * first
    mixed = mix(st, w1, C2)
    for q in range(A * S):
        mt1[q] = mixed[q * CQ:(q + 1) * CQ]
    g1[me] = mt1[a * S + part]
    for step in range(1, N):
        pa, pb = at(lax.rem(me + step, N))
        remote(mt1.at[pa * S + lax.rem(pb, S)], g1.at[me], EXP1, EXP1, (pa, pb))

    def fill(value):
        n = value.shape[1]
        high, low = split(value)
        t16[0:CIN, :n] = high.astype(F32)
        t16[CIN:2 * CIN, :n] = low.astype(F32)
        t16[2 * CIN:3 * CIN, :n] = high.astype(F32)
        return t16[:, :n].astype(BF16)

    def fill_pooled(ia, ip):
        for x in range(hx):
            pk_ref[ip * HX + ia * hx + x] = fill(pg[ia * S + ip, x * CIN:(x + 1) * CIN])

    share_relay(pg)
    for x in range(cells_x):
        fk_ref[x] = fill(f_ref[x * CIN:(x + 1) * CIN])
    if square:
        fill_pooled(a, part)
        fill_pooled(mate, part)
        fill_pooled(a, other)
        share_last(pg)
        fill_pooled(mate, other)
    for load in loads[18:18 + S]:
        load.wait()
    arrive(g1.at[pl.ds(0, N - 1)], EXP1)
    rows = jnp.concatenate(
        [jnp.concatenate([g1[i * H + h] for h in range(H)], axis=1) for i in range(KX)], axis=0
    )
    tables = tuple(jnp.concatenate([yic[n, k] for n in range(S)], axis=1) for k in range(2))
    y = mul3(split(rows), tables)
    for n in range(S):
        for i in range(KX):
            lines[n, i] = y[i * CQ:(i + 1) * CQ, n * LB:(n + 1) * LB]
    for turn in range(1, S):
        remote(lines.at[member(turn)], yall.at[a, part], LINE_PAIR, LINE_PAIR, (a, base + member(turn)))
    for i in range(KX):
        yall[a, part, i] = lines[part, i]
    near_send(yall, LINE, 0)

    def modes(value, rows_each):
        groups = rows_each // 8
        turned = rot_i(value)
        parts = []
        for g in range(groups):
            parts.append(jnp.concatenate([
                v[i * rows_each + g * 8:i * rows_each + g * 8 + 8] for v in (value, turned) for i in range(KX)
            ], axis=0))
        return parts

    l_xi.wait()
    table = wide((
        jnp.concatenate([xi[q, 0] for q in range(A)], axis=0),
        jnp.concatenate([xi[q, 1] for q in range(A)], axis=0),
    ))
    halves_y = []
    for n in range(S):
        halves_y += modes(y[:, n * LB:(n + 1) * LB], CQ)
    v = mul(table, deep(split(jnp.concatenate(halves_y, axis=1))))
    steps = HX // G1
    for n in range(S):
        for s in range(steps):
            vx[n * steps + s] = jnp.concatenate([
                v[(s * G1 + xx) * 8:(s * G1 + xx) * 8 + 8, (n * CG + g) * LB:(n * CG + g + 1) * LB]
                for xx in range(G1) for g in range(CG)
            ], axis=0)

    def coarse_step(s, carry):
        v = mul(tall(split(vx[s])), tzi_ref[...])
        near = jnp.concatenate([pk_ref[s * G1 + xx] for xx in range(G1)], axis=0)
        g = split(gelu(v + mul(bq_bd, near)))
        zc[s] = mul(tall(g), tzf_ref[...])
        return carry

    share_finish(pg)
    for ia in (sib, lax.rem(sib + 2, A)) if square else range(A):
        for ip in range(S):
            fill_pooled(ia, ip)
    l_tzi.wait()
    lax.fori_loop(0, S * steps, coarse_step, 0)

    l_xf.wait()
    for load in loads[18 + S:]:
        load.wait()
    z = jnp.concatenate([
        jnp.concatenate([
            zc[n * steps + s, xx * CQ + g * 8:xx * CQ + g * 8 + 8] for s in range(steps) for xx in range(G1)
        ], axis=0) for n in range(S) for g in range(CG)
    ], axis=1)
    z = mul(wide((xf[0], xf[1])), deep(split(z)))

    def spectrum(first, n):
        return jnp.concatenate([
            z[(first + i) * 8:(first + i + 1) * 8, (n * CG + g) * LB:(n * CG + g + 1) * LB]
            for i in range(KX) for g in range(CG)
        ], axis=0)

    value = jnp.concatenate([spectrum(0, n) + rot_f(spectrum(KX, n)) for n in range(S)], axis=1)
    tables = tuple(jnp.concatenate([yfc[n, k] for n in range(S)], axis=0) for k in range(2))
    out = mul3(split(value), tables)
    for i in range(KX):
        for h in range(H):
            buf2[i * H + h] = out[i * CQ:(i + 1) * CQ, h * LB:(h + 1) * LB]
    for step in range(1, N):
        peer = lax.rem(me + step, N)
        remote(buf2.at[peer], r3.at[me], RED, RED, at(peer))
    r3[me] = buf2[me]

    pair_finish(yall, LINE_PAIR)
    for turn in range(1, S):
        near_send(yall, LINE, turn)
    near_forward(yall, LINE, 0)
    l_w2.wait()
    arrive(r3.at[pl.ds(0, N - 1)], RED)
    for turn in range(1, S):
        near_forward(yall, LINE, turn)
    sums = []
    for q in range(A):
        for n in range(S):
            total = r3[q * B + n]
            for t in range(S + n, B, S):
                total = total + r3[q * B + t]
            sums.append(total)
    st = (jnp.concatenate(sums, axis=0) * scale2).T
    mixed = jnp.zeros((C1, LB), F32)
    for j in range(J):
        for k in range(KZ):
            q = j * KZ + k
            p = J * KZ + q
            re = st[q:q + 1]
            im = st[p:p + 1]
            wr = w2[j, 0, k]
            wi = w2[j, 1, k]
            real = jnp.sum(re * wr - im * wi, axis=1, keepdims=True)
            imag = jnp.sum(re * wi + im * wr, axis=1, keepdims=True)
            mixed = jnp.where(lane == q, real, jnp.where(lane == p, imag, mixed))
    ag2[me] = mixed

    def flip(t):
        value = b
        bit = 1
        while bit < B:
            if t & bit:
                value = value + bit - 2 * bit * lax.rem(b // bit, 2)
            bit *= 2
        return value

    def spread(t):
        source = a * B + flip(t)
        for step in range(1, X):
            remote(
                ag2.at[source], ag2.at[source], EXP2, SPREAD + step * B + t, (lax.rem(a + 2 * step, A), b)
            )
        remote(ag2.at[source], ag2.at[source], EXP2, EXP2, (sib, b))

    for t in range(B - 1, 0, -1):
        remote(ag2.at[me], ag2.at[me], EXP2, SPREAD + t, (a, flip(t)))
    spread(0)
    for turn in range(S):
        near_finish(yall, LINE, turn)
    parts = []
    for q in range(A):
        for n in range(S):
            parts += modes(jnp.concatenate([yall[q, n, i] for i in range(KX)], axis=0), CQ)
    v = mul(wide((xi[a, 0], xi[a, 1])), deep(split(jnp.concatenate(parts, axis=1))))
    for s in range(hx // GROUP):
        vn[s] = jnp.concatenate([
            v[(s * GROUP + xx) * 8:(s * GROUP + xx) * 8 + 8, g * LB:(g + 1) * LB]
            for xx in range(GROUP) for g in range(C2 // 8)
        ], axis=0)

    def narrow_step(s, carry):
        v = mul(tall(split(vn[s])), tzi_ref[...])
        near = jnp.concatenate([pk_ref[part * HX + a * hx + s * GROUP + xx] for xx in range(GROUP)], axis=0)
        g = split(gelu(v + mul(bp_bd, near)))
        narrow = mul(wo_bd, deep(g))
        for xx in range(GROUP):
            nar[s * GROUP + xx] = narrow[xx * C1:(xx + 1) * C1]
        return carry

    lax.fori_loop(0, hx // GROUP, narrow_step, 0)

    for t in range(1, B):
        source = a * B + flip(t)
        arrive(ag2.at[source], SPREAD + t)
        spread(t)
    for t in range(B):
        for step in range(1, X):
            source = lax.rem(a + A - 2 * step, A) * B + flip(t)
            arrive(ag2.at[source], SPREAD + step * B + t)
            remote(ag2.at[source], ag2.at[source], EXP2, EXP2, (sib, b))
    arrive(ag2.at[pl.ds(0, X * B)], EXP2)

    l_yi2.wait()
    l_xo.wait()
    rows = jnp.concatenate(
        [jnp.concatenate([ag2[i * H + h] for h in range(H)], axis=1) for i in range(KX)], axis=0
    )
    y = mul3(split(rows), (yi2[0], yi2[1]))
    halves_y = [modes(y[:, ch * LB:(ch + 1) * LB], C1) for ch in range(2)]
    v = mul(wide((xo[0], xo[1])), deep(split(jnp.concatenate(halves_y[0] + halves_y[1], axis=1))))
    CF = C1 // 8
    for s in range(cells_x // GROUP):
        for ch in range(2):
            vf[s, ch] = jnp.concatenate([
                v[(s * GROUP + xx) * 8:(s * GROUP + xx) * 8 + 8, (ch * CF + g) * LB:(ch * CF + g + 1) * LB]
                for xx in range(GROUP) for g in range(CF)
            ], axis=0)

    def fine_step(group, carry):
        near = jnp.concatenate([fk_ref[group * GROUP + xx] for xx in range(GROUP)], axis=0)
        for ch in range(2):
            v = mul(tall(split(vf[group, ch])), tzi_ref[...])
            rows = []
            for xx in range(0, GROUP, 2):
                half = nar.at[group * (GROUP // 2) + xx // 2]
                pieces = []
                for yy in range(YB):
                    at_y = (ch * YB + yy) // 2 * zn
                    pieces.append(half[:, at_y:at_y + zn])
                rows += [jnp.concatenate(pieces, axis=1) + bo_col] * 2
            g = split(gelu(v + jnp.concatenate(rows, axis=0)))
            cols = slice(ch * width, (ch + 1) * width)
            res = mul(pr_bd, deep(g)) + mul(pl_bd, near[:, cols])
            for yy in range(YB):
                os_ref[ch, yy * GROUP * CIN:(yy + 1) * GROUP * CIN] = res[:, yy * zn:(yy + 1) * zn]
            for xx in range(GROUP):
                for c in range(CIN):
                    o_ref[c, group * GROUP + xx, ch * YB:(ch + 1) * YB] = os_ref[
                        ch, pl.ds(xx * CIN + c, YB, stride=GROUP * CIN), :
                    ]
        return carry

    lax.fori_loop(0, cells_x // GROUP, fine_step, 0)
    waits = [
        (A2A, buf1.at[pl.ds(0, N - 1)]), (EXP1, g1.at[pl.ds(0, N - 1)]), (RED, buf2.at[pl.ds(0, N - 1)]),
        (EXP2, ag2.at[pl.ds(0, N - 1)]),
    ]
    if S > 1:
        waits.append((LINE_PAIR, yall.at[0, pl.ds(0, S - 1)]))
    waits.append((POOL, pg.at[pl.ds(0, A * S - 1)]))
    for turn in range(S):
        waits.append((LINE + turn, yall.at[pl.ds(0, A - 1), 0]))
    for phase, target in waits:
        whole(target, phase, phase).wait_send()


def on_device(
    A, B, fields, lift, lift_bias, spectral_in, bypass_in, bias_in, spectral_out, bypass_out,
    bias_out, proj, proj_bias,
):
    cin, xc, yc, zc = fields.shape
    C1 = lift.shape[0]
    C2 = bypass_in.shape[0]
    NX = xc * A
    NY = yc * B
    IL = KX // A
    H = B // IL
    J = KY // H
    N = A * B
    width = YB * zc
    S = parts_of(A, H, C2)
    CQ = C2 // (A * S)
    hx = xc // 2
    HX = hx * A
    G1 = GROUP * C2 // CQ
    cells = float(NX * NY * zc)
    back = math.sqrt(2.0 / (KX * KY * KZ))

    tz = z_table(zc)
    tzf = stacked(tz)
    tzi = stacked(np.ascontiguousarray(tz.T) * back)
    fine_x = x_angles(A, xc, NX)
    half_x = x_angles(A, xc // 2, NX // 2)
    eye = np.eye(cin)
    tx = np.stack([
        np.concatenate([np.kron(np.cos(fine_x[i].T), eye), np.kron(np.sin(fine_x[i].T), eye)], axis=1)
        for i in range(A)
    ])
    eye8 = np.eye(8)

    def lines(ang):
        return np.concatenate([np.kron(np.cos(ang), eye8), np.kron(np.sin(ang), eye8)], axis=1)

    xi = np.stack([lines(half_x[i]) for i in range(A)])
    xf = np.ascontiguousarray(xi.reshape(-1, xi.shape[2]).T)
    xo = np.stack([lines(fine_x[i]) for i in range(A)])
    yf1 = y_table(B, yc, NY, H)
    yfc = y_table(B, yc // 2, NY // 2, H)

    def per_device(table):
        return jnp.asarray(np.ascontiguousarray(np.swapaxes(halves(table), 0, 1)))

    tx_t = per_device(tx)
    yf1_t = per_device(yf1)
    yfc_t = per_device(yfc)
    yic_t = per_device(np.swapaxes(yfc, 1, 2))
    yi2_t = per_device(np.swapaxes(yf1, 1, 2))
    xi_t = per_device(xi)
    xo_t = per_device(xo)
    xf_t = jnp.asarray(halves(xf))

    weights2 = jnp.swapaxes(spectral_out, 3, 4)

    operands = [
        fields, lift.T, lift_bias[None], bypass_in.T, bias_in[None], bypass_out, bias_out[None], proj,
        proj_bias[None], jnp.asarray(tzf),
        jnp.asarray(tzi), spectral_in, weights2, tx_t, yf1_t, yfc_t, yic_t, yi2_t, xf_t, xi_t, xo_t,
    ]
    anywhere = pl.BlockSpec(memory_space=pl.ANY)
    V = pltpu.VMEM
    return pl.pallas_call(
        functools.partial(
            kernel, A, B, xc, yc, 1.0 / math.sqrt(cells), 1.0 / math.sqrt(cells / 4.0), math.sqrt(cells)
        ),
        out_shape=pltpu.VMEM((cin, xc, yc, zc), F32),
        in_specs=[anywhere] * len(operands),
        out_specs=pl.BlockSpec(memory_space=pltpu.VMEM),
        scratch_shapes=[
            V((xc, cin, yc, zc), F32), V((xc * cin, yc * zc), F32),
        ] + [V(v.shape, v.dtype) for v in operands[1:10]] + [
            V((2, YB * GROUP * cin, zc), F32),
            V(tzi.shape, BF16), V(spectral_in.shape, F32), V(weights2.shape, F32),
            V(tx_t.shape[1:], BF16), V(yf1_t.shape[1:], BF16), V((S,) + yfc_t.shape[1:], BF16),
            V((S,) + yic_t.shape[1:], BF16), V(yi2_t.shape[1:], BF16), V(xf_t.shape, BF16), V(xi_t.shape, BF16),
            V(xo_t.shape[1:], BF16),
            V((N, cin, LB), F32), V((N, cin, LB), F32), V((LB, LB), F32),
            V((A * S, CQ, LB), F32), V((N, CQ, LB), F32), V((S, KX, CQ, LB), F32), V((A, S, KX, CQ, LB), F32),
            V((A * S, hx * cin, width), F32), V((S * HX, 16, width), BF16),
            V((S * HX // G1, G1 * CQ, LB), F32), V((S * HX // G1, G1 * CQ, LB), F32), V((hx // GROUP, GROUP * C2, LB), F32),
            V((N, CQ, LB), F32), V((N, CQ, LB), F32), V((N, C1, LB), F32),
            V((xc // GROUP, 2, GROUP * C1, LB), F32),
            V((hx, C1, width), F32), V((xc, 16, yc * zc), BF16), V((16, yc * zc), F32),
            V((GROUP * C2, max(GROUP * C2, G1 * 16)), F32), V((A * S, CQ, 16), F32),
            pltpu.SemaphoreType.DMA((cin,)),
            pltpu.SemaphoreType.DMA((18 + 2 * S,)),
            pltpu.SemaphoreType.DMA((9 + S,)), pltpu.SemaphoreType.DMA((9 + S + A * B // 2 + A * S // 2,)),
        ],
        compiler_params=pltpu.CompilerParams(
            collective_id=0, has_side_effects=True, vmem_limit_bytes=60 * 1024 * 1024
        ),
    )(*operands)


def solution(mesh):
    A = mesh.shape["gx"]
    B = mesh.shape["gy"]
    in_specs = (
        P(None, "gx", "gy", None), P(), P(), P(("gx", "gy"), None, None, None, None), P(), P(),
        P(("gx", "gy"), None, None, None, None), P(), P(), P(), P(),
    )
    return jax.shard_map(
        functools.partial(on_device, A, B), mesh=mesh, in_specs=in_specs,
        out_specs=P(None, "gx", "gy", None), check_vma=False,
    )
```

```python
import functools
import math

import jax
import jax.numpy as jnp
import numpy as np
from jax import lax
from jax.experimental import pallas as pl
from jax.experimental.pallas import tpu as pltpu
from jax.sharding import PartitionSpec as P

KX = 16
KY = 16
KZ = 8
YB = 8
LB = 128
GROUP = 4
FINE = 8
F32 = jnp.float32
BF16 = jnp.bfloat16
MESH = pl.DeviceIdType.MESH


def freq(count):
    f = np.arange(count)
    return np.where(f < count // 2, f, f - count)


def halves(table):
    high = table.astype(np.float32).astype(jnp.bfloat16)
    low = (table - high.astype(np.float64)).astype(np.float32).astype(jnp.bfloat16)
    return np.stack([high, low])


def stacked(table):
    high, low = halves(table)
    return np.concatenate([high, high, low], axis=0)


def angles(places, frequency, length):
    turns = np.mod(places[:, None] * frequency[None, :], length)
    return turns * (2.0 * math.pi / length)


def z_table(z_length):
    ang = angles(np.arange(z_length), np.arange(KZ), z_length)
    table = np.zeros((YB, z_length, 2, YB, KZ))
    for y in range(YB):
        table[y, :, 0, y] = np.cos(ang)
        table[y, :, 1, y] = -np.sin(ang)
    return table.reshape(YB * z_length, LB)


def y_table(blocks, cells, length, groups):
    per = KY // groups
    frequency = freq(KY)
    out = np.zeros((blocks, cells // YB, 2, YB, KZ, groups, LB))
    for b in range(blocks):
        ang = angles(b * cells + np.arange(cells), frequency, length)
        for y in range(cells):
            for j in range(KY):
                c, s = np.cos(ang[y, j]), np.sin(ang[y, j])
                for k in range(KZ):
                    re = (j % per) * KZ + k
                    im = per * KZ + re
                    at = (b, y // YB)
                    out[at + (0, y % YB, k, j // per, re)] = c
                    out[at + (1, y % YB, k, j // per, re)] = s
                    out[at + (0, y % YB, k, j // per, im)] = -s
                    out[at + (1, y % YB, k, j // per, im)] = c
    return out.reshape(blocks, cells // YB * LB, groups * LB)


def x_angles(blocks, cells, length):
    return angles(np.arange(blocks * cells), freq(KX), length).reshape(blocks, cells, KX)


def split(value):
    high = value.astype(BF16)
    return high, (value - high.astype(F32)).astype(BF16)


def mul(a, b):
    return jnp.dot(a, b, preferred_element_type=F32)


def tall(a):
    return jnp.concatenate([a[0], a[1], a[0]], axis=1)


def deep(a):
    return jnp.concatenate([a[0], a[1], a[0]], axis=0)


def wide(a):
    return jnp.concatenate([a[0], a[0], a[1]], axis=1)


def mul3(a, b):
    return mul(a[0], b[0]) + (mul(a[1], b[0]) + mul(a[0], b[1]))


def wide_rows(a):
    return jnp.concatenate([a[0], a[0], a[1]], axis=0)


def left3(table, b):
    rows = table[0].shape[0]
    both = mul(jnp.concatenate([table[0], table[1]], axis=0), b[0])
    return both[:rows] + (both[rows:] + mul(table[0], b[1]))


def gelu(v):
    return (0.5 * v) * (1.0 + lax.erf(v * math.sqrt(0.5)))


def parts_of(A, H, channels):
    parts = 1
    while H % (2 * parts) == 0 and channels % (16 * parts * A) == 0:
        parts *= 2
    return parts


def kernel(
    A, B, cells_x, cells_y, scale1, scale2, gain,
    f_hbm, lift_hbm, lbias_hbm, byp_hbm, bi_hbm, wo_hbm, bo_hbm, pr_hbm, pb_hbm, tzf_hbm, tzi_hbm, w1_hbm, w2_hbm, tx_hbm, yf1_hbm, yfc_hbm, yic_hbm, yi2_hbm, xf_hbm, xi_hbm, xo_hbm,
    o_ref,
    fx, f_ref, lift_ref, lbias_ref, byp_ref, bi_ref, wo_ref, bo_ref, pr_ref, pb_ref, tzf_ref, os_ref,
    tzi_ref, w1, w2, tx, yf1, yfc, yic, yi2, xf, xi, xo,
    buf1, r1, mx, mt1, g1, lines, yall, pg, pk_ref, lw, ones, vx, zc, vn, buf2, r3, ag2, vf, nar, fk_ref, t16, bd, bpq,
    fsem, csem, ssem, rsem,
):
    a = lax.axis_index("gx")
    b = lax.axis_index("gy")
    me = a * B + b
    IL = KX // A
    H = B // IL
    J = KY // H
    N = A * B
    X = A // 2
    CIN, C1 = lift_ref.shape
    C2 = wo_ref.shape[1]
    S = parts_of(A, H, C2)
    CQ = C2 // (A * S)
    CG = CQ // 8
    hx = cells_x // 2
    HX = hx * A
    G1 = GROUP * C2 // CQ
    part = lax.rem(b, S)
    base = b - part
    core = lax.rem(a, 2)
    sib = a + 1 - 2 * core

    fields = [pltpu.make_async_copy(f_hbm.at[c], fx.at[:, c], fsem.at[c]) for c in range(CIN)]
    pairs = [
        (tzf_hbm, tzf_ref), (tx_hbm.at[a], tx), (yf1_hbm.at[b], yf1), (lift_hbm, lift_ref), (lbias_hbm, lbias_ref),
        (byp_hbm, byp_ref), (bi_hbm, bi_ref), (wo_hbm, wo_ref), (bo_hbm, bo_ref), (pr_hbm, pr_ref), (pb_hbm, pb_ref),
        (w1_hbm, w1), (xi_hbm, xi), (tzi_hbm, tzi_ref), (xf_hbm, xf), (w2_hbm, w2), (yi2_hbm.at[b], yi2), (xo_hbm.at[a], xo),
    ] + [(yic_hbm.at[base + n], yic.at[n]) for n in range(S)] + [(yfc_hbm.at[base + n], yfc.at[n]) for n in range(S)]
    loads = [pltpu.make_async_copy(src, dst, csem.at[k]) for k, (src, dst) in enumerate(pairs)]
    l_tzf, l_tx, l_yf1 = loads[:3]
    l_w1, l_xi, l_tzi, l_xf, l_w2, l_yi2, l_xo = loads[11:18]
    for load in fields + loads[:3]:
        load.start()

    barrier = pltpu.get_barrier_semaphore()
    for step in range(1, N):
        peer = lax.rem(me + step, N)
        pl.semaphore_signal(
            barrier, inc=1, device_id=(peer // B, lax.rem(peer, B)), device_id_type=MESH
        )
    for load in loads[3:]:
        load.start()

    lane = lax.broadcasted_iota(jnp.int32, (1, LB), 1)
    sign_f = jnp.where(lane < LB // 2, 1.0, -1.0).astype(F32)

    def rot_f(v):
        return pltpu.roll(v, LB // 2, 1) * sign_f

    def rot_i(v):
        return pltpu.roll(v, LB // 2, 1) * -sign_f

    def remote(source, target, phase, slot, device):
        pltpu.make_async_remote_copy(
            src_ref=source, dst_ref=target, send_sem=ssem.at[phase], recv_sem=rsem.at[slot],
            device_id=device, device_id_type=MESH,
        ).start()

    def whole(target, phase, slot):
        return pltpu.make_async_remote_copy(
            src_ref=target, dst_ref=target, send_sem=ssem.at[phase], recv_sem=rsem.at[slot],
            device_id=(sib, b), device_id_type=MESH,
        )

    def arrive(target, slot):
        whole(target, 0, slot).wait_recv()

    def at(index):
        return (index // B, lax.rem(index, B))

    A2A, EXP1, RED, EXP2, LINE_PAIR, POOL, POOL_X, POOL_Y, POOL_XY, LINE = range(10)
    SPREAD = LINE + S
    NEAR = SPREAD + X * B

    width = tzi_ref.shape[1]
    for load in fields:
        load.wait()
    flat = fx.reshape(f_ref.shape[0] * cells_y, f_ref.shape[1] // cells_y)
    zn = flat.shape[1]
    for y in range(cells_y):
        f_ref[:, y * zn:(y + 1) * zn] = flat[pl.ds(y, f_ref.shape[0], stride=cells_y), :]
    l_tzf.wait()
    def wave(pair):
        both = mul(pair[0], tzf_ref[...])
        return both[:, :LB] + (both[:, LB:] + mul(pair[1], tzf_ref[:, :LB]))

    zs = wave(split(jnp.concatenate([f_ref[:, :width], f_ref[:, width:]], axis=0)))
    zs = [zs[:zs.shape[0] // 2], zs[zs.shape[0] // 2:]]
    l_tx.wait()
    us = []
    for z in zs:
        us.append(mul3((tx[0], tx[1]), split(jnp.concatenate([z, rot_f(z)], axis=0))))
    l_yf1.wait()
    parts = mul3(split(jnp.concatenate(us, axis=1)), (yf1[0], yf1[1]))
    for i in range(KX):
        for h in range(H):
            buf1[i * H + h] = parts[i * CIN:(i + 1) * CIN, h * LB:(h + 1) * LB]
    r1[me] = buf1[me]
    pl.semaphore_wait(barrier, N - 1)

    for step in range(1, N):
        peer = lax.rem(me + step, N)
        remote(buf1.at[peer], r1.at[me], A2A, A2A, at(peer))

    for x in range(hx):
        both = f_ref[2 * x * CIN:(2 * x + 1) * CIN] + f_ref[(2 * x + 1) * CIN:(2 * x + 2) * CIN]
        pieces = [
            both[:, 2 * y * zn:(2 * y + 1) * zn] + both[:, (2 * y + 1) * zn:(2 * y + 2) * zn]
            for y in range(YB)
        ]
        pg[a * S + part, x * CIN:(x + 1) * CIN] = jnp.concatenate(pieces, axis=1) * 0.25

    def near_slot(phase, step):
        return NEAR + (phase - LINE) * X + step

    square = X == 2 and S == 2
    mate = lax.rem(a + 2, A)
    other = S - 1 - part

    def share_send(buffer):
        own = buffer.at[a * S + part]
        if square:
            remote(own, own, POOL, POOL_X, (mate, b))
            remote(own, own, POOL, POOL_Y, (a, base + other))
            remote(own, own, POOL, POOL, (sib, b))
        else:
            for ia in range(A):
                for turn in range(S):
                    if ia or turn:
                        remote(own, own, POOL, POOL, (lax.rem(a + ia, A), base + member(turn)))

    def share_relay(buffer):
        if square:
            left = buffer.at[mate * S + part]
            right = buffer.at[a * S + other]
            arrive(left, POOL_X)
            arrive(right, POOL_Y)
            ia = a * core + mate * (1 - core)
            ip = other * core + part * (1 - core)
            target = (mate * core + a * (1 - core), b * core + (base + other) * (1 - core))
            relayed = buffer.at[ia * S + ip]
            remote(relayed, relayed, POOL, POOL_XY, target)
            remote(left, left, POOL, POOL, (sib, b))
            remote(right, right, POOL, POOL, (sib, b))

    def share_last(buffer):
        if square:
            corner = buffer.at[mate * S + other]
            arrive(corner, POOL_XY)
            remote(corner, corner, POOL, POOL, (sib, b))

    def share_finish(buffer):
        arrive(buffer.at[pl.ds(0, A * S // 2 if square else A * S - 1)], POOL)

    def member(turn):
        return lax.rem(part + turn, S)

    def pair_finish(buffer, phase):
        if S > 1:
            arrive(buffer.at[0, pl.ds(0, S - 1)], phase)

    def near_send(buffer, phase, turn):
        own = buffer.at[a, member(turn)]
        for step in range(1, X):
            remote(own, own, phase + turn, near_slot(phase + turn, step), (lax.rem(a + 2 * step, A), b))
        remote(own, own, phase + turn, phase + turn, (sib, b))

    def near_forward(buffer, phase, turn):
        for step in range(1, X):
            other = buffer.at[lax.rem(a + A - 2 * step, A), member(turn)]
            arrive(other, near_slot(phase + turn, step))
            remote(other, other, phase + turn, phase + turn, (sib, b))

    def near_finish(buffer, phase, turn):
        arrive(buffer.at[pl.ds(0, X), 0], phase + turn)

    share_send(pg)

    for load in loads[3:12]:
        load.wait()
    mx[...] = jnp.zeros_like(mx)
    mx[0:CIN, :C1] = lift_ref[...]
    mx[CIN:CIN + 1, :C1] = lbias_ref[...]
    mx[CIN + 1:CIN + 2, :C1] = bo_ref[...]
    lift8 = jnp.concatenate([mx[0:8, :C1]], axis=0)
    columns = mx[...].T[:C1]
    bo_col = columns[:, CIN + 1:CIN + 2]

    def left16(matrix, bias):
        n = matrix.shape[1]
        high, low = split(matrix[0:CIN])
        b0 = bias.astype(BF16)
        rest = bias - b0.astype(F32)
        b1 = rest.astype(BF16)
        b2 = (rest - b1.astype(F32)).astype(BF16)
        mx[...] = jnp.zeros_like(mx)
        mx[0:CIN, :n] = high.astype(F32)
        mx[CIN:2 * CIN, :n] = high.astype(F32)
        mx[2 * CIN:3 * CIN, :n] = low.astype(F32)
        for row, value in enumerate((b0, b1, b2)):
            mx[3 * CIN + row:3 * CIN + row + 1, :n] = value.astype(F32)
        return mx[...].T[:n, :16].astype(BF16)

    highest = lax.Precision.HIGHEST
    eighth = lax.broadcasted_iota(jnp.int32, (1, ones.shape[1]), 1) // 8
    m = jnp.dot(lift8, byp_ref[...], precision=highest, preferred_element_type=F32)
    bp16 = left16(m, m[CIN:CIN + 1] + bi_ref[...])
    m = lax.dot_general(
        lift8, pr_ref[...], (((1,), (1,)), ((), ())), precision=highest, preferred_element_type=F32
    )
    pl16 = left16(m, m[CIN:CIN + 1] + pb_ref[...])
    t16[...] = jnp.ones_like(t16)

    def diagonal(value, count):
        rows, cols = value.shape
        bd[...] = jnp.zeros_like(bd)
        for g in range(count):
            bd[g * rows:(g + 1) * rows, g * cols:(g + 1) * cols] = value
        return bd[0:count * rows, 0:count * cols]

    bp_all = bp16.astype(F32)
    for q in range(A * S):
        bpq[q] = bp_all[q * CQ:(q + 1) * CQ]
    bq_bd = diagonal(bpq[a * S + part], min(G1, 16)).astype(BF16)
    bp_bd = diagonal(bp_all, GROUP).astype(BF16)
    pl_bd = diagonal(pl16.astype(F32), FINE).astype(BF16)
    wo_bd = wide(split(diagonal(wo_ref[...], GROUP)))
    pr_bd = split(diagonal(pr_ref[...], FINE))
    Q = J * KZ
    lifts = tall(split(lift8))
    for j in range(J):
        for k in range(KZ):
            both = []
            for n in range(2):
                both.append(mul(lifts, wide_rows(split(w1[j, n, k]))))
            lw[0, j * KZ + k] = jnp.concatenate([both[0], both[1]], axis=1)
            lw[1, j * KZ + k] = jnp.concatenate([-both[1], both[0]], axis=1)
    for row in range(Q):
        ones[row:row + 1] = jnp.where(eighth == row, 1.0, 0.0).astype(F32)
    blocks = ones[...].astype(BF16)
    arrive(r1.at[pl.ds(0, N - 1)], A2A)

    s4 = jnp.sum(r1[...], axis=0) * scale1
    first = jnp.where((lane == 0) & (me == 0), gain, 0.0).astype(F32)
    mx[...] = jnp.zeros_like(mx)
    mx[0:CIN] = s4
    mx[CIN:CIN + 1] = first
    s8 = mx[0:8]
    mixed = split(jnp.concatenate(
        [s8[:, q:q + 1] * lw[0, q] + s8[:, Q + q:Q + q + 1] * lw[1, q] for q in range(Q)], axis=0
    ))
    mx[0:Q] = mul(blocks, mixed[0]) + mul(blocks, mixed[1])
    turned = mx[...].T
    mixed = turned[:C2] + pltpu.roll(turned[C2:], Q, 1)
    for q in range(A * S):
        mt1[q] = mixed[q * CQ:(q + 1) * CQ]
    g1[me] = mt1[a * S + part]
    for step in range(1, N):
        pa, pb = at(lax.rem(me + step, N))
        remote(mt1.at[pa * S + lax.rem(pb, S)], g1.at[me], EXP1, EXP1, (pa, pb))

    def fill(value):
        n = value.shape[1]
        high, low = split(value)
        t16[0:CIN, :n] = high.astype(F32)
        t16[CIN:2 * CIN, :n] = low.astype(F32)
        t16[2 * CIN:3 * CIN, :n] = high.astype(F32)
        return t16[:, :n].astype(BF16)

    def fill_pooled(ia, ip):
        for x in range(hx):
            pk_ref[ip * HX + ia * hx + x] = fill(pg[ia * S + ip, x * CIN:(x + 1) * CIN])

    share_relay(pg)
    for x in range(cells_x):
        fk_ref[x] = fill(f_ref[x * CIN:(x + 1) * CIN])
    if square:
        fill_pooled(a, part)
        fill_pooled(mate, part)
        fill_pooled(a, other)
        share_last(pg)
        fill_pooled(mate, other)
    for load in loads[18:18 + S]:
        load.wait()
    arrive(g1.at[pl.ds(0, N - 1)], EXP1)
    rows = jnp.concatenate(
        [jnp.concatenate([g1[i * H + h] for h in range(H)], axis=1) for i in range(KX)], axis=0
    )
    tables = tuple(jnp.concatenate([yic[n, k] for n in range(S)], axis=1) for k in range(2))
    y = mul3(split(rows), tables)
    for n in range(S):
        for i in range(KX):
            lines[n, i] = y[i * CQ:(i + 1) * CQ, n * LB:(n + 1) * LB]
    for turn in range(1, S):
        remote(lines.at[member(turn)], yall.at[a, part], LINE_PAIR, LINE_PAIR, (a, base + member(turn)))
    for i in range(KX):
        yall[a, part, i] = lines[part, i]
    near_send(yall, LINE, 0)

    def modes(value, rows_each):
        groups = rows_each // 8
        turned = rot_i(value)
        parts = []
        for g in range(groups):
            parts.append(jnp.concatenate([
                v[i * rows_each + g * 8:i * rows_each + g * 8 + 8] for v in (value, turned) for i in range(KX)
            ], axis=0))
        return parts

    l_xi.wait()
    table = tuple(jnp.concatenate([xi[q, k] for q in range(A)], axis=0) for k in range(2))
    halves_y = []
    for n in range(S):
        halves_y += modes(y[:, n * LB:(n + 1) * LB], CQ)
    v = left3(table, split(jnp.concatenate(halves_y, axis=1)))
    steps = HX // G1
    for n in range(S):
        for s in range(steps):
            vx[n * steps + s] = jnp.concatenate([
                v[(s * G1 + xx) * 8:(s * G1 + xx) * 8 + 8, (n * CG + g) * LB:(n * CG + g + 1) * LB]
                for xx in range(G1) for g in range(CG)
            ], axis=0)

    def coarse_step(s, carry):
        v = mul(tall(split(vx[s])), tzi_ref[...])
        count = min(G1, 16)
        near = jnp.concatenate([
            mul(bq_bd, jnp.concatenate([pk_ref[s * G1 + g + xx] for xx in range(count)], axis=0))
            for g in range(0, G1, count)
        ], axis=0)
        g = split(gelu(v + near))
        zc[s] = wave(g)
        return carry

    share_finish(pg)
    for ia in (sib, lax.rem(sib + 2, A)) if square else range(A):
        for ip in range(S):
            fill_pooled(ia, ip)
    l_tzi.wait()
    lax.fori_loop(0, S * steps, coarse_step, 0)

    l_xf.wait()
    for load in loads[18 + S:]:
        load.wait()
    z = jnp.concatenate([
        jnp.concatenate([
            zc[n * steps + s, xx * CQ + g * 8:xx * CQ + g * 8 + 8] for s in range(steps) for xx in range(G1)
        ], axis=0) for n in range(S) for g in range(CG)
    ], axis=1)
    z = mul(wide((xf[0], xf[1])), deep(split(z)))

    def spectrum(first, n):
        return jnp.concatenate([
            z[(first + i) * 8:(first + i + 1) * 8, (n * CG + g) * LB:(n * CG + g + 1) * LB]
            for i in range(KX) for g in range(CG)
        ], axis=0)

    value = jnp.concatenate([spectrum(0, n) + rot_f(spectrum(KX, n)) for n in range(S)], axis=1)
    tables = tuple(jnp.concatenate([yfc[n, k] for n in range(S)], axis=0) for k in range(2))
    out = mul3(split(value), tables)
    for i in range(KX):
        for h in range(H):
            buf2[i * H + h] = out[i * CQ:(i + 1) * CQ, h * LB:(h + 1) * LB]
    for step in range(1, N):
        peer = lax.rem(me + step, N)
        remote(buf2.at[peer], r3.at[me], RED, RED, at(peer))
    r3[me] = buf2[me]

    pair_finish(yall, LINE_PAIR)
    for turn in range(1, S):
        near_send(yall, LINE, turn)
    near_forward(yall, LINE, 0)
    l_w2.wait()
    arrive(r3.at[pl.ds(0, N - 1)], RED)
    for turn in range(1, S):
        near_forward(yall, LINE, turn)
    sums = []
    for q in range(A):
        for n in range(S):
            total = r3[q * B + n]
            for t in range(S + n, B, S):
                total = total + r3[q * B + t]
            sums.append(total)
    st = (jnp.concatenate(sums, axis=0) * scale2).T
    mixed = jnp.zeros((C1, LB), F32)
    for j in range(J):
        for k in range(KZ):
            q = j * KZ + k
            re = st[q:q + 1]
            im = st[Q + q:Q + q + 1]
            wr = w2[j, 0, k]
            wi = w2[j, 1, k]
            real = jnp.sum(re * wr - im * wi, axis=1, keepdims=True)
            imag = jnp.sum(re * wi + im * wr, axis=1, keepdims=True)
            mixed = jnp.where(lane == q, real, jnp.where(lane == Q + q, imag, mixed))
    ag2[me] = mixed

    def flip(t):
        value = b
        bit = 1
        while bit < B:
            if t & bit:
                value = value + bit - 2 * bit * lax.rem(b // bit, 2)
            bit *= 2
        return value

    NEARBY = B // 2

    def spread(t):
        source = a * B + flip(t)
        for step in range(1, X):
            remote(
                ag2.at[source], ag2.at[source], EXP2, SPREAD + step * B + t, (lax.rem(a + 2 * step, A), b)
            )
            if t >= NEARBY:
                remote(ag2.at[source], ag2.at[source], EXP2, EXP2, (lax.rem(sib + 2 * step, A), b))
        remote(ag2.at[source], ag2.at[source], EXP2, EXP2, (sib, b))

    for t in range(B - 1, 0, -1):
        remote(ag2.at[me], ag2.at[me], EXP2, SPREAD + t, (a, flip(t)))
    spread(0)
    for turn in range(S):
        near_finish(yall, LINE, turn)
    parts = []
    for q in range(A):
        for n in range(S):
            parts += modes(jnp.concatenate([yall[q, n, i] for i in range(KX)], axis=0), CQ)
    v = left3((xi[a, 0], xi[a, 1]), split(jnp.concatenate(parts, axis=1)))
    for s in range(hx // GROUP):
        vn[s] = jnp.concatenate([
            v[(s * GROUP + xx) * 8:(s * GROUP + xx) * 8 + 8, g * LB:(g + 1) * LB]
            for xx in range(GROUP) for g in range(C2 // 8)
        ], axis=0)

    def narrow_step(s, carry):
        v = mul(tall(split(vn[s])), tzi_ref[...])
        near = jnp.concatenate([pk_ref[part * HX + a * hx + s * GROUP + xx] for xx in range(GROUP)], axis=0)
        g = split(gelu(v + mul(bp_bd, near)))
        narrow = mul(wo_bd, deep(g))
        for xx in range(GROUP):
            nar[s * GROUP + xx] = narrow[xx * C1:(xx + 1) * C1]
        return carry

    lax.fori_loop(0, hx // GROUP, narrow_step, 0)

    for t in range(1, B):
        source = a * B + flip(t)
        arrive(ag2.at[source], SPREAD + t)
        spread(t)
    for t in range(B):
        for step in range(1, X):
            source = lax.rem(a + A - 2 * step, A) * B + flip(t)
            arrive(ag2.at[source], SPREAD + step * B + t)
            if t < NEARBY:
                remote(ag2.at[source], ag2.at[source], EXP2, EXP2, (sib, b))
    arrive(ag2.at[pl.ds(0, X * B)], EXP2)

    l_yi2.wait()
    l_xo.wait()
    rows = jnp.concatenate(
        [jnp.concatenate([ag2[i * H + h] for h in range(H)], axis=1) for i in range(KX)], axis=0
    )
    y = mul3(split(rows), (yi2[0], yi2[1]))
    halves_y = [modes(y[:, ch * LB:(ch + 1) * LB], C1) for ch in range(2)]
    v = left3((xo[0], xo[1]), split(jnp.concatenate(halves_y[0] + halves_y[1], axis=1)))
    CF = C1 // 8
    for s in range(cells_x // FINE):
        for ch in range(2):
            vf[s, ch] = jnp.concatenate([
                v[(s * FINE + xx) * 8:(s * FINE + xx) * 8 + 8, (ch * CF + g) * LB:(ch * CF + g + 1) * LB]
                for xx in range(FINE) for g in range(CF)
            ], axis=0)

    def fine_step(group, carry):
        near = jnp.concatenate([fk_ref[group * FINE + xx] for xx in range(FINE)], axis=0)
        for ch in range(2):
            v = mul(tall(split(vf[group, ch])), tzi_ref[...])
            rows = []
            for xx in range(0, FINE, 2):
                half = nar.at[group * (FINE // 2) + xx // 2]
                pieces = []
                for yy in range(YB):
                    at_y = (ch * YB + yy) // 2 * zn
                    pieces.append(half[:, at_y:at_y + zn])
                rows += [jnp.concatenate(pieces, axis=1) + bo_col] * 2
            g = split(gelu(v + jnp.concatenate(rows, axis=0)))
            cols = slice(ch * width, (ch + 1) * width)
            res = left3(pr_bd, g) + mul(pl_bd, near[:, cols])
            for yy in range(YB):
                os_ref[ch, yy * FINE * CIN:(yy + 1) * FINE * CIN] = res[:, yy * zn:(yy + 1) * zn]
            for xx in range(FINE):
                for c in range(CIN):
                    o_ref[c, group * FINE + xx, ch * YB:(ch + 1) * YB] = os_ref[
                        ch, pl.ds(xx * CIN + c, YB, stride=FINE * CIN), :
                    ]
        return carry

    lax.fori_loop(0, cells_x // FINE, fine_step, 0, unroll=True)
    waits = [
        (A2A, buf1.at[pl.ds(0, N - 1)]), (EXP1, g1.at[pl.ds(0, N - 1)]), (RED, buf2.at[pl.ds(0, N - 1)]),
        (EXP2, ag2.at[pl.ds(0, N - 1)]),
    ]
    if S > 1:
        waits.append((LINE_PAIR, yall.at[0, pl.ds(0, S - 1)]))
    waits.append((POOL, pg.at[pl.ds(0, A * S - 1)]))
    for turn in range(S):
        waits.append((LINE + turn, yall.at[pl.ds(0, A - 1), 0]))
    for phase, target in waits:
        whole(target, phase, phase).wait_send()


def on_device(
    A, B, fields, lift, lift_bias, spectral_in, bypass_in, bias_in, spectral_out, bypass_out,
    bias_out, proj, proj_bias,
):
    cin, xc, yc, zc = fields.shape
    C1 = lift.shape[0]
    C2 = bypass_in.shape[0]
    NX = xc * A
    NY = yc * B
    IL = KX // A
    H = B // IL
    J = KY // H
    N = A * B
    width = YB * zc
    S = parts_of(A, H, C2)
    CQ = C2 // (A * S)
    hx = xc // 2
    HX = hx * A
    G1 = GROUP * C2 // CQ
    cells = float(NX * NY * zc)
    back = math.sqrt(2.0 / (KX * KY * KZ))

    tz = z_table(zc)
    tzf = np.concatenate(list(halves(tz)), axis=1)
    tzi = stacked(np.ascontiguousarray(tz.T) * back)
    fine_x = x_angles(A, xc, NX)
    half_x = x_angles(A, xc // 2, NX // 2)
    eye = np.eye(cin)
    tx = np.stack([
        np.concatenate([np.kron(np.cos(fine_x[i].T), eye), np.kron(np.sin(fine_x[i].T), eye)], axis=1)
        for i in range(A)
    ])
    eye8 = np.eye(8)

    def lines(ang):
        return np.concatenate([np.kron(np.cos(ang), eye8), np.kron(np.sin(ang), eye8)], axis=1)

    xi = np.stack([lines(half_x[i]) for i in range(A)])
    xf = np.ascontiguousarray(xi.reshape(-1, xi.shape[2]).T)
    xo = np.stack([lines(fine_x[i]) for i in range(A)])
    yf1 = y_table(B, yc, NY, H)
    yfc = y_table(B, yc // 2, NY // 2, H)

    def per_device(table):
        return jnp.asarray(np.ascontiguousarray(np.swapaxes(halves(table), 0, 1)))

    tx_t = per_device(tx)
    yf1_t = per_device(yf1)
    yfc_t = per_device(yfc)
    yic_t = per_device(np.swapaxes(yfc, 1, 2))
    yi2_t = per_device(np.swapaxes(yf1, 1, 2))
    xi_t = per_device(xi)
    xo_t = per_device(xo)
    xf_t = jnp.asarray(halves(xf))

    weights2 = jnp.swapaxes(spectral_out, 3, 4)

    operands = [
        fields, lift.T, lift_bias[None], bypass_in.T, bias_in[None], bypass_out, bias_out[None], proj,
        proj_bias[None], jnp.asarray(tzf),
        jnp.asarray(tzi), spectral_in, weights2, tx_t, yf1_t, yfc_t, yic_t, yi2_t, xf_t, xi_t, xo_t,
    ]
    anywhere = pl.BlockSpec(memory_space=pl.ANY)
    V = pltpu.VMEM
    return pl.pallas_call(
        functools.partial(
            kernel, A, B, xc, yc, 1.0 / math.sqrt(cells), 1.0 / math.sqrt(cells / 4.0), math.sqrt(cells)
        ),
        out_shape=pltpu.VMEM((cin, xc, yc, zc), F32),
        in_specs=[anywhere] * len(operands),
        out_specs=pl.BlockSpec(memory_space=pltpu.VMEM),
        scratch_shapes=[
            V((xc, cin, yc, zc), F32), V((xc * cin, yc * zc), F32),
        ] + [V(v.shape, v.dtype) for v in operands[1:10]] + [
            V((2, YB * FINE * cin, zc), F32),
            V(tzi.shape, BF16), V(spectral_in.shape, F32), V(weights2.shape, F32),
            V(tx_t.shape[1:], BF16), V(yf1_t.shape[1:], BF16), V((S,) + yfc_t.shape[1:], BF16),
            V((S,) + yic_t.shape[1:], BF16), V(yi2_t.shape[1:], BF16), V(xf_t.shape, BF16), V(xi_t.shape, BF16),
            V(xo_t.shape[1:], BF16),
            V((N, cin, LB), F32), V((N, cin, LB), F32), V((LB, LB), F32),
            V((A * S, CQ, LB), F32), V((N, CQ, LB), F32), V((S, KX, CQ, LB), F32), V((A, S, KX, CQ, LB), F32),
            V((A * S, hx * cin, width), F32), V((S * HX, 16, width), BF16),
            V((2, J * KZ, 8, 2 * C2), F32), V((J * KZ, J * KZ * 8), F32),
            V((S * HX // G1, G1 * CQ, LB), F32), V((S * HX // G1, G1 * CQ, LB), F32), V((hx // GROUP, GROUP * C2, LB), F32),
            V((N, CQ, LB), F32), V((N, CQ, LB), F32), V((N, C1, LB), F32),
            V((xc // FINE, 2, FINE * C1, LB), F32),
            V((hx, C1, width), F32), V((xc, 16, yc * zc), BF16), V((16, yc * zc), F32),
            V((GROUP * C2, GROUP * C2), F32), V((A * S, CQ, 16), F32),
            pltpu.SemaphoreType.DMA((cin,)),
            pltpu.SemaphoreType.DMA((18 + 2 * S,)),
            pltpu.SemaphoreType.DMA((9 + S,)), pltpu.SemaphoreType.DMA((9 + S + A * B // 2 + A * S // 2,)),
        ],
        compiler_params=pltpu.CompilerParams(
            collective_id=0, has_side_effects=True, vmem_limit_bytes=60 * 1024 * 1024
        ),
    )(*operands)


def solution(mesh):
    A = mesh.shape["gx"]
    B = mesh.shape["gy"]
    in_specs = (
        P(None, "gx", "gy", None), P(), P(), P(("gx", "gy"), None, None, None, None), P(), P(),
        P(("gx", "gy"), None, None, None, None), P(), P(), P(), P(),
    )
    return jax.shard_map(
        functools.partial(on_device, A, B), mesh=mesh, in_specs=in_specs,
        out_specs=P(None, "gx", "gy", None), check_vma=False,
    )
```

```python
import functools
import math

import jax
import jax.numpy as jnp
import numpy as np
from jax import lax
from jax.experimental import pallas as pl
from jax.experimental.pallas import tpu as pltpu
from jax.sharding import PartitionSpec as P

KX = 16
KY = 16
KZ = 8
YB = 8
LB = 128
GROUP = 4
FINE = 8
F32 = jnp.float32
BF16 = jnp.bfloat16
MESH = pl.DeviceIdType.MESH


def freq(count):
    f = np.arange(count)
    return np.where(f < count // 2, f, f - count)


def halves(table):
    high = table.astype(np.float32).astype(jnp.bfloat16)
    low = (table - high.astype(np.float64)).astype(np.float32).astype(jnp.bfloat16)
    return np.stack([high, low])


def stacked(table):
    high, low = halves(table)
    return np.concatenate([high, high, low], axis=0)


def angles(places, frequency, length):
    turns = np.mod(places[:, None] * frequency[None, :], length)
    return turns * (2.0 * math.pi / length)


def z_table(z_length):
    ang = angles(np.arange(z_length), np.arange(KZ), z_length)
    table = np.zeros((YB, z_length, 2, YB, KZ))
    for y in range(YB):
        table[y, :, 0, y] = np.cos(ang)
        table[y, :, 1, y] = -np.sin(ang)
    return table.reshape(YB * z_length, LB)


def y_table(blocks, cells, length, groups):
    per = KY // groups
    frequency = freq(KY)
    out = np.zeros((blocks, cells // YB, 2, YB, KZ, groups, LB))
    for b in range(blocks):
        ang = angles(b * cells + np.arange(cells), frequency, length)
        for y in range(cells):
            for j in range(KY):
                c, s = np.cos(ang[y, j]), np.sin(ang[y, j])
                for k in range(KZ):
                    re = (j % per) * KZ + k
                    im = per * KZ + re
                    at = (b, y // YB)
                    out[at + (0, y % YB, k, j // per, re)] = c
                    out[at + (1, y % YB, k, j // per, re)] = s
                    out[at + (0, y % YB, k, j // per, im)] = -s
                    out[at + (1, y % YB, k, j // per, im)] = c
    return out.reshape(blocks, cells // YB * LB, groups * LB)


def x_angles(blocks, cells, length):
    return angles(np.arange(blocks * cells), freq(KX), length).reshape(blocks, cells, KX)


def split(value):
    high = value.astype(BF16)
    return high, (value - high.astype(F32)).astype(BF16)


def mul(a, b):
    return jnp.dot(a, b, preferred_element_type=F32)


def tall(a):
    return jnp.concatenate([a[0], a[1], a[0]], axis=1)


def deep(a):
    return jnp.concatenate([a[0], a[1], a[0]], axis=0)


def wide(a):
    return jnp.concatenate([a[0], a[0], a[1]], axis=1)


def mul3(a, b):
    return mul(a[0], b[0]) + (mul(a[1], b[0]) + mul(a[0], b[1]))


def wide_rows(a):
    return jnp.concatenate([a[0], a[0], a[1]], axis=0)


def left3(table, b):
    rows = table[0].shape[0]
    both = mul(jnp.concatenate([table[0], table[1]], axis=0), b[0])
    return both[:rows] + (both[rows:] + mul(table[0], b[1]))


def gelu(v):
    return (0.5 * v) * (1.0 + lax.erf(v * math.sqrt(0.5)))


def parts_of(A, H, channels):
    parts = 1
    while H % (2 * parts) == 0 and channels % (16 * parts * A) == 0:
        parts *= 2
    return parts


def kernel(
    A, B, cells_x, cells_y, scale1, scale2, gain,
    f_hbm, lift_hbm, lbias_hbm, byp_hbm, bi_hbm, wo_hbm, bo_hbm, pr_hbm, pb_hbm, tzf_hbm, tzi_hbm, w1_hbm, w2_hbm, tx_hbm, yf1_hbm, yfc_hbm, yic_hbm, yi2_hbm, xf_hbm, xi_hbm, xo_hbm,
    o_ref,
    fx, f_ref, lift_ref, lbias_ref, byp_ref, bi_ref, wo_ref, bo_ref, pr_ref, pb_ref, tzf_ref, os_ref,
    tzi_ref, w1, w2, tx, yf1, yfc, yic, yi2, xf, xi, xo,
    buf1, r1, mx, mt1, g1, lines, yall, pg, pk_ref, lw, ones, ye, vx, zc, vn, buf2, r3, ag2, vf, nar, fk_ref, t16, bd, bpq,
    fsem, csem, ssem, rsem,
):
    a = lax.axis_index("gx")
    b = lax.axis_index("gy")
    me = a * B + b
    IL = KX // A
    H = B // IL
    J = KY // H
    N = A * B
    X = A // 2
    CIN, C1 = lift_ref.shape
    C2 = wo_ref.shape[1]
    S = parts_of(A, H, C2)
    CQ = C2 // (A * S)
    CG = CQ // 8
    hx = cells_x // 2
    HX = hx * A
    G1 = GROUP * C2 // CQ
    part = lax.rem(b, S)
    base = b - part
    core = lax.rem(a, 2)
    sib = a + 1 - 2 * core

    def flip(t):
        value = b
        bit = 1
        while bit < B:
            if t & bit:
                value = value + bit - 2 * bit * lax.rem(b // bit, 2)
            bit *= 2
        return value

    lines_b = [flip(t) for t in range(B)]
    lines_a = [lax.rem(a + ia, A) for ia in range(A)]
    peers = [(lines_a[ia], lines_b[t]) for t in reversed(range(B)) for ia in reversed(range(A)) if t or ia]

    fields = [pltpu.make_async_copy(f_hbm.at[c], fx.at[:, c], fsem.at[c]) for c in range(CIN)]
    pairs = [
        (tzf_hbm, tzf_ref), (tx_hbm.at[a], tx), (yf1_hbm.at[b], yf1), (lift_hbm, lift_ref), (lbias_hbm, lbias_ref),
        (byp_hbm, byp_ref), (bi_hbm, bi_ref), (wo_hbm, wo_ref), (bo_hbm, bo_ref), (pr_hbm, pr_ref), (pb_hbm, pb_ref),
        (w1_hbm, w1), (xi_hbm, xi), (tzi_hbm, tzi_ref), (xf_hbm, xf), (w2_hbm, w2), (yi2_hbm.at[b], yi2), (xo_hbm.at[a], xo),
    ] + [(yic_hbm.at[base + n], yic.at[n]) for n in range(S)] + [(yfc_hbm.at[base + n], yfc.at[n]) for n in range(S)]
    loads = [pltpu.make_async_copy(src, dst, csem.at[k]) for k, (src, dst) in enumerate(pairs)]
    l_tzf, l_tx, l_yf1 = loads[:3]
    l_w1, l_xi, l_tzi, l_xf, l_w2, l_yi2, l_xo = loads[11:18]
    for load in fields + loads[:3]:
        load.start()

    barrier = pltpu.get_barrier_semaphore()
    for pa, pb in peers:
        pl.semaphore_signal(barrier, inc=1, device_id=(pa, pb), device_id_type=MESH)
    for load in loads[3:]:
        load.start()

    lane = lax.broadcasted_iota(jnp.int32, (1, LB), 1)
    sign_f = jnp.where(lane < LB // 2, 1.0, -1.0).astype(F32)

    def rot_f(v):
        return pltpu.roll(v, LB // 2, 1) * sign_f

    def rot_i(v):
        return pltpu.roll(v, LB // 2, 1) * -sign_f

    def remote(source, target, phase, slot, device):
        pltpu.make_async_remote_copy(
            src_ref=source, dst_ref=target, send_sem=ssem.at[phase], recv_sem=rsem.at[slot],
            device_id=device, device_id_type=MESH,
        ).start()

    def whole(target, phase, slot):
        return pltpu.make_async_remote_copy(
            src_ref=target, dst_ref=target, send_sem=ssem.at[phase], recv_sem=rsem.at[slot],
            device_id=(sib, b), device_id_type=MESH,
        )

    def arrive(target, slot):
        whole(target, 0, slot).wait_recv()

    A2A, EXP1, RED, EXP2, LINE_PAIR, POOL, POOL_X, POOL_Y, POOL_XY, POOL_LAST, LINE = range(11)
    SPREAD = LINE + S
    NEAR = SPREAD + X * B

    width = tzi_ref.shape[1]
    for load in fields:
        load.wait()
    flat = fx.reshape(f_ref.shape[0] * cells_y, f_ref.shape[1] // cells_y)
    zn = flat.shape[1]
    for y in range(cells_y):
        f_ref[:, y * zn:(y + 1) * zn] = flat[pl.ds(y, f_ref.shape[0], stride=cells_y), :]
    l_tzf.wait()
    def wave(pair):
        both = mul(pair[0], tzf_ref[...])
        return both[:, :LB] + (both[:, LB:] + mul(pair[1], tzf_ref[:, :LB]))

    zs = wave(split(jnp.concatenate([f_ref[:, :width], f_ref[:, width:]], axis=0)))
    zs = [zs[:zs.shape[0] // 2], zs[zs.shape[0] // 2:]]
    l_tx.wait()
    us = []
    for z in zs:
        us.append(mul3((tx[0], tx[1]), split(jnp.concatenate([z, rot_f(z)], axis=0))))
    l_yf1.wait()
    parts = mul3(split(jnp.concatenate(us, axis=1)), (yf1[0], yf1[1]))
    for i in range(KX):
        for h in range(H):
            buf1[i * H + h] = parts[i * CIN:(i + 1) * CIN, h * LB:(h + 1) * LB]
    r1[me] = buf1[me]
    pl.semaphore_wait(barrier, N - 1)

    for pa, pb in peers:
        remote(buf1.at[pa * B + pb], r1.at[me], A2A, A2A, (pa, pb))

    for x in range(hx):
        both = f_ref[2 * x * CIN:(2 * x + 1) * CIN] + f_ref[(2 * x + 1) * CIN:(2 * x + 2) * CIN]
        pieces = [
            both[:, 2 * y * zn:(2 * y + 1) * zn] + both[:, (2 * y + 1) * zn:(2 * y + 2) * zn]
            for y in range(YB)
        ]
        pg[a * S + part, x * CIN:(x + 1) * CIN] = jnp.concatenate(pieces, axis=1) * 0.25

    def near_slot(phase, step):
        return NEAR + (phase - LINE) * X + step

    square = X == 2 and S == 2
    mate = lax.rem(a + 2, A)
    other = S - 1 - part

    def share_send(buffer):
        own = buffer.at[a * S + part]
        if square:
            remote(own, own, POOL, POOL_X, (mate, b))
            remote(own, own, POOL, POOL_Y, (a, base + other))
            remote(own, own, POOL, POOL, (sib, b))
        else:
            for ia in range(A):
                for turn in range(S):
                    if ia or turn:
                        remote(own, own, POOL, POOL, (lax.rem(a + ia, A), base + member(turn)))

    def share_relay(buffer):
        if square:
            left = buffer.at[mate * S + part]
            right = buffer.at[a * S + other]
            arrive(left, POOL_X)
            arrive(right, POOL_Y)
            ia = a * core + mate * (1 - core)
            ip = other * core + part * (1 - core)
            target = (mate * core + a * (1 - core), b * core + (base + other) * (1 - core))
            relayed = buffer.at[ia * S + ip]
            remote(relayed, relayed, POOL, POOL_XY, target)
            remote(left, left, POOL, POOL, (sib, b))
            remote(right, right, POOL, POOL, (sib, b))

    def share_last(buffer):
        if square:
            corner = buffer.at[mate * S + other]
            arrive(corner, POOL_XY)
            remote(corner, corner, POOL, POOL_LAST, (sib, b))

    def share_finish(buffer):
        arrive(buffer.at[pl.ds(0, A * S // 2 - 1 if square else A * S - 1)], POOL)

    def member(turn):
        return lax.rem(part + turn, S)

    def pair_finish(buffer, phase):
        if S > 1:
            arrive(buffer.at[0, pl.ds(0, S - 1)], phase)

    def near_send(buffer, phase, turn):
        own = buffer.at[a, member(turn)]
        for step in range(1, X):
            remote(own, own, phase + turn, near_slot(phase + turn, step), (lax.rem(a + 2 * step, A), b))
        remote(own, own, phase + turn, phase + turn, (sib, b))

    def near_forward(buffer, phase, turn):
        for step in range(1, X):
            other = buffer.at[lax.rem(a + A - 2 * step, A), member(turn)]
            arrive(other, near_slot(phase + turn, step))
            remote(other, other, phase + turn, phase + turn, (sib, b))

    def near_finish(buffer, phase, turn):
        arrive(buffer.at[pl.ds(0, X), 0], phase + turn)

    share_send(pg)

    for load in loads[3:12]:
        load.wait()
    mx[...] = jnp.zeros_like(mx)
    mx[0:CIN, :C1] = lift_ref[...]
    mx[CIN:CIN + 1, :C1] = lbias_ref[...]
    mx[CIN + 1:CIN + 2, :C1] = bo_ref[...]
    lift8 = jnp.concatenate([mx[0:8, :C1]], axis=0)
    columns = mx[...].T[:C1]
    bo_col = columns[:, CIN + 1:CIN + 2]

    def left16(matrix, bias):
        n = matrix.shape[1]
        high, low = split(matrix[0:CIN])
        b0 = bias.astype(BF16)
        rest = bias - b0.astype(F32)
        b1 = rest.astype(BF16)
        b2 = (rest - b1.astype(F32)).astype(BF16)
        mx[...] = jnp.zeros_like(mx)
        mx[0:CIN, :n] = high.astype(F32)
        mx[CIN:2 * CIN, :n] = high.astype(F32)
        mx[2 * CIN:3 * CIN, :n] = low.astype(F32)
        for row, value in enumerate((b0, b1, b2)):
            mx[3 * CIN + row:3 * CIN + row + 1, :n] = value.astype(F32)
        return mx[...].T[:n, :16].astype(BF16)

    highest = lax.Precision.HIGHEST
    eighth = lax.broadcasted_iota(jnp.int32, (1, ones.shape[1]), 1) // 8
    m = jnp.dot(lift8, byp_ref[...], precision=highest, preferred_element_type=F32)
    bp16 = left16(m, m[CIN:CIN + 1] + bi_ref[...])
    m = lax.dot_general(
        lift8, pr_ref[...], (((1,), (1,)), ((), ())), precision=highest, preferred_element_type=F32
    )
    pl16 = left16(m, m[CIN:CIN + 1] + pb_ref[...])
    t16[...] = jnp.ones_like(t16)

    def diagonal(value, count):
        rows, cols = value.shape
        bd[...] = jnp.zeros_like(bd)
        for g in range(count):
            bd[g * rows:(g + 1) * rows, g * cols:(g + 1) * cols] = value
        return bd[0:count * rows, 0:count * cols]

    bp_all = bp16.astype(F32)
    for q in range(A * S):
        bpq[q] = bp_all[q * CQ:(q + 1) * CQ]
    bq_bd = diagonal(bpq[a * S + part], min(G1, 16)).astype(BF16)
    bp_bd = diagonal(bp_all, GROUP).astype(BF16)
    pl_bd = diagonal(pl16.astype(F32), FINE).astype(BF16)
    wo_bd = wide(split(diagonal(wo_ref[...], GROUP)))
    pr_bd = split(diagonal(pr_ref[...], FINE))
    Q = J * KZ
    lifts = tall(split(lift8))
    for j in range(J):
        for k in range(KZ):
            both = []
            for n in range(2):
                both.append(mul(lifts, wide_rows(split(w1[j, n, k]))))
            lw[0, j * KZ + k] = jnp.concatenate([both[0], both[1]], axis=1)
            lw[1, j * KZ + k] = jnp.concatenate([-both[1], both[0]], axis=1)
    for row in range(Q):
        ones[row:row + 1] = jnp.where(eighth == row, 1.0, 0.0).astype(F32)
    blocks = ones[...].astype(BF16)
    arrive(r1.at[pl.ds(0, N - 1)], A2A)

    s4 = jnp.sum(r1[...], axis=0) * scale1
    first = jnp.where((lane == 0) & (me == 0), gain, 0.0).astype(F32)
    mx[...] = jnp.zeros_like(mx)
    mx[0:CIN] = s4
    mx[CIN:CIN + 1] = first
    s8 = mx[0:8]
    mixed = split(jnp.concatenate(
        [s8[:, q:q + 1] * lw[0, q] + s8[:, Q + q:Q + q + 1] * lw[1, q] for q in range(Q)], axis=0
    ))
    mx[0:Q] = mul(blocks, mixed[0]) + mul(blocks, mixed[1])
    turned = mx[...].T
    mixed = turned[:C2] + pltpu.roll(turned[C2:], Q, 1)
    for q in range(A * S):
        mt1[q] = mixed[q * CQ:(q + 1) * CQ]
    g1[me] = mt1[a * S + part]
    for pa, pb in peers:
        remote(mt1.at[pa * S + lax.rem(pb, S)], g1.at[me], EXP1, EXP1, (pa, pb))

    def fill(value):
        n = value.shape[1]
        high, low = split(value)
        t16[0:CIN, :n] = high.astype(F32)
        t16[CIN:2 * CIN, :n] = low.astype(F32)
        t16[2 * CIN:3 * CIN, :n] = high.astype(F32)
        return t16[:, :n].astype(BF16)

    def fill_pooled(ia, ip):
        for x in range(hx):
            pk_ref[ip * HX + ia * hx + x] = fill(pg[ia * S + ip, x * CIN:(x + 1) * CIN])

    share_relay(pg)
    for x in range(cells_x):
        fk_ref[x] = fill(f_ref[x * CIN:(x + 1) * CIN])
    if square:
        fill_pooled(a, part)
        fill_pooled(mate, part)
        fill_pooled(a, other)
        share_finish(pg)
        fill_pooled(sib, part)
        fill_pooled(lax.rem(sib + 2, A), part)
        fill_pooled(sib, other)
        share_last(pg)
        fill_pooled(mate, other)
    for load in loads[18:18 + S]:
        load.wait()
    arrive(g1.at[pl.ds(0, N - 1)], EXP1)
    rows = jnp.concatenate(
        [jnp.concatenate([g1[i * H + h] for h in range(H)], axis=1) for i in range(KX)], axis=0
    )
    tables = tuple(jnp.concatenate([yic[n, k] for n in range(S)], axis=1) for k in range(2))
    y = mul3(split(rows), tables)
    for n in range(S):
        for i in range(KX):
            lines[n, i] = y[i * CQ:(i + 1) * CQ, n * LB:(n + 1) * LB]
    for turn in range(1, S):
        remote(lines.at[member(turn)], yall.at[a, part], LINE_PAIR, LINE_PAIR, (a, base + member(turn)))
    for i in range(KX):
        yall[a, part, i] = lines[part, i]
    near_send(yall, LINE, 0)

    def modes(value, rows_each):
        groups = rows_each // 8
        turned = rot_i(value)
        parts = []
        for g in range(groups):
            parts.append(jnp.concatenate([
                v[i * rows_each + g * 8:i * rows_each + g * 8 + 8] for v in (value, turned) for i in range(KX)
            ], axis=0))
        return parts

    l_xi.wait()
    table = tuple(jnp.concatenate([xi[q, k] for q in range(A)], axis=0) for k in range(2))
    halves_y = []
    for n in range(S):
        halves_y += modes(y[:, n * LB:(n + 1) * LB], CQ)
    v = left3(table, split(jnp.concatenate(halves_y, axis=1)))
    steps = HX // G1
    for n in range(S):
        for s in range(steps):
            vx[n * steps + s] = jnp.concatenate([
                v[(s * G1 + xx) * 8:(s * G1 + xx) * 8 + 8, (n * CG + g) * LB:(n * CG + g + 1) * LB]
                for xx in range(G1) for g in range(CG)
            ], axis=0)

    def coarse_step(s, carry):
        v = mul(tall(split(vx[s])), tzi_ref[...])
        count = min(G1, 16)
        near = jnp.concatenate([
            mul(bq_bd, jnp.concatenate([pk_ref[s * G1 + g + xx] for xx in range(count)], axis=0))
            for g in range(0, G1, count)
        ], axis=0)
        g = split(gelu(v + near))
        zc[s] = wave(g)
        return carry

    if square:
        arrive(pg.at[lax.rem(sib + 2, A) * S + other], POOL_LAST)
        fill_pooled(lax.rem(sib + 2, A), other)
    else:
        share_finish(pg)
        for ia in range(A):
            for ip in range(S):
                fill_pooled(ia, ip)
    l_tzi.wait()
    lax.fori_loop(0, S * steps, coarse_step, 0)

    l_xf.wait()
    for load in loads[18 + S:]:
        load.wait()
    z = jnp.concatenate([
        jnp.concatenate([
            zc[n * steps + s, xx * CQ + g * 8:xx * CQ + g * 8 + 8] for s in range(steps) for xx in range(G1)
        ], axis=0) for n in range(S) for g in range(CG)
    ], axis=1)
    z = mul(wide((xf[0], xf[1])), deep(split(z)))

    def spectrum(first, n):
        return jnp.concatenate([
            z[(first + i) * 8:(first + i + 1) * 8, (n * CG + g) * LB:(n * CG + g + 1) * LB]
            for i in range(KX) for g in range(CG)
        ], axis=0)

    value = jnp.concatenate([spectrum(0, n) + rot_f(spectrum(KX, n)) for n in range(S)], axis=1)
    tables = tuple(jnp.concatenate([yfc[n, k] for n in range(S)], axis=0) for k in range(2))
    out = mul3(split(value), tables)
    for i in range(KX):
        for h in range(H):
            buf2[i * H + h] = out[i * CQ:(i + 1) * CQ, h * LB:(h + 1) * LB]
    for pa, pb in peers:
        remote(buf2.at[pa * B + pb], r3.at[me], RED, RED, (pa, pb))
    r3[me] = buf2[me]

    pair_finish(yall, LINE_PAIR)
    for turn in range(1, S):
        near_send(yall, LINE, turn)
    near_forward(yall, LINE, 0)
    l_w2.wait()
    arrive(r3.at[pl.ds(0, N - 1)], RED)
    for turn in range(1, S):
        near_forward(yall, LINE, turn)
    sums = []
    for q in range(A):
        for n in range(S):
            total = r3[q * B + n]
            for t in range(S + n, B, S):
                total = total + r3[q * B + t]
            sums.append(total)
    st = (jnp.concatenate(sums, axis=0) * scale2).T
    mixed = jnp.zeros((C1, LB), F32)
    for j in range(J):
        for k in range(KZ):
            q = j * KZ + k
            re = st[q:q + 1]
            im = st[Q + q:Q + q + 1]
            wr = w2[j, 0, k]
            wi = w2[j, 1, k]
            real = jnp.sum(re * wr - im * wi, axis=1, keepdims=True)
            imag = jnp.sum(re * wi + im * wr, axis=1, keepdims=True)
            mixed = jnp.where(lane == q, real, jnp.where(lane == Q + q, imag, mixed))
    ag2[me] = mixed

    NEARBY = B // 2

    def spread(t):
        source = a * B + flip(t)
        for step in range(1, X):
            remote(
                ag2.at[source], ag2.at[source], EXP2, SPREAD + step * B + t, (lax.rem(a + 2 * step, A), b)
            )
            if t >= NEARBY:
                remote(ag2.at[source], ag2.at[source], EXP2, EXP2, (lax.rem(sib + 2 * step, A), b))
        remote(ag2.at[source], ag2.at[source], EXP2, EXP2, (sib, b))

    for t in range(B - 1, 0, -1):
        remote(ag2.at[me], ag2.at[me], EXP2, SPREAD + t, (a, flip(t)))
    spread(0)
    for turn in range(S):
        near_finish(yall, LINE, turn)
    parts = []
    for q in range(A):
        for n in range(S):
            parts += modes(jnp.concatenate([yall[q, n, i] for i in range(KX)], axis=0), CQ)
    v = left3((xi[a, 0], xi[a, 1]), split(jnp.concatenate(parts, axis=1)))
    for s in range(hx // GROUP):
        vn[s] = jnp.concatenate([
            v[(s * GROUP + xx) * 8:(s * GROUP + xx) * 8 + 8, g * LB:(g + 1) * LB]
            for xx in range(GROUP) for g in range(C2 // 8)
        ], axis=0)

    def narrow_step(s, carry):
        v = mul(tall(split(vn[s])), tzi_ref[...])
        near = jnp.concatenate([pk_ref[part * HX + a * hx + s * GROUP + xx] for xx in range(GROUP)], axis=0)
        g = split(gelu(v + mul(bp_bd, near)))
        narrow = mul(wo_bd, deep(g))
        for xx in range(GROUP):
            nar[s * GROUP + xx] = narrow[xx * C1:(xx + 1) * C1]
        return carry

    lax.fori_loop(0, hx // GROUP, narrow_step, 0)

    for t in range(1, B):
        source = a * B + flip(t)
        arrive(ag2.at[source], SPREAD + t)
        spread(t)
    def expand(ia):
        rows = jnp.concatenate([
            jnp.concatenate([ag2[(ia * IL + g) * H + h] for h in range(H)], axis=1) for g in range(IL)
        ], axis=0)
        ye[ia] = mul3(split(rows), (yi2[0], yi2[1]))

    l_yi2.wait()
    expand(a)
    for t in range(B):
        for step in range(1, X):
            source = lax.rem(a + A - 2 * step, A) * B + flip(t)
            arrive(ag2.at[source], SPREAD + step * B + t)
            if t < NEARBY:
                remote(ag2.at[source], ag2.at[source], EXP2, EXP2, (sib, b))
    for step in range(1, X):
        expand(lax.rem(a + 2 * step, A))
    arrive(ag2.at[pl.ds(0, X * B)], EXP2)

    for ia in [sib] + [lax.rem(sib + 2 * step, A) for step in range(1, X)]:
        expand(ia)
    l_xo.wait()
    y = jnp.concatenate([ye[ia] for ia in range(A)], axis=0)
    halves_y = [modes(y[:, ch * LB:(ch + 1) * LB], C1) for ch in range(2)]
    v = left3((xo[0], xo[1]), split(jnp.concatenate(halves_y[0] + halves_y[1], axis=1)))
    CF = C1 // 8
    for s in range(cells_x // FINE):
        for ch in range(2):
            vf[s, ch] = jnp.concatenate([
                v[(s * FINE + xx) * 8:(s * FINE + xx) * 8 + 8, (ch * CF + g) * LB:(ch * CF + g + 1) * LB]
                for xx in range(FINE) for g in range(CF)
            ], axis=0)

    def fine_step(group, carry):
        near = jnp.concatenate([fk_ref[group * FINE + xx] for xx in range(FINE)], axis=0)
        for ch in range(2):
            v = mul(tall(split(vf[group, ch])), tzi_ref[...])
            rows = []
            for xx in range(0, FINE, 2):
                half = nar.at[group * (FINE // 2) + xx // 2]
                pieces = []
                for yy in range(YB):
                    at_y = (ch * YB + yy) // 2 * zn
                    pieces.append(half[:, at_y:at_y + zn])
                rows += [jnp.concatenate(pieces, axis=1) + bo_col] * 2
            g = split(gelu(v + jnp.concatenate(rows, axis=0)))
            cols = slice(ch * width, (ch + 1) * width)
            res = left3(pr_bd, g) + mul(pl_bd, near[:, cols])
            for yy in range(YB):
                os_ref[ch, yy * FINE * CIN:(yy + 1) * FINE * CIN] = res[:, yy * zn:(yy + 1) * zn]
            for xx in range(FINE):
                for c in range(CIN):
                    o_ref[c, group * FINE + xx, ch * YB:(ch + 1) * YB] = os_ref[
                        ch, pl.ds(xx * CIN + c, YB, stride=FINE * CIN), :
                    ]
        return carry

    lax.fori_loop(0, cells_x // FINE, fine_step, 0, unroll=True)
    waits = [
        (A2A, buf1.at[pl.ds(0, N - 1)]), (EXP1, g1.at[pl.ds(0, N - 1)]), (RED, buf2.at[pl.ds(0, N - 1)]),
        (EXP2, ag2.at[pl.ds(0, N - 1)]),
    ]
    if S > 1:
        waits.append((LINE_PAIR, yall.at[0, pl.ds(0, S - 1)]))
    waits.append((POOL, pg.at[pl.ds(0, A * S - 1)]))
    for turn in range(S):
        waits.append((LINE + turn, yall.at[pl.ds(0, A - 1), 0]))
    for phase, target in waits:
        whole(target, phase, phase).wait_send()


def on_device(
    A, B, fields, lift, lift_bias, spectral_in, bypass_in, bias_in, spectral_out, bypass_out,
    bias_out, proj, proj_bias,
):
    cin, xc, yc, zc = fields.shape
    C1 = lift.shape[0]
    C2 = bypass_in.shape[0]
    NX = xc * A
    NY = yc * B
    IL = KX // A
    H = B // IL
    J = KY // H
    N = A * B
    width = YB * zc
    S = parts_of(A, H, C2)
    CQ = C2 // (A * S)
    hx = xc // 2
    HX = hx * A
    G1 = GROUP * C2 // CQ
    cells = float(NX * NY * zc)
    back = math.sqrt(2.0 / (KX * KY * KZ))

    tz = z_table(zc)
    tzf = np.concatenate(list(halves(tz)), axis=1)
    tzi = stacked(np.ascontiguousarray(tz.T) * back)
    fine_x = x_angles(A, xc, NX)
    half_x = x_angles(A, xc // 2, NX // 2)
    eye = np.eye(cin)
    tx = np.stack([
        np.concatenate([np.kron(np.cos(fine_x[i].T), eye), np.kron(np.sin(fine_x[i].T), eye)], axis=1)
        for i in range(A)
    ])
    eye8 = np.eye(8)

    def lines(ang):
        return np.concatenate([np.kron(np.cos(ang), eye8), np.kron(np.sin(ang), eye8)], axis=1)

    xi = np.stack([lines(half_x[i]) for i in range(A)])
    xf = np.ascontiguousarray(xi.reshape(-1, xi.shape[2]).T)
    xo = np.stack([lines(fine_x[i]) for i in range(A)])
    yf1 = y_table(B, yc, NY, H)
    yfc = y_table(B, yc // 2, NY // 2, H)

    def per_device(table):
        return jnp.asarray(np.ascontiguousarray(np.swapaxes(halves(table), 0, 1)))

    tx_t = per_device(tx)
    yf1_t = per_device(yf1)
    yfc_t = per_device(yfc)
    yic_t = per_device(np.swapaxes(yfc, 1, 2))
    yi2_t = per_device(np.swapaxes(yf1, 1, 2))
    xi_t = per_device(xi)
    xo_t = per_device(xo)
    xf_t = jnp.asarray(halves(xf))

    weights2 = jnp.swapaxes(spectral_out, 3, 4)

    operands = [
        fields, lift.T, lift_bias[None], bypass_in.T, bias_in[None], bypass_out, bias_out[None], proj,
        proj_bias[None], jnp.asarray(tzf),
        jnp.asarray(tzi), spectral_in, weights2, tx_t, yf1_t, yfc_t, yic_t, yi2_t, xf_t, xi_t, xo_t,
    ]
    anywhere = pl.BlockSpec(memory_space=pl.ANY)
    V = pltpu.VMEM
    return pl.pallas_call(
        functools.partial(
            kernel, A, B, xc, yc, 1.0 / math.sqrt(cells), 1.0 / math.sqrt(cells / 4.0), math.sqrt(cells)
        ),
        out_shape=pltpu.VMEM((cin, xc, yc, zc), F32),
        in_specs=[anywhere] * len(operands),
        out_specs=pl.BlockSpec(memory_space=pltpu.VMEM),
        scratch_shapes=[
            V((xc, cin, yc, zc), F32), V((xc * cin, yc * zc), F32),
        ] + [V(v.shape, v.dtype) for v in operands[1:10]] + [
            V((2, YB * FINE * cin, zc), F32),
            V(tzi.shape, BF16), V(spectral_in.shape, F32), V(weights2.shape, F32),
            V(tx_t.shape[1:], BF16), V(yf1_t.shape[1:], BF16), V((S,) + yfc_t.shape[1:], BF16),
            V((S,) + yic_t.shape[1:], BF16), V(yi2_t.shape[1:], BF16), V(xf_t.shape, BF16), V(xi_t.shape, BF16),
            V(xo_t.shape[1:], BF16),
            V((N, cin, LB), F32), V((N, cin, LB), F32), V((LB, LB), F32),
            V((A * S, CQ, LB), F32), V((N, CQ, LB), F32), V((S, KX, CQ, LB), F32), V((A, S, KX, CQ, LB), F32),
            V((A * S, hx * cin, width), F32), V((S * HX, 16, width), BF16),
            V((2, J * KZ, 8, 2 * C2), F32), V((J * KZ, J * KZ * 8), F32), V((A, IL * C1, 2 * LB), F32),
            V((S * HX // G1, G1 * CQ, LB), F32), V((S * HX // G1, G1 * CQ, LB), F32), V((hx // GROUP, GROUP * C2, LB), F32),
            V((N, CQ, LB), F32), V((N, CQ, LB), F32), V((N, C1, LB), F32),
            V((xc // FINE, 2, FINE * C1, LB), F32),
            V((hx, C1, width), F32), V((xc, 16, yc * zc), BF16), V((16, yc * zc), F32),
            V((GROUP * C2, GROUP * C2), F32), V((A * S, CQ, 16), F32),
            pltpu.SemaphoreType.DMA((cin,)),
            pltpu.SemaphoreType.DMA((18 + 2 * S,)),
            pltpu.SemaphoreType.DMA((10 + S,)), pltpu.SemaphoreType.DMA((10 + S + A * B // 2 + A * S // 2,)),
        ],
        compiler_params=pltpu.CompilerParams(
            collective_id=0, has_side_effects=True, vmem_limit_bytes=60 * 1024 * 1024
        ),
    )(*operands)


def solution(mesh):
    A = mesh.shape["gx"]
    B = mesh.shape["gy"]
    in_specs = (
        P(None, "gx", "gy", None), P(), P(), P(("gx", "gy"), None, None, None, None), P(), P(),
        P(("gx", "gy"), None, None, None, None), P(), P(), P(), P(),
    )
    return jax.shard_map(
        functools.partial(on_device, A, B), mesh=mesh, in_specs=in_specs,
        out_specs=P(None, "gx", "gy", None), check_vma=False,
    )
```

```python
import functools
import math

import jax
import jax.numpy as jnp
import numpy as np
from jax import lax
from jax.experimental import pallas as pl
from jax.experimental.pallas import tpu as pltpu
from jax.sharding import PartitionSpec as P

KX = 16
KY = 16
KZ = 8
YB = 8
LB = 128
GROUP = 4
FINE = 16
F32 = jnp.float32
BF16 = jnp.bfloat16
MESH = pl.DeviceIdType.MESH
ROOT = math.sqrt(0.5)


def freq(count):
    f = np.arange(count)
    return np.where(f < count // 2, f, f - count)


def halves(table):
    high = table.astype(np.float32).astype(jnp.bfloat16)
    low = (table - high.astype(np.float64)).astype(np.float32).astype(jnp.bfloat16)
    return np.stack([high, low])


def stacked(table):
    high, low = halves(table)
    return np.concatenate([high, high, low], axis=0)


def angles(places, frequency, length):
    turns = np.mod(places[:, None] * frequency[None, :], length)
    return turns * (2.0 * math.pi / length)


def z_table(z_length):
    ang = angles(np.arange(z_length), np.arange(KZ), z_length)
    table = np.zeros((YB, z_length, 2, YB, KZ))
    for y in range(YB):
        table[y, :, 0, y] = np.cos(ang)
        table[y, :, 1, y] = -np.sin(ang)
    return table.reshape(YB * z_length, LB)


def y_table(blocks, cells, length, groups):
    per = KY // groups
    frequency = freq(KY)
    out = np.zeros((blocks, cells // YB, 2, YB, KZ, groups, LB))
    for b in range(blocks):
        ang = angles(b * cells + np.arange(cells), frequency, length)
        for y in range(cells):
            for j in range(KY):
                c, s = np.cos(ang[y, j]), np.sin(ang[y, j])
                for k in range(KZ):
                    re = (j % per) * KZ + k
                    im = per * KZ + re
                    at = (b, y // YB)
                    out[at + (0, y % YB, k, j // per, re)] = c
                    out[at + (1, y % YB, k, j // per, re)] = s
                    out[at + (0, y % YB, k, j // per, im)] = -s
                    out[at + (1, y % YB, k, j // per, im)] = c
    return out.reshape(blocks, cells // YB * LB, groups * LB)


def x_angles(blocks, cells, length):
    return angles(np.arange(blocks * cells), freq(KX), length).reshape(blocks, cells, KX)


def split(value):
    high = value.astype(BF16)
    return high, (value - high.astype(F32)).astype(BF16)


def mul(a, b):
    return jnp.dot(a, b, preferred_element_type=F32)


def tall(a):
    return jnp.concatenate([a[0], a[1], a[0]], axis=1)


def deep(a):
    return jnp.concatenate([a[0], a[1], a[0]], axis=0)


def wide(a):
    return jnp.concatenate([a[0], a[0], a[1]], axis=1)


def mul3(a, b):
    return mul(a[0], b[0]) + (mul(a[1], b[0]) + mul(a[0], b[1]))


def wide_rows(a):
    return jnp.concatenate([a[0], a[0], a[1]], axis=0)


def left3(table, b):
    rows = table[0].shape[0]
    both = mul(jnp.concatenate([table[0], table[1]], axis=0), b[0])
    return both[:rows] + (both[rows:] + mul(table[0], b[1]))


def bend(v):
    return v * (1.0 + lax.erf(v))


def parts_of(A, H, channels):
    parts = 1
    while H % (2 * parts) == 0 and channels % (16 * parts * A) == 0:
        parts *= 2
    return parts


def kernel(
    A, B, cells_x, cells_y, scale1, scale2, gain,
    f_hbm, lift_hbm, lbias_hbm, byp_hbm, bi_hbm, wo_hbm, bo_hbm, pr_hbm, pb_hbm, tzf_hbm, tzi_hbm, w1_hbm, w2_hbm, tx_hbm, yf1_hbm, yfc_hbm, yic_hbm, yi2_hbm, xf_hbm, xi_hbm, xo_hbm,
    o_ref,
    fx, f_ref, lift_ref, lbias_ref, byp_ref, bi_ref, wo_ref, bo_ref, pr_ref, pb_ref, tzf_ref, os_ref,
    tzi_ref, w1, w2, tx, yf1, yfc, yic, yi2, xf, xi, xo,
    buf1, r1, mx, mt1, g1, lines, yall, pg, pk_ref, lw, ones, ye, vx, zc, vn, buf2, r3, ag2, vf, nar, fk_ref, t16, bd, bpq,
    fsem, csem, ssem, rsem,
):
    a = lax.axis_index("gx")
    b = lax.axis_index("gy")
    me = a * B + b
    IL = KX // A
    H = B // IL
    J = KY // H
    N = A * B
    X = A // 2
    CIN, C1 = lift_ref.shape
    C2 = wo_ref.shape[1]
    S = parts_of(A, H, C2)
    CQ = C2 // (A * S)
    CG = CQ // 8
    hx = cells_x // 2
    HX = hx * A
    G1 = GROUP * C2 // CQ
    part = lax.rem(b, S)
    base = b - part
    core = lax.rem(a, 2)
    sib = a + 1 - 2 * core

    def flip(t):
        value = b
        bit = 1
        while bit < B:
            if t & bit:
                value = value + bit - 2 * bit * lax.rem(b // bit, 2)
            bit *= 2
        return value

    lines_b = [flip(t) for t in range(B)]
    lines_a = [lax.rem(a + ia, A) for ia in range(A)]
    peers = [(lines_a[ia], lines_b[t]) for t in reversed(range(B)) for ia in reversed(range(A)) if t or ia]

    fields = [pltpu.make_async_copy(f_hbm.at[c], fx.at[:, c], fsem.at[c]) for c in range(CIN)]
    pairs = [
        (tzf_hbm, tzf_ref), (tx_hbm.at[a], tx), (yf1_hbm.at[b], yf1), (lift_hbm, lift_ref), (lbias_hbm, lbias_ref),
        (byp_hbm, byp_ref), (bi_hbm, bi_ref), (wo_hbm, wo_ref), (bo_hbm, bo_ref), (pr_hbm, pr_ref), (pb_hbm, pb_ref),
        (w1_hbm, w1), (xi_hbm, xi), (tzi_hbm, tzi_ref), (xf_hbm, xf), (w2_hbm, w2), (yi2_hbm.at[b], yi2), (xo_hbm.at[a], xo),
    ] + [(yic_hbm.at[base + n], yic.at[n]) for n in range(S)] + [(yfc_hbm.at[base + n], yfc.at[n]) for n in range(S)]
    loads = [pltpu.make_async_copy(src, dst, csem.at[k]) for k, (src, dst) in enumerate(pairs)]
    l_tzf, l_tx, l_yf1 = loads[:3]
    l_w1, l_xi, l_tzi, l_xf, l_w2, l_yi2, l_xo = loads[11:18]
    for load in fields + loads[:3]:
        load.start()

    barrier = pltpu.get_barrier_semaphore()
    for pa, pb in peers:
        pl.semaphore_signal(barrier, inc=1, device_id=(pa, pb), device_id_type=MESH)
    for load in loads[3:]:
        load.start()

    lane = lax.broadcasted_iota(jnp.int32, (1, LB), 1)
    sign_f = jnp.where(lane < LB // 2, 1.0, -1.0).astype(F32)

    def rot_f(v):
        return pltpu.roll(v, LB // 2, 1) * sign_f

    def rot_i(v):
        return pltpu.roll(v, LB // 2, 1) * -sign_f

    def remote(source, target, phase, slot, device):
        pltpu.make_async_remote_copy(
            src_ref=source, dst_ref=target, send_sem=ssem.at[phase], recv_sem=rsem.at[slot],
            device_id=device, device_id_type=MESH,
        ).start()

    def whole(target, phase, slot):
        return pltpu.make_async_remote_copy(
            src_ref=target, dst_ref=target, send_sem=ssem.at[phase], recv_sem=rsem.at[slot],
            device_id=(sib, b), device_id_type=MESH,
        )

    def arrive(target, slot):
        whole(target, 0, slot).wait_recv()

    A2A, EXP1, RED, EXP2, LINE_PAIR, POOL, POOL_X, POOL_Y, POOL_XY, POOL_LAST, LINE = range(11)
    SPREAD = LINE + S
    NEAR = SPREAD + X * B

    width = tzi_ref.shape[1]
    for load in fields:
        load.wait()
    flat = fx.reshape(f_ref.shape[0] * cells_y, f_ref.shape[1] // cells_y)
    zn = flat.shape[1]
    for y in range(cells_y):
        f_ref[:, y * zn:(y + 1) * zn] = flat[pl.ds(y, f_ref.shape[0], stride=cells_y), :]
    l_tzf.wait()
    def wave(pair):
        both = mul(pair[0], tzf_ref[...])
        return both[:, :LB] + (both[:, LB:] + mul(pair[1], tzf_ref[:, :LB]))

    zs = wave(split(jnp.concatenate([f_ref[:, :width], f_ref[:, width:]], axis=0)))
    zs = [zs[:zs.shape[0] // 2], zs[zs.shape[0] // 2:]]
    l_tx.wait()
    us = []
    for z in zs:
        us.append(mul3((tx[0], tx[1]), split(jnp.concatenate([z, rot_f(z)], axis=0))))
    l_yf1.wait()
    parts = mul3(split(jnp.concatenate(us, axis=1)), (yf1[0], yf1[1]))
    for i in range(KX):
        for h in range(H):
            buf1[i * H + h] = parts[i * CIN:(i + 1) * CIN, h * LB:(h + 1) * LB]
    r1[me] = buf1[me]
    pl.semaphore_wait(barrier, N - 1)

    for pa, pb in peers:
        remote(buf1.at[pa * B + pb], r1.at[me], A2A, A2A, (pa, pb))

    for x in range(hx):
        both = f_ref[2 * x * CIN:(2 * x + 1) * CIN] + f_ref[(2 * x + 1) * CIN:(2 * x + 2) * CIN]
        pieces = [
            both[:, 2 * y * zn:(2 * y + 1) * zn] + both[:, (2 * y + 1) * zn:(2 * y + 2) * zn]
            for y in range(YB)
        ]
        pg[a * S + part, x * CIN:(x + 1) * CIN] = jnp.concatenate(pieces, axis=1) * 0.25

    def near_slot(phase, step):
        return NEAR + (phase - LINE) * X + step

    square = X == 2 and S == 2
    mate = lax.rem(a + 2, A)
    other = S - 1 - part

    def share_send(buffer):
        own = buffer.at[a * S + part]
        if square:
            remote(own, own, POOL, POOL_X, (mate, b))
            remote(own, own, POOL, POOL_Y, (a, base + other))
            remote(own, own, POOL, POOL, (sib, b))
        else:
            for ia in range(A):
                for turn in range(S):
                    if ia or turn:
                        remote(own, own, POOL, POOL, (lax.rem(a + ia, A), base + member(turn)))

    def share_relay(buffer):
        if square:
            left = buffer.at[mate * S + part]
            right = buffer.at[a * S + other]
            arrive(left, POOL_X)
            arrive(right, POOL_Y)
            ia = a * core + mate * (1 - core)
            ip = other * core + part * (1 - core)
            target = (mate * core + a * (1 - core), b * core + (base + other) * (1 - core))
            relayed = buffer.at[ia * S + ip]
            remote(relayed, relayed, POOL, POOL_XY, target)
            remote(left, left, POOL, POOL, (sib, b))
            remote(right, right, POOL, POOL, (sib, b))

    def share_last(buffer):
        if square:
            corner = buffer.at[mate * S + other]
            arrive(corner, POOL_XY)
            remote(corner, corner, POOL, POOL_LAST, (sib, b))

    def share_finish(buffer):
        arrive(buffer.at[pl.ds(0, A * S // 2 - 1 if square else A * S - 1)], POOL)

    def member(turn):
        return lax.rem(part + turn, S)

    def pair_finish(buffer, phase):
        if S > 1:
            arrive(buffer.at[0, pl.ds(0, S - 1)], phase)

    def near_send(buffer, phase, turn):
        own = buffer.at[a, member(turn)]
        for step in range(1, X):
            remote(own, own, phase + turn, near_slot(phase + turn, step), (lax.rem(a + 2 * step, A), b))
        remote(own, own, phase + turn, phase + turn, (sib, b))

    def near_forward(buffer, phase, turn):
        for step in range(1, X):
            other = buffer.at[lax.rem(a + A - 2 * step, A), member(turn)]
            arrive(other, near_slot(phase + turn, step))
            remote(other, other, phase + turn, phase + turn, (sib, b))

    def near_finish(buffer, phase, turn):
        arrive(buffer.at[pl.ds(0, X), 0], phase + turn)

    share_send(pg)

    for load in loads[3:12]:
        load.wait()
    mx[...] = jnp.zeros_like(mx)
    mx[0:CIN, :C1] = lift_ref[...]
    mx[CIN:CIN + 1, :C1] = lbias_ref[...]
    mx[CIN + 1:CIN + 2, :C1] = bo_ref[...]
    lift8 = jnp.concatenate([mx[0:8, :C1]], axis=0)
    columns = mx[...].T[:C1]
    bo_col = columns[:, CIN + 1:CIN + 2] * ROOT

    def left16(matrix, bias):
        n = matrix.shape[1]
        high, low = split(matrix[0:CIN])
        b0 = bias.astype(BF16)
        rest = bias - b0.astype(F32)
        b1 = rest.astype(BF16)
        b2 = (rest - b1.astype(F32)).astype(BF16)
        mx[...] = jnp.zeros_like(mx)
        mx[0:CIN, :n] = high.astype(F32)
        mx[CIN:2 * CIN, :n] = high.astype(F32)
        mx[2 * CIN:3 * CIN, :n] = low.astype(F32)
        for row, value in enumerate((b0, b1, b2)):
            mx[3 * CIN + row:3 * CIN + row + 1, :n] = value.astype(F32)
        return mx[...].T[:n, :16].astype(BF16)

    highest = lax.Precision.HIGHEST
    eighth = lax.broadcasted_iota(jnp.int32, (1, ones.shape[1]), 1) // 8
    m = jnp.dot(lift8, byp_ref[...], precision=highest, preferred_element_type=F32)
    bp16 = left16(m * ROOT, (m[CIN:CIN + 1] + bi_ref[...]) * ROOT)
    m = lax.dot_general(
        lift8, pr_ref[...], (((1,), (1,)), ((), ())), precision=highest, preferred_element_type=F32
    )
    pl16 = left16(m, m[CIN:CIN + 1] + pb_ref[...])
    t16[...] = jnp.ones_like(t16)

    def diagonal(value, count):
        rows, cols = value.shape
        bd[...] = jnp.zeros_like(bd)
        for g in range(count):
            bd[g * rows:(g + 1) * rows, g * cols:(g + 1) * cols] = value
        return bd[0:count * rows, 0:count * cols]

    bp_all = bp16.astype(F32)
    for q in range(A * S):
        bpq[q] = bp_all[q * CQ:(q + 1) * CQ]
    bq_bd = diagonal(bpq[a * S + part], min(G1, 16)).astype(BF16)
    bp_bd = diagonal(bp_all, GROUP).astype(BF16)
    pl_bd = diagonal(pl16.astype(F32), FINE).astype(BF16)
    wo_bd = wide(split(diagonal(wo_ref[...] * 0.5, GROUP)))
    pr_bd = split(diagonal(pr_ref[...] * ROOT, FINE))
    Q = J * KZ
    lifts = tall(split(lift8))
    for j in range(J):
        for k in range(KZ):
            both = []
            for n in range(2):
                both.append(mul(lifts, wide_rows(split(w1[j, n, k]))))
            lw[0, j * KZ + k] = jnp.concatenate([both[0], both[1]], axis=1)
            lw[1, j * KZ + k] = jnp.concatenate([-both[1], both[0]], axis=1)
    for row in range(Q):
        ones[row:row + 1] = jnp.where(eighth == row, 1.0, 0.0).astype(F32)
    blocks = ones[...].astype(BF16)
    arrive(r1.at[pl.ds(0, N - 1)], A2A)

    s4 = jnp.sum(r1[...], axis=0) * scale1
    first = jnp.where((lane == 0) & (me == 0), gain, 0.0).astype(F32)
    mx[...] = jnp.zeros_like(mx)
    mx[0:CIN] = s4
    mx[CIN:CIN + 1] = first
    s8 = mx[0:8]
    mixed = split(jnp.concatenate(
        [s8[:, q:q + 1] * lw[0, q] + s8[:, Q + q:Q + q + 1] * lw[1, q] for q in range(Q)], axis=0
    ))
    mx[0:Q] = mul(blocks, mixed[0]) + mul(blocks, mixed[1])
    turned = mx[...].T
    mixed = turned[:C2] + pltpu.roll(turned[C2:], Q, 1)
    for q in range(A * S):
        mt1[q] = mixed[q * CQ:(q + 1) * CQ]
    g1[me] = mt1[a * S + part]
    for pa, pb in peers:
        remote(mt1.at[pa * S + lax.rem(pb, S)], g1.at[me], EXP1, EXP1, (pa, pb))

    def fill(value):
        n = value.shape[1]
        high, low = split(value)
        t16[0:CIN, :n] = high.astype(F32)
        t16[CIN:2 * CIN, :n] = low.astype(F32)
        t16[2 * CIN:3 * CIN, :n] = high.astype(F32)
        return t16[:, :n].astype(BF16)

    def fill_pooled(ia, ip):
        for x in range(hx):
            pk_ref[ip * HX + ia * hx + x] = fill(pg[ia * S + ip, x * CIN:(x + 1) * CIN])

    share_relay(pg)
    for x in range(cells_x):
        fk_ref[x] = fill(f_ref[x * CIN:(x + 1) * CIN])
    if square:
        fill_pooled(a, part)
        fill_pooled(mate, part)
        fill_pooled(a, other)
        share_finish(pg)
        fill_pooled(sib, part)
        fill_pooled(lax.rem(sib + 2, A), part)
        fill_pooled(sib, other)
        share_last(pg)
        fill_pooled(mate, other)
    for load in loads[18:18 + S]:
        load.wait()
    arrive(g1.at[pl.ds(0, N - 1)], EXP1)
    rows = jnp.concatenate(
        [jnp.concatenate([g1[i * H + h] for h in range(H)], axis=1) for i in range(KX)], axis=0
    )
    tables = tuple(jnp.concatenate([yic[n, k] for n in range(S)], axis=1) for k in range(2))
    y = mul3(split(rows), tables)
    for n in range(S):
        for i in range(KX):
            lines[n, i] = y[i * CQ:(i + 1) * CQ, n * LB:(n + 1) * LB]
    for turn in range(1, S):
        remote(lines.at[member(turn)], yall.at[a, part], LINE_PAIR, LINE_PAIR, (a, base + member(turn)))
    for i in range(KX):
        yall[a, part, i] = lines[part, i]
    near_send(yall, LINE, 0)

    def modes(value, rows_each):
        groups = rows_each // 8
        turned = rot_i(value)
        parts = []
        for g in range(groups):
            parts.append(jnp.concatenate([
                v[i * rows_each + g * 8:i * rows_each + g * 8 + 8] for v in (value, turned) for i in range(KX)
            ], axis=0))
        return parts

    l_xi.wait()
    table = tuple(jnp.concatenate([xi[q, k] for q in range(A)], axis=0) for k in range(2))
    halves_y = []
    for n in range(S):
        halves_y += modes(y[:, n * LB:(n + 1) * LB], CQ)
    v = left3(table, split(jnp.concatenate(halves_y, axis=1)))
    steps = HX // G1
    for n in range(S):
        for s in range(steps):
            vx[n * steps + s] = jnp.concatenate([
                v[(s * G1 + xx) * 8:(s * G1 + xx) * 8 + 8, (n * CG + g) * LB:(n * CG + g + 1) * LB]
                for xx in range(G1) for g in range(CG)
            ], axis=0)

    def coarse_step(s, carry):
        v = mul(tall(split(vx[s])), tzi_ref[...])
        count = min(G1, 16)
        near = jnp.concatenate([
            mul(bq_bd, jnp.concatenate([pk_ref[s * G1 + g + xx] for xx in range(count)], axis=0))
            for g in range(0, G1, count)
        ], axis=0)
        g = split(bend(v + near))
        zc[s] = wave(g)
        return carry

    if square:
        arrive(pg.at[lax.rem(sib + 2, A) * S + other], POOL_LAST)
        fill_pooled(lax.rem(sib + 2, A), other)
    else:
        share_finish(pg)
        for ia in range(A):
            for ip in range(S):
                fill_pooled(ia, ip)
    l_tzi.wait()
    lax.fori_loop(0, S * steps, coarse_step, 0)

    l_xf.wait()
    for load in loads[18 + S:]:
        load.wait()
    z = jnp.concatenate([
        jnp.concatenate([
            zc[n * steps + s, xx * CQ + g * 8:xx * CQ + g * 8 + 8] for s in range(steps) for xx in range(G1)
        ], axis=0) for n in range(S) for g in range(CG)
    ], axis=1)
    z = mul(wide((xf[0], xf[1])), deep(split(z)))

    def spectrum(first, n):
        return jnp.concatenate([
            z[(first + i) * 8:(first + i + 1) * 8, (n * CG + g) * LB:(n * CG + g + 1) * LB]
            for i in range(KX) for g in range(CG)
        ], axis=0)

    value = jnp.concatenate([spectrum(0, n) + rot_f(spectrum(KX, n)) for n in range(S)], axis=1)
    tables = tuple(jnp.concatenate([yfc[n, k] for n in range(S)], axis=0) for k in range(2))
    out = mul3(split(value), tables)
    for i in range(KX):
        for h in range(H):
            buf2[i * H + h] = out[i * CQ:(i + 1) * CQ, h * LB:(h + 1) * LB]
    for pa, pb in peers:
        remote(buf2.at[pa * B + pb], r3.at[me], RED, RED, (pa, pb))
    r3[me] = buf2[me]

    pair_finish(yall, LINE_PAIR)
    for turn in range(1, S):
        near_send(yall, LINE, turn)
    near_forward(yall, LINE, 0)
    l_w2.wait()
    arrive(r3.at[pl.ds(0, N - 1)], RED)
    for turn in range(1, S):
        near_forward(yall, LINE, turn)
    sums = []
    for q in range(A):
        for n in range(S):
            total = r3[q * B + n]
            for t in range(S + n, B, S):
                total = total + r3[q * B + t]
            sums.append(total)
    st = (jnp.concatenate(sums, axis=0) * scale2).T
    mixed = jnp.zeros((C1, LB), F32)
    for j in range(J):
        for k in range(KZ):
            q = j * KZ + k
            re = st[q:q + 1]
            im = st[Q + q:Q + q + 1]
            wr = w2[j, 0, k]
            wi = w2[j, 1, k]
            real = jnp.sum(re * wr - im * wi, axis=1, keepdims=True)
            imag = jnp.sum(re * wi + im * wr, axis=1, keepdims=True)
            mixed = jnp.where(lane == q, real, jnp.where(lane == Q + q, imag, mixed))
    ag2[me] = mixed

    NEARBY = B // 2

    def spread(t):
        source = a * B + flip(t)
        for step in range(1, X):
            remote(
                ag2.at[source], ag2.at[source], EXP2, SPREAD + step * B + t, (lax.rem(a + 2 * step, A), b)
            )
            if t >= NEARBY:
                remote(ag2.at[source], ag2.at[source], EXP2, EXP2, (lax.rem(sib + 2 * step, A), b))
        remote(ag2.at[source], ag2.at[source], EXP2, EXP2, (sib, b))

    for t in range(B - 1, 0, -1):
        remote(ag2.at[me], ag2.at[me], EXP2, SPREAD + t, (a, flip(t)))
    spread(0)
    for turn in range(S):
        near_finish(yall, LINE, turn)
    parts = []
    for q in range(A):
        for n in range(S):
            parts += modes(jnp.concatenate([yall[q, n, i] for i in range(KX)], axis=0), CQ)
    v = left3((xi[a, 0], xi[a, 1]), split(jnp.concatenate(parts, axis=1)))
    for s in range(hx // GROUP):
        vn[s] = jnp.concatenate([
            v[(s * GROUP + xx) * 8:(s * GROUP + xx) * 8 + 8, g * LB:(g + 1) * LB]
            for xx in range(GROUP) for g in range(C2 // 8)
        ], axis=0)

    def narrow_step(s, carry):
        v = mul(tall(split(vn[s])), tzi_ref[...])
        near = jnp.concatenate([pk_ref[part * HX + a * hx + s * GROUP + xx] for xx in range(GROUP)], axis=0)
        g = split(bend(v + mul(bp_bd, near)))
        narrow = mul(wo_bd, deep(g))
        for xx in range(GROUP):
            nar[s * GROUP + xx] = narrow[xx * C1:(xx + 1) * C1] + bo_col
        return carry

    lax.fori_loop(0, hx // GROUP, narrow_step, 0)

    for t in range(1, B):
        source = a * B + flip(t)
        arrive(ag2.at[source], SPREAD + t)
        spread(t)
    def expand(ia):
        rows = jnp.concatenate([
            jnp.concatenate([ag2[(ia * IL + g) * H + h] for h in range(H)], axis=1) for g in range(IL)
        ], axis=0)
        ye[ia] = mul3(split(rows), (yi2[0], yi2[1]))

    l_yi2.wait()
    expand(a)
    for t in range(B):
        for step in range(1, X):
            source = lax.rem(a + A - 2 * step, A) * B + flip(t)
            arrive(ag2.at[source], SPREAD + step * B + t)
            if t < NEARBY:
                remote(ag2.at[source], ag2.at[source], EXP2, EXP2, (sib, b))
    for step in range(1, X):
        expand(lax.rem(a + 2 * step, A))
    arrive(ag2.at[pl.ds(0, X * B)], EXP2)

    for ia in [sib] + [lax.rem(sib + 2 * step, A) for step in range(1, X)]:
        expand(ia)
    l_xo.wait()
    y = jnp.concatenate([ye[ia] for ia in range(A)], axis=0)
    halves_y = [modes(y[:, ch * LB:(ch + 1) * LB], C1) for ch in range(2)]
    v = left3((xo[0], xo[1]), split(jnp.concatenate(halves_y[0] + halves_y[1], axis=1)))
    CF = C1 // 8
    for s in range(cells_x // FINE):
        for ch in range(2):
            vf[s, ch] = jnp.concatenate([
                v[(s * FINE + xx) * 8:(s * FINE + xx) * 8 + 8, (ch * CF + g) * LB:(ch * CF + g + 1) * LB]
                for xx in range(FINE) for g in range(CF)
            ], axis=0)

    def fine_step(group, carry):
        near = jnp.concatenate([fk_ref[group * FINE + xx] for xx in range(FINE)], axis=0)
        for ch in range(2):
            v = mul(tall(split(vf[group, ch])), tzi_ref[...])
            rows = []
            for xx in range(0, FINE, 2):
                half = nar.at[group * (FINE // 2) + xx // 2]
                pieces = []
                for yy in range(YB):
                    at_y = (ch * YB + yy) // 2 * zn
                    pieces.append(half[:, at_y:at_y + zn])
                rows += [jnp.concatenate(pieces, axis=1)] * 2
            g = split(bend(v + jnp.concatenate(rows, axis=0)))
            cols = slice(ch * width, (ch + 1) * width)
            res = left3(pr_bd, g) + mul(pl_bd, near[:, cols])
            for yy in range(YB):
                os_ref[ch, yy * FINE * CIN:(yy + 1) * FINE * CIN] = res[:, yy * zn:(yy + 1) * zn]
            for xx in range(FINE):
                for c in range(CIN):
                    o_ref[c, group * FINE + xx, ch * YB:(ch + 1) * YB] = os_ref[
                        ch, pl.ds(xx * CIN + c, YB, stride=FINE * CIN), :
                    ]
        return carry

    lax.fori_loop(0, cells_x // FINE, fine_step, 0, unroll=True)
    waits = [
        (A2A, buf1.at[pl.ds(0, N - 1)]), (EXP1, g1.at[pl.ds(0, N - 1)]), (RED, buf2.at[pl.ds(0, N - 1)]),
        (EXP2, ag2.at[pl.ds(0, N - 1)]),
    ]
    if S > 1:
        waits.append((LINE_PAIR, yall.at[0, pl.ds(0, S - 1)]))
    waits.append((POOL, pg.at[pl.ds(0, A * S - 1)]))
    for turn in range(S):
        waits.append((LINE + turn, yall.at[pl.ds(0, A - 1), 0]))
    for phase, target in waits:
        whole(target, phase, phase).wait_send()


def on_device(
    A, B, fields, lift, lift_bias, spectral_in, bypass_in, bias_in, spectral_out, bypass_out,
    bias_out, proj, proj_bias,
):
    cin, xc, yc, zc = fields.shape
    C1 = lift.shape[0]
    C2 = bypass_in.shape[0]
    NX = xc * A
    NY = yc * B
    IL = KX // A
    H = B // IL
    J = KY // H
    N = A * B
    width = YB * zc
    S = parts_of(A, H, C2)
    CQ = C2 // (A * S)
    hx = xc // 2
    HX = hx * A
    G1 = GROUP * C2 // CQ
    cells = float(NX * NY * zc)
    back = math.sqrt(2.0 / (KX * KY * KZ))

    tz = z_table(zc)
    tzf = np.concatenate(list(halves(tz)), axis=1)
    tzi = stacked(np.ascontiguousarray(tz.T) * (back * ROOT))
    fine_x = x_angles(A, xc, NX)
    half_x = x_angles(A, xc // 2, NX // 2)
    eye = np.eye(cin)
    tx = np.stack([
        np.concatenate([np.kron(np.cos(fine_x[i].T), eye), np.kron(np.sin(fine_x[i].T), eye)], axis=1)
        for i in range(A)
    ])
    eye8 = np.eye(8)

    def lines(ang):
        return np.concatenate([np.kron(np.cos(ang), eye8), np.kron(np.sin(ang), eye8)], axis=1)

    xi = np.stack([lines(half_x[i]) for i in range(A)])
    xf = np.ascontiguousarray(xi.reshape(-1, xi.shape[2]).T)
    xo = np.stack([lines(fine_x[i]) for i in range(A)])
    yf1 = y_table(B, yc, NY, H)
    yfc = y_table(B, yc // 2, NY // 2, H)

    def per_device(table):
        return jnp.asarray(np.ascontiguousarray(np.swapaxes(halves(table), 0, 1)))

    tx_t = per_device(tx)
    yf1_t = per_device(yf1)
    yfc_t = per_device(yfc)
    yic_t = per_device(np.swapaxes(yfc, 1, 2))
    yi2_t = per_device(np.swapaxes(yf1, 1, 2))
    xi_t = per_device(xi)
    xo_t = per_device(xo)
    xf_t = jnp.asarray(halves(xf))

    weights2 = jnp.swapaxes(spectral_out, 3, 4)

    operands = [
        fields, lift.T, lift_bias[None], bypass_in.T, bias_in[None], bypass_out, bias_out[None], proj,
        proj_bias[None], jnp.asarray(tzf),
        jnp.asarray(tzi), spectral_in, weights2, tx_t, yf1_t, yfc_t, yic_t, yi2_t, xf_t, xi_t, xo_t,
    ]
    anywhere = pl.BlockSpec(memory_space=pl.ANY)
    V = pltpu.VMEM
    return pl.pallas_call(
        functools.partial(
            kernel, A, B, xc, yc, 1.0 / math.sqrt(cells), ROOT / math.sqrt(cells / 4.0), math.sqrt(cells)
        ),
        out_shape=pltpu.VMEM((cin, xc, yc, zc), F32),
        in_specs=[anywhere] * len(operands),
        out_specs=pl.BlockSpec(memory_space=pltpu.VMEM),
        scratch_shapes=[
            V((xc, cin, yc, zc), F32), V((xc * cin, yc * zc), F32),
        ] + [V(v.shape, v.dtype) for v in operands[1:10]] + [
            V((2, YB * FINE * cin, zc), F32),
            V(tzi.shape, BF16), V(spectral_in.shape, F32), V(weights2.shape, F32),
            V(tx_t.shape[1:], BF16), V(yf1_t.shape[1:], BF16), V((S,) + yfc_t.shape[1:], BF16),
            V((S,) + yic_t.shape[1:], BF16), V(yi2_t.shape[1:], BF16), V(xf_t.shape, BF16), V(xi_t.shape, BF16),
            V(xo_t.shape[1:], BF16),
            V((N, cin, LB), F32), V((N, cin, LB), F32), V((LB, LB), F32),
            V((A * S, CQ, LB), F32), V((N, CQ, LB), F32), V((S, KX, CQ, LB), F32), V((A, S, KX, CQ, LB), F32),
            V((A * S, hx * cin, width), F32), V((S * HX, 16, width), BF16),
            V((2, J * KZ, 8, 2 * C2), F32), V((J * KZ, J * KZ * 8), F32), V((A, IL * C1, 2 * LB), F32),
            V((S * HX // G1, G1 * CQ, LB), F32), V((S * HX // G1, G1 * CQ, LB), F32), V((hx // GROUP, GROUP * C2, LB), F32),
            V((N, CQ, LB), F32), V((N, CQ, LB), F32), V((N, C1, LB), F32),
            V((xc // FINE, 2, FINE * C1, LB), F32),
            V((hx, C1, width), F32), V((xc, 16, yc * zc), BF16), V((16, yc * zc), F32),
            V((GROUP * C2, max(GROUP * C2, FINE * C1)), F32), V((A * S, CQ, 16), F32),
            pltpu.SemaphoreType.DMA((cin,)),
            pltpu.SemaphoreType.DMA((18 + 2 * S,)),
            pltpu.SemaphoreType.DMA((10 + S,)), pltpu.SemaphoreType.DMA((10 + S + A * B // 2 + A * S // 2,)),
        ],
        compiler_params=pltpu.CompilerParams(
            collective_id=0, has_side_effects=True, vmem_limit_bytes=60 * 1024 * 1024
        ),
    )(*operands)


def solution(mesh):
    A = mesh.shape["gx"]
    B = mesh.shape["gy"]
    in_specs = (
        P(None, "gx", "gy", None), P(), P(), P(("gx", "gy"), None, None, None, None), P(), P(),
        P(("gx", "gy"), None, None, None, None), P(), P(), P(), P(),
    )
    return jax.shard_map(
        functools.partial(on_device, A, B), mesh=mesh, in_specs=in_specs,
        out_specs=P(None, "gx", "gy", None), check_vma=False,
    )
```

```python
import functools
import math

import jax
import jax.numpy as jnp
import numpy as np
from jax import lax
from jax.experimental import pallas as pl
from jax.experimental.pallas import tpu as pltpu
from jax.sharding import PartitionSpec as P

KX = 16
KY = 16
KZ = 8
YB = 8
LB = 128
GROUP = 4
FINE = 16
F32 = jnp.float32
BF16 = jnp.bfloat16
MESH = pl.DeviceIdType.MESH
ROOT = math.sqrt(0.5)


def freq(count):
    f = np.arange(count)
    return np.where(f < count // 2, f, f - count)


def halves(table):
    high = table.astype(np.float32).astype(jnp.bfloat16)
    low = (table - high.astype(np.float64)).astype(np.float32).astype(jnp.bfloat16)
    return np.stack([high, low])


def stacked(table):
    high, low = halves(table)
    return np.concatenate([high, high, low], axis=0)


def angles(places, frequency, length):
    turns = np.mod(places[:, None] * frequency[None, :], length)
    return turns * (2.0 * math.pi / length)


def z_table(z_length):
    ang = angles(np.arange(z_length), np.arange(KZ), z_length)
    table = np.zeros((YB, z_length, 2, YB, KZ))
    for y in range(YB):
        table[y, :, 0, y] = np.cos(ang)
        table[y, :, 1, y] = -np.sin(ang)
    return table.reshape(YB * z_length, LB)


def y_table(blocks, cells, length, groups):
    per = KY // groups
    frequency = freq(KY)
    out = np.zeros((blocks, cells // YB, 2, YB, KZ, groups, LB))
    for b in range(blocks):
        ang = angles(b * cells + np.arange(cells), frequency, length)
        for y in range(cells):
            for j in range(KY):
                c, s = np.cos(ang[y, j]), np.sin(ang[y, j])
                for k in range(KZ):
                    re = (j % per) * KZ + k
                    im = per * KZ + re
                    at = (b, y // YB)
                    out[at + (0, y % YB, k, j // per, re)] = c
                    out[at + (1, y % YB, k, j // per, re)] = s
                    out[at + (0, y % YB, k, j // per, im)] = -s
                    out[at + (1, y % YB, k, j // per, im)] = c
    return out.reshape(blocks, cells // YB * LB, groups * LB)


def x_angles(blocks, cells, length):
    return angles(np.arange(blocks * cells), freq(KX), length).reshape(blocks, cells, KX)


def split(value):
    high = value.astype(BF16)
    return high, (value - high.astype(F32)).astype(BF16)


def mul(a, b):
    return jnp.dot(a, b, preferred_element_type=F32)


def tall(a):
    return jnp.concatenate([a[0], a[1], a[0]], axis=1)


def deep(a):
    return jnp.concatenate([a[0], a[1], a[0]], axis=0)


def wide(a):
    return jnp.concatenate([a[0], a[0], a[1]], axis=1)


def mul3(a, b):
    return mul(a[0], b[0]) + (mul(a[1], b[0]) + mul(a[0], b[1]))


def wide_rows(a):
    return jnp.concatenate([a[0], a[0], a[1]], axis=0)


def left3(table, b):
    rows = table[0].shape[0]
    both = mul(jnp.concatenate([table[0], table[1]], axis=0), b[0])
    return both[:rows] + (both[rows:] + mul(table[0], b[1]))


def bend(v):
    return v * (1.0 + lax.erf(v))


def parts_of(A, H, channels):
    parts = 1
    while H % (2 * parts) == 0 and channels % (16 * parts * A) == 0:
        parts *= 2
    return parts


def kernel(
    A, B, cells_x, cells_y, scale1, scale2, gain,
    f_hbm, lift_hbm, lbias_hbm, byp_hbm, bi_hbm, wo_hbm, bo_hbm, pr_hbm, pb_hbm, tzf_hbm, tzi_hbm, w1_hbm, w2_hbm, tx_hbm, yf1_hbm, yfc_hbm, yic_hbm, yi2_hbm, xf_hbm, xi_hbm, xo_hbm,
    o_ref,
    fx, f_ref, lift_ref, lbias_ref, byp_ref, bi_ref, wo_ref, bo_ref, pr_ref, pb_ref, tzf_ref, os_ref,
    tzi_ref, w1, w2, tx, yf1, yfc, yic, yi2, xf, xi, xo,
    buf1, r1, mx, mt1, g1, lines, yall, pg, pk_ref, lw, ones, ye, vx, zc, vn, buf2, r3, ag2, vf, nar, fk_ref, t16, bd, bpq,
    fsem, csem, ssem, rsem,
):
    a = lax.axis_index("gx")
    b = lax.axis_index("gy")
    me = a * B + b
    IL = KX // A
    H = B // IL
    J = KY // H
    N = A * B
    X = A // 2
    CIN, C1 = lift_ref.shape
    C2 = wo_ref.shape[1]
    S = parts_of(A, H, C2)
    CQ = C2 // (A * S)
    CG = CQ // 8
    hx = cells_x // 2
    HX = hx * A
    G1 = GROUP * C2 // CQ
    part = lax.rem(b, S)
    base = b - part
    core = lax.rem(a, 2)
    sib = a + 1 - 2 * core

    def flip(t):
        value = b
        bit = 1
        while bit < B:
            if t & bit:
                value = value + bit - 2 * bit * lax.rem(b // bit, 2)
            bit *= 2
        return value

    lines_b = [flip(t) for t in range(B)]
    lines_a = [lax.rem(a + ia, A) for ia in range(A)]
    peers = [(lines_a[ia], lines_b[t]) for t in reversed(range(B)) for ia in reversed(range(A)) if t or ia]

    fields = [pltpu.make_async_copy(f_hbm.at[c], fx.at[:, c], fsem.at[c]) for c in range(CIN)]
    pairs = [
        (tzf_hbm, tzf_ref), (tx_hbm.at[a], tx), (yf1_hbm.at[b], yf1), (lift_hbm, lift_ref), (lbias_hbm, lbias_ref),
        (byp_hbm, byp_ref), (bi_hbm, bi_ref), (wo_hbm, wo_ref), (bo_hbm, bo_ref), (pr_hbm, pr_ref), (pb_hbm, pb_ref),
        (w1_hbm, w1), (xi_hbm, xi), (tzi_hbm, tzi_ref), (xf_hbm, xf), (w2_hbm, w2), (yi2_hbm.at[b], yi2), (xo_hbm.at[a], xo),
    ] + [(yic_hbm.at[base + n], yic.at[n]) for n in range(S)] + [(yfc_hbm.at[base + n], yfc.at[n]) for n in range(S)]
    loads = [pltpu.make_async_copy(src, dst, csem.at[k]) for k, (src, dst) in enumerate(pairs)]
    l_tzf, l_tx, l_yf1 = loads[:3]
    l_w1, l_xi, l_tzi, l_xf, l_w2, l_yi2, l_xo = loads[11:18]
    for load in fields + loads[:3]:
        load.start()

    barrier = pltpu.get_barrier_semaphore()
    for pa, pb in peers:
        pl.semaphore_signal(barrier, inc=1, device_id=(pa, pb), device_id_type=MESH)
    for load in loads[3:]:
        load.start()

    lane = lax.broadcasted_iota(jnp.int32, (1, LB), 1)
    sign_f = jnp.where(lane < LB // 2, 1.0, -1.0).astype(F32)

    def rot_f(v):
        return pltpu.roll(v, LB // 2, 1) * sign_f

    def rot_i(v):
        return pltpu.roll(v, LB // 2, 1) * -sign_f

    def remote(source, target, phase, slot, device):
        pltpu.make_async_remote_copy(
            src_ref=source, dst_ref=target, send_sem=ssem.at[phase], recv_sem=rsem.at[slot],
            device_id=device, device_id_type=MESH,
        ).start()

    def whole(target, phase, slot):
        return pltpu.make_async_remote_copy(
            src_ref=target, dst_ref=target, send_sem=ssem.at[phase], recv_sem=rsem.at[slot],
            device_id=(sib, b), device_id_type=MESH,
        )

    def arrive(target, slot):
        whole(target, 0, slot).wait_recv()

    A2A, EXP1, RED, EXP2, LINE_PAIR, POOL, POOL_X, POOL_Y, POOL_XY, POOL_LAST, LINE = range(11)
    SPREAD = LINE + S
    NEAR = SPREAD + X * B

    width = tzi_ref.shape[1]
    for load in fields:
        load.wait()
    flat = fx.reshape(f_ref.shape[0] * cells_y, f_ref.shape[1] // cells_y)
    zn = flat.shape[1]
    for y in range(cells_y):
        f_ref[:, y * zn:(y + 1) * zn] = flat[pl.ds(y, f_ref.shape[0], stride=cells_y), :]
    l_tzf.wait()
    def wave(pair):
        both = mul(pair[0], tzf_ref[...])
        return both[:, :LB] + (both[:, LB:] + mul(pair[1], tzf_ref[:, :LB]))

    zs = wave(split(jnp.concatenate([f_ref[:, :width], f_ref[:, width:]], axis=0)))
    zs = [zs[:zs.shape[0] // 2], zs[zs.shape[0] // 2:]]
    l_tx.wait()
    us = []
    for z in zs:
        us.append(mul3((tx[0], tx[1]), split(jnp.concatenate([z, rot_f(z)], axis=0))))
    l_yf1.wait()
    parts = mul3(split(jnp.concatenate(us, axis=1)), (yf1[0], yf1[1]))
    for i in range(KX):
        for h in range(H):
            buf1[i * H + h] = parts[i * CIN:(i + 1) * CIN, h * LB:(h + 1) * LB]
    r1[me] = buf1[me]
    pl.semaphore_wait(barrier, N - 1)

    for pa, pb in peers:
        remote(buf1.at[pa * B + pb], r1.at[me], A2A, A2A, (pa, pb))

    for x in range(hx):
        both = f_ref[2 * x * CIN:(2 * x + 1) * CIN] + f_ref[(2 * x + 1) * CIN:(2 * x + 2) * CIN]
        pieces = [
            both[:, 2 * y * zn:(2 * y + 1) * zn] + both[:, (2 * y + 1) * zn:(2 * y + 2) * zn]
            for y in range(YB)
        ]
        pg[a * S + part, x * CIN:(x + 1) * CIN] = jnp.concatenate(pieces, axis=1) * 0.25

    def near_slot(phase, step):
        return NEAR + (phase - LINE) * X + step

    square = X == 2 and S == 2
    mate = lax.rem(a + 2, A)
    other = S - 1 - part

    def share_send(buffer):
        own = buffer.at[a * S + part]
        if square:
            remote(own, own, POOL, POOL_X, (mate, b))
            remote(own, own, POOL, POOL_Y, (a, base + other))
            remote(own, own, POOL, POOL, (sib, b))
        else:
            for ia in range(A):
                for turn in range(S):
                    if ia or turn:
                        remote(own, own, POOL, POOL, (lax.rem(a + ia, A), base + member(turn)))

    def share_relay(buffer):
        if square:
            left = buffer.at[mate * S + part]
            right = buffer.at[a * S + other]
            arrive(left, POOL_X)
            arrive(right, POOL_Y)
            ia = a * core + mate * (1 - core)
            ip = other * core + part * (1 - core)
            target = (mate * core + a * (1 - core), b * core + (base + other) * (1 - core))
            relayed = buffer.at[ia * S + ip]
            remote(relayed, relayed, POOL, POOL_XY, target)
            remote(left, left, POOL, POOL, (sib, b))
            remote(right, right, POOL, POOL, (sib, b))

    def share_last(buffer):
        if square:
            corner = buffer.at[mate * S + other]
            arrive(corner, POOL_XY)
            remote(corner, corner, POOL, POOL_LAST, (sib, b))

    def share_finish(buffer):
        arrive(buffer.at[pl.ds(0, A * S // 2 - 1 if square else A * S - 1)], POOL)

    def member(turn):
        return lax.rem(part + turn, S)

    def pair_finish(buffer, phase):
        if S > 1:
            arrive(buffer.at[0, pl.ds(0, S - 1)], phase)

    def near_send(buffer, phase, turn):
        own = buffer.at[a, member(turn)]
        for step in range(1, X):
            remote(own, own, phase + turn, near_slot(phase + turn, step), (lax.rem(a + 2 * step, A), b))
        remote(own, own, phase + turn, phase + turn, (sib, b))

    def near_forward(buffer, phase, turn):
        for step in range(1, X):
            other = buffer.at[lax.rem(a + A - 2 * step, A), member(turn)]
            arrive(other, near_slot(phase + turn, step))
            remote(other, other, phase + turn, phase + turn, (sib, b))

    def near_finish(buffer, phase, turn):
        arrive(buffer.at[pl.ds(0, X), 0], phase + turn)

    share_send(pg)

    for load in loads[3:12]:
        load.wait()
    mx[...] = jnp.zeros_like(mx)
    mx[0:CIN, :C1] = lift_ref[...]
    mx[CIN:CIN + 1, :C1] = lbias_ref[...]
    mx[CIN + 1:CIN + 2, :C1] = bo_ref[...]
    lift8 = jnp.concatenate([mx[0:8, :C1]], axis=0)
    columns = mx[...].T[:C1]
    bo_col = columns[:, CIN + 1:CIN + 2] * ROOT

    def left16(matrix, bias):
        n = matrix.shape[1]
        high, low = split(matrix[0:CIN])
        b0 = bias.astype(BF16)
        rest = bias - b0.astype(F32)
        b1 = rest.astype(BF16)
        b2 = (rest - b1.astype(F32)).astype(BF16)
        mx[...] = jnp.zeros_like(mx)
        mx[0:CIN, :n] = high.astype(F32)
        mx[CIN:2 * CIN, :n] = high.astype(F32)
        mx[2 * CIN:3 * CIN, :n] = low.astype(F32)
        for row, value in enumerate((b0, b1, b2)):
            mx[3 * CIN + row:3 * CIN + row + 1, :n] = value.astype(F32)
        return mx[...].T[:n, :16].astype(BF16)

    highest = lax.Precision.HIGHEST
    eighth = lax.broadcasted_iota(jnp.int32, (1, ones.shape[1]), 1) // 8
    m = jnp.dot(lift8, byp_ref[...], precision=highest, preferred_element_type=F32)
    bp16 = left16(m * ROOT, (m[CIN:CIN + 1] + bi_ref[...]) * ROOT)
    m = lax.dot_general(
        lift8, pr_ref[...], (((1,), (1,)), ((), ())), precision=highest, preferred_element_type=F32
    )
    pl16 = left16(m, m[CIN:CIN + 1] + pb_ref[...])
    t16[...] = jnp.ones_like(t16)

    def diagonal(value, count):
        rows, cols = value.shape
        bd[...] = jnp.zeros_like(bd)
        for g in range(count):
            bd[g * rows:(g + 1) * rows, g * cols:(g + 1) * cols] = value
        return bd[0:count * rows, 0:count * cols]

    bp_all = bp16.astype(F32)
    for q in range(A * S):
        bpq[q] = bp_all[q * CQ:(q + 1) * CQ]
    bq_bd = diagonal(bpq[a * S + part], min(G1, 16)).astype(BF16)
    bp_bd = diagonal(bp_all, GROUP).astype(BF16)
    pl_bd = diagonal(pl16.astype(F32), FINE).astype(BF16)
    wo_bd = wide(split(diagonal(wo_ref[...] * 0.5, GROUP)))
    pr_bd = split(diagonal(pr_ref[...] * ROOT, FINE))
    Q = J * KZ
    lifts = tall(split(lift8))
    for j in range(J):
        for k in range(KZ):
            both = []
            for n in range(2):
                both.append(mul(lifts, wide_rows(split(w1[j, n, k]))))
            lw[0, j * KZ + k] = jnp.concatenate([both[0], both[1]], axis=1)
            lw[1, j * KZ + k] = jnp.concatenate([-both[1], both[0]], axis=1)
    for row in range(Q):
        ones[row:row + 1] = jnp.where(eighth == row, 1.0, 0.0).astype(F32)
    blocks = ones[...].astype(BF16)
    arrive(r1.at[pl.ds(0, N - 1)], A2A)

    s4 = jnp.sum(r1[...], axis=0) * scale1
    first = jnp.where((lane == 0) & (me == 0), gain, 0.0).astype(F32)
    mx[...] = jnp.zeros_like(mx)
    mx[0:CIN] = s4
    mx[CIN:CIN + 1] = first
    s8 = mx[0:8]
    mixed = split(jnp.concatenate(
        [s8[:, q:q + 1] * lw[0, q] + s8[:, Q + q:Q + q + 1] * lw[1, q] for q in range(Q)], axis=0
    ))
    mx[0:Q] = mul(blocks, mixed[0]) + mul(blocks, mixed[1])
    turned = mx[...].T
    mixed = turned[:C2] + pltpu.roll(turned[C2:], Q, 1)
    for q in range(A * S):
        mt1[q] = mixed[q * CQ:(q + 1) * CQ]
    g1[me] = mt1[a * S + part]
    for pa, pb in peers:
        remote(mt1.at[pa * S + lax.rem(pb, S)], g1.at[me], EXP1, EXP1, (pa, pb))

    def fill(value):
        n = value.shape[1]
        high, low = split(value)
        t16[0:CIN, :n] = high.astype(F32)
        t16[CIN:2 * CIN, :n] = low.astype(F32)
        t16[2 * CIN:3 * CIN, :n] = high.astype(F32)
        return t16[:, :n].astype(BF16)

    def fill_pooled(ia, ip):
        for x in range(hx):
            pk_ref[ip * HX + ia * hx + x] = fill(pg[ia * S + ip, x * CIN:(x + 1) * CIN])

    share_relay(pg)
    for x in range(cells_x):
        fk_ref[x] = fill(f_ref[x * CIN:(x + 1) * CIN])
    if square:
        fill_pooled(a, part)
        fill_pooled(mate, part)
        fill_pooled(a, other)
        share_finish(pg)
        fill_pooled(sib, part)
        fill_pooled(lax.rem(sib + 2, A), part)
        fill_pooled(sib, other)
        share_last(pg)
        fill_pooled(mate, other)
    for load in loads[18:18 + S]:
        load.wait()
    arrive(g1.at[pl.ds(0, N - 1)], EXP1)
    rows = jnp.concatenate(
        [jnp.concatenate([g1[i * H + h] for h in range(H)], axis=1) for i in range(KX)], axis=0
    )
    tables = tuple(jnp.concatenate([yic[n, k] for n in range(S)], axis=1) for k in range(2))
    y = mul3(split(rows), tables)
    for n in range(S):
        for i in range(KX):
            lines[n, i] = y[i * CQ:(i + 1) * CQ, n * LB:(n + 1) * LB]
    for turn in range(1, S):
        remote(lines.at[member(turn)], yall.at[a, part], LINE_PAIR, LINE_PAIR, (a, base + member(turn)))
    for i in range(KX):
        yall[a, part, i] = lines[part, i]
    near_send(yall, LINE, 0)

    def modes(value, rows_each):
        groups = rows_each // 8
        turned = rot_i(value)
        parts = []
        for g in range(groups):
            parts.append(jnp.concatenate([
                v[i * rows_each + g * 8:i * rows_each + g * 8 + 8] for v in (value, turned) for i in range(KX)
            ], axis=0))
        return parts

    l_xi.wait()
    table = tuple(jnp.concatenate([xi[q, k] for q in range(A)], axis=0) for k in range(2))
    halves_y = []
    for n in range(S):
        halves_y += modes(y[:, n * LB:(n + 1) * LB], CQ)
    v = left3(table, split(jnp.concatenate(halves_y, axis=1)))
    steps = HX // G1
    for n in range(S):
        for s in range(steps):
            vx[n * steps + s] = jnp.concatenate([
                v[(s * G1 + xx) * 8:(s * G1 + xx) * 8 + 8, (n * CG + g) * LB:(n * CG + g + 1) * LB]
                for xx in range(G1) for g in range(CG)
            ], axis=0)

    def coarse_step(s, carry):
        v = mul(tall(split(vx[s])), tzi_ref[...])
        count = min(G1, 16)
        near = jnp.concatenate([
            mul(bq_bd, jnp.concatenate([pk_ref[s * G1 + g + xx] for xx in range(count)], axis=0))
            for g in range(0, G1, count)
        ], axis=0)
        g = split(bend(v + near))
        zc[s] = wave(g)
        return carry

    if square:
        arrive(pg.at[lax.rem(sib + 2, A) * S + other], POOL_LAST)
        fill_pooled(lax.rem(sib + 2, A), other)
    else:
        share_finish(pg)
        for ia in range(A):
            for ip in range(S):
                fill_pooled(ia, ip)
    l_tzi.wait()
    lax.fori_loop(0, S * steps, coarse_step, 0, unroll=True)

    l_xf.wait()
    for load in loads[18 + S:]:
        load.wait()
    z = jnp.concatenate([
        jnp.concatenate([
            zc[n * steps + s, xx * CQ + g * 8:xx * CQ + g * 8 + 8] for s in range(steps) for xx in range(G1)
        ], axis=0) for n in range(S) for g in range(CG)
    ], axis=1)
    z = mul(wide((xf[0], xf[1])), deep(split(z)))

    def spectrum(first, n):
        return jnp.concatenate([
            z[(first + i) * 8:(first + i + 1) * 8, (n * CG + g) * LB:(n * CG + g + 1) * LB]
            for i in range(KX) for g in range(CG)
        ], axis=0)

    value = jnp.concatenate([spectrum(0, n) + rot_f(spectrum(KX, n)) for n in range(S)], axis=1)
    tables = tuple(jnp.concatenate([yfc[n, k] for n in range(S)], axis=0) for k in range(2))
    out = mul3(split(value), tables)
    for i in range(KX):
        for h in range(H):
            buf2[i * H + h] = out[i * CQ:(i + 1) * CQ, h * LB:(h + 1) * LB]
    for pa, pb in peers:
        remote(buf2.at[pa * B + pb], r3.at[me], RED, RED, (pa, pb))
    r3[me] = buf2[me]

    pair_finish(yall, LINE_PAIR)
    for turn in range(1, S):
        near_send(yall, LINE, turn)
    near_forward(yall, LINE, 0)
    l_w2.wait()
    arrive(r3.at[pl.ds(0, N - 1)], RED)
    for turn in range(1, S):
        near_forward(yall, LINE, turn)
    sums = []
    for q in range(A):
        for n in range(S):
            total = r3[q * B + n]
            for t in range(S + n, B, S):
                total = total + r3[q * B + t]
            sums.append(total)
    st = (jnp.concatenate(sums, axis=0) * scale2).T
    mixed = jnp.zeros((C1, LB), F32)
    for j in range(J):
        for k in range(KZ):
            q = j * KZ + k
            re = st[q:q + 1]
            im = st[Q + q:Q + q + 1]
            wr = w2[j, 0, k]
            wi = w2[j, 1, k]
            real = jnp.sum(re * wr - im * wi, axis=1, keepdims=True)
            imag = jnp.sum(re * wi + im * wr, axis=1, keepdims=True)
            mixed = jnp.where(lane == q, real, jnp.where(lane == Q + q, imag, mixed))
    ag2[me] = mixed

    NEARBY = B // 2

    def spread(t):
        source = a * B + flip(t)
        for step in range(1, X):
            remote(
                ag2.at[source], ag2.at[source], EXP2, SPREAD + step * B + t, (lax.rem(a + 2 * step, A), b)
            )
            if t >= NEARBY:
                remote(ag2.at[source], ag2.at[source], EXP2, EXP2, (lax.rem(sib + 2 * step, A), b))
        remote(ag2.at[source], ag2.at[source], EXP2, EXP2, (sib, b))

    for t in range(B - 1, 0, -1):
        remote(ag2.at[me], ag2.at[me], EXP2, SPREAD + t, (a, flip(t)))
    spread(0)
    for t in range(1, B):
        source = a * B + flip(t)
        arrive(ag2.at[source], SPREAD + t)
        spread(t)
    for turn in range(S):
        near_finish(yall, LINE, turn)
    parts = []
    for q in range(A):
        for n in range(S):
            parts += modes(jnp.concatenate([yall[q, n, i] for i in range(KX)], axis=0), CQ)
    v = left3((xi[a, 0], xi[a, 1]), split(jnp.concatenate(parts, axis=1)))
    for s in range(hx // GROUP):
        vn[s] = jnp.concatenate([
            v[(s * GROUP + xx) * 8:(s * GROUP + xx) * 8 + 8, g * LB:(g + 1) * LB]
            for xx in range(GROUP) for g in range(C2 // 8)
        ], axis=0)

    def narrow_step(s, carry):
        v = mul(tall(split(vn[s])), tzi_ref[...])
        near = jnp.concatenate([pk_ref[part * HX + a * hx + s * GROUP + xx] for xx in range(GROUP)], axis=0)
        g = split(bend(v + mul(bp_bd, near)))
        narrow = mul(wo_bd, deep(g))
        for xx in range(GROUP):
            nar[s * GROUP + xx] = narrow[xx * C1:(xx + 1) * C1] + bo_col
        return carry

    lax.fori_loop(0, hx // GROUP, narrow_step, 0, unroll=True)

    def expand(ia):
        rows = jnp.concatenate([
            jnp.concatenate([ag2[(ia * IL + g) * H + h] for h in range(H)], axis=1) for g in range(IL)
        ], axis=0)
        ye[ia] = mul3(split(rows), (yi2[0], yi2[1]))

    l_yi2.wait()
    expand(a)
    for t in range(B):
        for step in range(1, X):
            source = lax.rem(a + A - 2 * step, A) * B + flip(t)
            arrive(ag2.at[source], SPREAD + step * B + t)
            if t < NEARBY:
                remote(ag2.at[source], ag2.at[source], EXP2, EXP2, (sib, b))
    for step in range(1, X):
        expand(lax.rem(a + 2 * step, A))
    arrive(ag2.at[pl.ds(0, X * B)], EXP2)

    for ia in [sib] + [lax.rem(sib + 2 * step, A) for step in range(1, X)]:
        expand(ia)
    l_xo.wait()
    y = jnp.concatenate([ye[ia] for ia in range(A)], axis=0)
    halves_y = [modes(y[:, ch * LB:(ch + 1) * LB], C1) for ch in range(2)]
    v = left3((xo[0], xo[1]), split(jnp.concatenate(halves_y[0] + halves_y[1], axis=1)))
    CF = C1 // 8
    for s in range(cells_x // FINE):
        for ch in range(2):
            vf[s, ch] = jnp.concatenate([
                v[(s * FINE + xx) * 8:(s * FINE + xx) * 8 + 8, (ch * CF + g) * LB:(ch * CF + g + 1) * LB]
                for xx in range(FINE) for g in range(CF)
            ], axis=0)

    def fine_step(group, carry):
        near = jnp.concatenate([fk_ref[group * FINE + xx] for xx in range(FINE)], axis=0)
        for ch in range(2):
            v = mul(tall(split(vf[group, ch])), tzi_ref[...])
            rows = []
            for xx in range(0, FINE, 2):
                half = nar.at[group * (FINE // 2) + xx // 2]
                pieces = []
                for yy in range(YB):
                    at_y = (ch * YB + yy) // 2 * zn
                    pieces.append(half[:, at_y:at_y + zn])
                rows += [jnp.concatenate(pieces, axis=1)] * 2
            g = split(bend(v + jnp.concatenate(rows, axis=0)))
            cols = slice(ch * width, (ch + 1) * width)
            res = left3(pr_bd, g) + mul(pl_bd, near[:, cols])
            for yy in range(YB):
                os_ref[ch, yy * FINE * CIN:(yy + 1) * FINE * CIN] = res[:, yy * zn:(yy + 1) * zn]
            for xx in range(FINE):
                for c in range(CIN):
                    o_ref[c, group * FINE + xx, ch * YB:(ch + 1) * YB] = os_ref[
                        ch, pl.ds(xx * CIN + c, YB, stride=FINE * CIN), :
                    ]
        return carry

    lax.fori_loop(0, cells_x // FINE, fine_step, 0, unroll=True)
    waits = [
        (A2A, buf1.at[pl.ds(0, N - 1)]), (EXP1, g1.at[pl.ds(0, N - 1)]), (RED, buf2.at[pl.ds(0, N - 1)]),
        (EXP2, ag2.at[pl.ds(0, N - 1)]),
    ]
    if S > 1:
        waits.append((LINE_PAIR, yall.at[0, pl.ds(0, S - 1)]))
    waits.append((POOL, pg.at[pl.ds(0, A * S - 1)]))
    for turn in range(S):
        waits.append((LINE + turn, yall.at[pl.ds(0, A - 1), 0]))
    for phase, target in waits:
        whole(target, phase, phase).wait_send()


def on_device(
    A, B, fields, lift, lift_bias, spectral_in, bypass_in, bias_in, spectral_out, bypass_out,
    bias_out, proj, proj_bias,
):
    cin, xc, yc, zc = fields.shape
    C1 = lift.shape[0]
    C2 = bypass_in.shape[0]
    NX = xc * A
    NY = yc * B
    IL = KX // A
    H = B // IL
    J = KY // H
    N = A * B
    width = YB * zc
    S = parts_of(A, H, C2)
    CQ = C2 // (A * S)
    hx = xc // 2
    HX = hx * A
    G1 = GROUP * C2 // CQ
    cells = float(NX * NY * zc)
    back = math.sqrt(2.0 / (KX * KY * KZ))

    tz = z_table(zc)
    tzf = np.concatenate(list(halves(tz)), axis=1)
    tzi = stacked(np.ascontiguousarray(tz.T) * (back * ROOT))
    fine_x = x_angles(A, xc, NX)
    half_x = x_angles(A, xc // 2, NX // 2)
    eye = np.eye(cin)
    tx = np.stack([
        np.concatenate([np.kron(np.cos(fine_x[i].T), eye), np.kron(np.sin(fine_x[i].T), eye)], axis=1)
        for i in range(A)
    ])
    eye8 = np.eye(8)

    def lines(ang):
        return np.concatenate([np.kron(np.cos(ang), eye8), np.kron(np.sin(ang), eye8)], axis=1)

    xi = np.stack([lines(half_x[i]) for i in range(A)])
    xf = np.ascontiguousarray(xi.reshape(-1, xi.shape[2]).T)
    xo = np.stack([lines(fine_x[i]) for i in range(A)])
    yf1 = y_table(B, yc, NY, H)
    yfc = y_table(B, yc // 2, NY // 2, H)

    def per_device(table):
        return jnp.asarray(np.ascontiguousarray(np.swapaxes(halves(table), 0, 1)))

    tx_t = per_device(tx)
    yf1_t = per_device(yf1)
    yfc_t = per_device(yfc)
    yic_t = per_device(np.swapaxes(yfc, 1, 2))
    yi2_t = per_device(np.swapaxes(yf1, 1, 2))
    xi_t = per_device(xi)
    xo_t = per_device(xo)
    xf_t = jnp.asarray(halves(xf))

    weights2 = jnp.swapaxes(spectral_out, 3, 4)

    operands = [
        fields, lift.T, lift_bias[None], bypass_in.T, bias_in[None], bypass_out, bias_out[None], proj,
        proj_bias[None], jnp.asarray(tzf),
        jnp.asarray(tzi), spectral_in, weights2, tx_t, yf1_t, yfc_t, yic_t, yi2_t, xf_t, xi_t, xo_t,
    ]
    anywhere = pl.BlockSpec(memory_space=pl.ANY)
    V = pltpu.VMEM
    return pl.pallas_call(
        functools.partial(
            kernel, A, B, xc, yc, 1.0 / math.sqrt(cells), ROOT / math.sqrt(cells / 4.0), math.sqrt(cells)
        ),
        out_shape=pltpu.VMEM((cin, xc, yc, zc), F32),
        in_specs=[anywhere] * len(operands),
        out_specs=pl.BlockSpec(memory_space=pltpu.VMEM),
        scratch_shapes=[
            V((xc, cin, yc, zc), F32), V((xc * cin, yc * zc), F32),
        ] + [V(v.shape, v.dtype) for v in operands[1:10]] + [
            V((2, YB * FINE * cin, zc), F32),
            V(tzi.shape, BF16), V(spectral_in.shape, F32), V(weights2.shape, F32),
            V(tx_t.shape[1:], BF16), V(yf1_t.shape[1:], BF16), V((S,) + yfc_t.shape[1:], BF16),
            V((S,) + yic_t.shape[1:], BF16), V(yi2_t.shape[1:], BF16), V(xf_t.shape, BF16), V(xi_t.shape, BF16),
            V(xo_t.shape[1:], BF16),
            V((N, cin, LB), F32), V((N, cin, LB), F32), V((LB, LB), F32),
            V((A * S, CQ, LB), F32), V((N, CQ, LB), F32), V((S, KX, CQ, LB), F32), V((A, S, KX, CQ, LB), F32),
            V((A * S, hx * cin, width), F32), V((S * HX, 16, width), BF16),
            V((2, J * KZ, 8, 2 * C2), F32), V((J * KZ, J * KZ * 8), F32), V((A, IL * C1, 2 * LB), F32),
            V((S * HX // G1, G1 * CQ, LB), F32), V((S * HX // G1, G1 * CQ, LB), F32), V((hx // GROUP, GROUP * C2, LB), F32),
            V((N, CQ, LB), F32), V((N, CQ, LB), F32), V((N, C1, LB), F32),
            V((xc // FINE, 2, FINE * C1, LB), F32),
            V((hx, C1, width), F32), V((xc, 16, yc * zc), BF16), V((16, yc * zc), F32),
            V((GROUP * C2, max(GROUP * C2, FINE * C1)), F32), V((A * S, CQ, 16), F32),
            pltpu.SemaphoreType.DMA((cin,)),
            pltpu.SemaphoreType.DMA((18 + 2 * S,)),
            pltpu.SemaphoreType.DMA((10 + S,)), pltpu.SemaphoreType.DMA((10 + S + A * B // 2 + A * S // 2,)),
        ],
        compiler_params=pltpu.CompilerParams(
            collective_id=0, has_side_effects=True, vmem_limit_bytes=60 * 1024 * 1024
        ),
    )(*operands)


def solution(mesh):
    A = mesh.shape["gx"]
    B = mesh.shape["gy"]
    in_specs = (
        P(None, "gx", "gy", None), P(), P(), P(("gx", "gy"), None, None, None, None), P(), P(),
        P(("gx", "gy"), None, None, None, None), P(), P(), P(), P(),
    )
    return jax.shard_map(
        functools.partial(on_device, A, B), mesh=mesh, in_specs=in_specs,
        out_specs=P(None, "gx", "gy", None), check_vma=False,
    )
```

```python
import functools
import math

import jax
import jax.numpy as jnp
import numpy as np
from jax import lax
from jax.experimental import pallas as pl
from jax.experimental.pallas import tpu as pltpu
from jax.sharding import PartitionSpec as P

KX = 16
KY = 16
KZ = 8
YB = 8
LB = 128
GROUP = 4
FINE = 16
F32 = jnp.float32
BF16 = jnp.bfloat16
MESH = pl.DeviceIdType.MESH
ROOT = math.sqrt(0.5)


def freq(count):
    f = np.arange(count)
    return np.where(f < count // 2, f, f - count)


def halves(table):
    high = table.astype(np.float32).astype(jnp.bfloat16)
    low = (table - high.astype(np.float64)).astype(np.float32).astype(jnp.bfloat16)
    return np.stack([high, low])


def stacked(table):
    high, low = halves(table)
    return np.concatenate([high, high, low], axis=0)


def angles(places, frequency, length):
    turns = np.mod(places[:, None] * frequency[None, :], length)
    return turns * (2.0 * math.pi / length)


def z_table(z_length):
    ang = angles(np.arange(z_length), np.arange(KZ), z_length)
    table = np.zeros((YB, z_length, 2, YB, KZ))
    for y in range(YB):
        table[y, :, 0, y] = np.cos(ang)
        table[y, :, 1, y] = -np.sin(ang)
    return table.reshape(YB * z_length, LB)


def y_table(blocks, cells, length, groups):
    per = KY // groups
    frequency = freq(KY)
    out = np.zeros((blocks, cells // YB, 2, YB, KZ, groups, LB))
    for b in range(blocks):
        ang = angles(b * cells + np.arange(cells), frequency, length)
        for y in range(cells):
            for j in range(KY):
                c, s = np.cos(ang[y, j]), np.sin(ang[y, j])
                for k in range(KZ):
                    re = (j % per) * KZ + k
                    im = per * KZ + re
                    at = (b, y // YB)
                    out[at + (0, y % YB, k, j // per, re)] = c
                    out[at + (1, y % YB, k, j // per, re)] = s
                    out[at + (0, y % YB, k, j // per, im)] = -s
                    out[at + (1, y % YB, k, j // per, im)] = c
    return out.reshape(blocks, cells // YB * LB, groups * LB)


def x_angles(blocks, cells, length):
    return angles(np.arange(blocks * cells), freq(KX), length).reshape(blocks, cells, KX)


def split(value):
    high = value.astype(BF16)
    return high, (value - high.astype(F32)).astype(BF16)


def mul(a, b):
    return jnp.dot(a, b, preferred_element_type=F32)


def tall(a):
    return jnp.concatenate([a[0], a[1], a[0]], axis=1)


def deep(a):
    return jnp.concatenate([a[0], a[1], a[0]], axis=0)


def wide(a):
    return jnp.concatenate([a[0], a[0], a[1]], axis=1)


def mul3(a, b):
    return mul(a[0], b[0]) + (mul(a[1], b[0]) + mul(a[0], b[1]))


def wide_rows(a):
    return jnp.concatenate([a[0], a[0], a[1]], axis=0)


def left3(table, b):
    rows = table[0].shape[0]
    both = mul(jnp.concatenate([table[0], table[1]], axis=0), b[0])
    return both[:rows] + (both[rows:] + mul(table[0], b[1]))


def bend(v):
    return v * (1.0 + lax.erf(v))


def parts_of(A, H, channels):
    parts = 1
    while H % (2 * parts) == 0 and channels % (16 * parts * A) == 0:
        parts *= 2
    return parts


def kernel(
    A, B, cells_x, cells_y, scale1, scale2, gain,
    f_hbm, lift_hbm, lbias_hbm, byp_hbm, bi_hbm, wo_hbm, bo_hbm, pr_hbm, pb_hbm, tzf_hbm, tzi_hbm, w1_hbm, w2_hbm, tx_hbm, yf1_hbm, yfc_hbm, yic_hbm, yi2_hbm, xf_hbm, xi_hbm, xo_hbm,
    o_ref,
    fx, f_ref, lift_ref, lbias_ref, byp_ref, bi_ref, wo_ref, bo_ref, pr_ref, pb_ref, tzf_ref, os_ref,
    tzi_ref, w1, w2, tx, yf1, yfc, yic, yi2, xf, xi, xo,
    buf1, r1, mx, mt1, g1, lines, yall, pg, pk_ref, lw, ones, ye, vx, zc, vn, buf2, r3, ag2, vf, nar, fk_ref, t16, bd, bpq,
    fsem, csem, ssem, rsem,
):
    a = lax.axis_index("gx")
    b = lax.axis_index("gy")
    me = a * B + b
    IL = KX // A
    H = B // IL
    J = KY // H
    N = A * B
    X = A // 2
    CIN, C1 = lift_ref.shape
    C2 = wo_ref.shape[1]
    S = parts_of(A, H, C2)
    CQ = C2 // (A * S)
    CG = CQ // 8
    hx = cells_x // 2
    HX = hx * A
    G1 = GROUP * C2 // CQ
    part = lax.rem(b, S)
    base = b - part
    core = lax.rem(a, 2)
    sib = a + 1 - 2 * core

    def flip(t):
        value = b
        bit = 1
        while bit < B:
            if t & bit:
                value = value + bit - 2 * bit * lax.rem(b // bit, 2)
            bit *= 2
        return value

    lines_b = [flip(t) for t in range(B)]
    lines_a = [lax.rem(a + ia, A) for ia in range(A)]
    peers = [(lines_a[ia], lines_b[t]) for t in reversed(range(B)) for ia in reversed(range(A)) if t or ia]

    fields = [pltpu.make_async_copy(f_hbm.at[c], fx.at[:, c], fsem.at[c]) for c in range(CIN)]
    pairs = [
        (tzf_hbm, tzf_ref), (tx_hbm.at[a], tx), (yf1_hbm.at[b], yf1), (lift_hbm, lift_ref), (lbias_hbm, lbias_ref),
        (byp_hbm, byp_ref), (bi_hbm, bi_ref), (wo_hbm, wo_ref), (bo_hbm, bo_ref), (pr_hbm, pr_ref), (pb_hbm, pb_ref),
        (w1_hbm, w1), (xi_hbm, xi), (tzi_hbm, tzi_ref), (xf_hbm, xf), (w2_hbm, w2), (yi2_hbm.at[b], yi2), (xo_hbm.at[a], xo),
    ] + [(yic_hbm.at[base + n], yic.at[n]) for n in range(S)] + [(yfc_hbm.at[base + n], yfc.at[n]) for n in range(S)]
    loads = [pltpu.make_async_copy(src, dst, csem.at[k]) for k, (src, dst) in enumerate(pairs)]
    l_tzf, l_tx, l_yf1 = loads[:3]
    l_w1, l_xi, l_tzi, l_xf, l_w2, l_yi2, l_xo = loads[11:18]
    for load in fields + loads[:3]:
        load.start()

    barrier = pltpu.get_barrier_semaphore()
    for pa, pb in peers:
        pl.semaphore_signal(barrier, inc=1, device_id=(pa, pb), device_id_type=MESH)
    for load in loads[3:]:
        load.start()

    lane = lax.broadcasted_iota(jnp.int32, (1, LB), 1)
    sign_f = jnp.where(lane < LB // 2, 1.0, -1.0).astype(F32)

    def rot_f(v):
        return pltpu.roll(v, LB // 2, 1) * sign_f

    def rot_i(v):
        return pltpu.roll(v, LB // 2, 1) * -sign_f

    def remote(source, target, phase, slot, device):
        pltpu.make_async_remote_copy(
            src_ref=source, dst_ref=target, send_sem=ssem.at[phase], recv_sem=rsem.at[slot],
            device_id=device, device_id_type=MESH,
        ).start()

    def whole(target, phase, slot):
        return pltpu.make_async_remote_copy(
            src_ref=target, dst_ref=target, send_sem=ssem.at[phase], recv_sem=rsem.at[slot],
            device_id=(sib, b), device_id_type=MESH,
        )

    def arrive(target, slot):
        whole(target, 0, slot).wait_recv()

    A2A, EXP1, RED, EXP2, LINE_PAIR, POOL, POOL_X, POOL_Y, POOL_XY, POOL_LAST, LINE = range(11)
    SPREAD = LINE + S
    NEAR = SPREAD + X * B

    width = tzi_ref.shape[1]
    for load in fields:
        load.wait()
    flat = fx.reshape(f_ref.shape[0] * cells_y, f_ref.shape[1] // cells_y)
    zn = flat.shape[1]
    for y in range(cells_y):
        f_ref[:, y * zn:(y + 1) * zn] = flat[pl.ds(y, f_ref.shape[0], stride=cells_y), :]
    l_tzf.wait()
    def wave(pair):
        both = mul(pair[0], tzf_ref[...])
        return both[:, :LB] + (both[:, LB:] + mul(pair[1], tzf_ref[:, :LB]))

    zs = wave(split(jnp.concatenate([f_ref[:, :width], f_ref[:, width:]], axis=0)))
    zs = [zs[:zs.shape[0] // 2], zs[zs.shape[0] // 2:]]
    l_tx.wait()
    us = []
    for z in zs:
        us.append(mul3((tx[0], tx[1]), split(jnp.concatenate([z, rot_f(z)], axis=0))))
    l_yf1.wait()
    parts = mul3(split(jnp.concatenate(us, axis=1)), (yf1[0], yf1[1]))
    for i in range(KX):
        for h in range(H):
            buf1[i * H + h] = parts[i * CIN:(i + 1) * CIN, h * LB:(h + 1) * LB]
    r1[me] = buf1[me]
    pl.semaphore_wait(barrier, N - 1)

    for pa, pb in peers:
        remote(buf1.at[pa * B + pb], r1.at[me], A2A, A2A, (pa, pb))

    for x in range(hx):
        both = f_ref[2 * x * CIN:(2 * x + 1) * CIN] + f_ref[(2 * x + 1) * CIN:(2 * x + 2) * CIN]
        pieces = [
            both[:, 2 * y * zn:(2 * y + 1) * zn] + both[:, (2 * y + 1) * zn:(2 * y + 2) * zn]
            for y in range(YB)
        ]
        pg[a * S + part, x * CIN:(x + 1) * CIN] = jnp.concatenate(pieces, axis=1) * 0.25

    def near_slot(phase, step):
        return NEAR + (phase - LINE) * X + step

    square = X == 2 and S == 2
    mate = lax.rem(a + 2, A)
    other = S - 1 - part

    def share_send(buffer):
        own = buffer.at[a * S + part]
        if square:
            remote(own, own, POOL, POOL_X, (mate, b))
            remote(own, own, POOL, POOL_Y, (a, base + other))
            remote(own, own, POOL, POOL, (sib, b))
        else:
            for ia in range(A):
                for turn in range(S):
                    if ia or turn:
                        remote(own, own, POOL, POOL, (lax.rem(a + ia, A), base + member(turn)))

    def share_relay(buffer):
        if square:
            left = buffer.at[mate * S + part]
            right = buffer.at[a * S + other]
            arrive(left, POOL_X)
            arrive(right, POOL_Y)
            ia = a * core + mate * (1 - core)
            ip = other * core + part * (1 - core)
            target = (mate * core + a * (1 - core), b * core + (base + other) * (1 - core))
            relayed = buffer.at[ia * S + ip]
            remote(relayed, relayed, POOL, POOL_XY, target)
            remote(left, left, POOL, POOL, (sib, b))
            remote(right, right, POOL, POOL, (sib, b))

    def share_last(buffer):
        if square:
            corner = buffer.at[mate * S + other]
            arrive(corner, POOL_XY)
            remote(corner, corner, POOL, POOL_LAST, (sib, b))

    def share_finish(buffer):
        arrive(buffer.at[pl.ds(0, A * S // 2 - 1 if square else A * S - 1)], POOL)

    def member(turn):
        return lax.rem(part + turn, S)

    def pair_finish(buffer, phase):
        if S > 1:
            arrive(buffer.at[0, pl.ds(0, S - 1)], phase)

    def near_send(buffer, phase, turn):
        own = buffer.at[a, member(turn)]
        for step in range(1, X):
            remote(own, own, phase + turn, near_slot(phase + turn, step), (lax.rem(a + 2 * step, A), b))
        remote(own, own, phase + turn, phase + turn, (sib, b))

    def near_forward(buffer, phase, turn):
        for step in range(1, X):
            other = buffer.at[lax.rem(a + A - 2 * step, A), member(turn)]
            arrive(other, near_slot(phase + turn, step))
            remote(other, other, phase + turn, phase + turn, (sib, b))

    def near_finish(buffer, phase, turn):
        arrive(buffer.at[pl.ds(0, X), 0], phase + turn)

    share_send(pg)

    for load in loads[3:12]:
        load.wait()
    mx[...] = jnp.zeros_like(mx)
    mx[0:CIN, :C1] = lift_ref[...]
    mx[CIN:CIN + 1, :C1] = lbias_ref[...]
    mx[CIN + 1:CIN + 2, :C1] = bo_ref[...]
    lift8 = jnp.concatenate([mx[0:8, :C1]], axis=0)
    columns = mx[...].T[:C1]
    bo_col = columns[:, CIN + 1:CIN + 2] * ROOT

    def left16(matrix, bias):
        n = matrix.shape[1]
        high, low = split(matrix[0:CIN])
        b0 = bias.astype(BF16)
        rest = bias - b0.astype(F32)
        b1 = rest.astype(BF16)
        b2 = (rest - b1.astype(F32)).astype(BF16)
        mx[...] = jnp.zeros_like(mx)
        mx[0:CIN, :n] = high.astype(F32)
        mx[CIN:2 * CIN, :n] = high.astype(F32)
        mx[2 * CIN:3 * CIN, :n] = low.astype(F32)
        for row, value in enumerate((b0, b1, b2)):
            mx[3 * CIN + row:3 * CIN + row + 1, :n] = value.astype(F32)
        return mx[...].T[:n, :16].astype(BF16)

    highest = lax.Precision.HIGHEST
    eighth = lax.broadcasted_iota(jnp.int32, (1, ones.shape[1]), 1) // 8
    m = jnp.dot(lift8, byp_ref[...], precision=highest, preferred_element_type=F32)
    bp16 = left16(m * ROOT, (m[CIN:CIN + 1] + bi_ref[...]) * ROOT)
    m = lax.dot_general(
        lift8, pr_ref[...], (((1,), (1,)), ((), ())), precision=highest, preferred_element_type=F32
    )
    pl16 = left16(m, m[CIN:CIN + 1] + pb_ref[...])
    t16[...] = jnp.ones_like(t16)

    def diagonal(value, count):
        rows, cols = value.shape
        bd[...] = jnp.zeros_like(bd)
        for g in range(count):
            bd[g * rows:(g + 1) * rows, g * cols:(g + 1) * cols] = value
        return bd[0:count * rows, 0:count * cols]

    bp_all = bp16.astype(F32)
    for q in range(A * S):
        bpq[q] = bp_all[q * CQ:(q + 1) * CQ]
    bq_bd = diagonal(bpq[a * S + part], min(G1, 16)).astype(BF16)
    bp_bd = diagonal(bp_all, GROUP).astype(BF16)
    pl_bd = diagonal(pl16.astype(F32), FINE).astype(BF16)
    wo_bd = wide(split(diagonal(wo_ref[...] * 0.5, GROUP)))
    pr_bd = split(diagonal(pr_ref[...] * ROOT, FINE))
    Q = J * KZ
    lifts = tall(split(lift8))
    for j in range(J):
        for k in range(KZ):
            both = []
            for n in range(2):
                both.append(mul(lifts, wide_rows(split(w1[j, n, k]))))
            lw[0, j * KZ + k] = jnp.concatenate([both[0], both[1]], axis=1)
            lw[1, j * KZ + k] = jnp.concatenate([-both[1], both[0]], axis=1)
    for row in range(Q):
        ones[row:row + 1] = jnp.where(eighth == row, 1.0, 0.0).astype(F32)
    blocks = ones[...].astype(BF16)
    arrive(r1.at[pl.ds(0, N - 1)], A2A)

    s4 = jnp.sum(r1[...], axis=0) * scale1
    first = jnp.where((lane == 0) & (me == 0), gain, 0.0).astype(F32)
    mx[...] = jnp.zeros_like(mx)
    mx[0:CIN] = s4
    mx[CIN:CIN + 1] = first
    s8 = mx[0:8]
    mixed = split(jnp.concatenate(
        [s8[:, q:q + 1] * lw[0, q] + s8[:, Q + q:Q + q + 1] * lw[1, q] for q in range(Q)], axis=0
    ))
    mx[0:Q] = mul(blocks, mixed[0]) + mul(blocks, mixed[1])
    turned = mx[...].T
    mixed = turned[:C2] + pltpu.roll(turned[C2:], Q, 1)
    for q in range(A * S):
        mt1[q] = mixed[q * CQ:(q + 1) * CQ]
    g1[me] = mt1[a * S + part]
    for pa, pb in peers:
        remote(mt1.at[pa * S + lax.rem(pb, S)], g1.at[me], EXP1, EXP1, (pa, pb))

    def fill(value):
        n = value.shape[1]
        high, low = split(value)
        t16[0:CIN, :n] = high.astype(F32)
        t16[CIN:2 * CIN, :n] = low.astype(F32)
        t16[2 * CIN:3 * CIN, :n] = high.astype(F32)
        return t16[:, :n].astype(BF16)

    def fill_pooled(ia, ip):
        for x in range(hx):
            pk_ref[ip * HX + ia * hx + x] = fill(pg[ia * S + ip, x * CIN:(x + 1) * CIN])

    share_relay(pg)
    for x in range(cells_x):
        fk_ref[x] = fill(f_ref[x * CIN:(x + 1) * CIN])
    if square:
        fill_pooled(a, part)
        fill_pooled(mate, part)
        fill_pooled(a, other)
        share_finish(pg)
        fill_pooled(sib, part)
        fill_pooled(lax.rem(sib + 2, A), part)
        fill_pooled(sib, other)
        share_last(pg)
        fill_pooled(mate, other)
    for load in loads[18:18 + S]:
        load.wait()
    arrive(g1.at[pl.ds(0, N - 1)], EXP1)
    rows = jnp.concatenate(
        [jnp.concatenate([g1[i * H + h] for h in range(H)], axis=1) for i in range(KX)], axis=0
    )
    tables = tuple(jnp.concatenate([yic[n, k] for n in range(S)], axis=1) for k in range(2))
    y = mul3(split(rows), tables)
    for n in range(S):
        for i in range(KX):
            lines[n, i] = y[i * CQ:(i + 1) * CQ, n * LB:(n + 1) * LB]
    for turn in range(1, S):
        remote(lines.at[member(turn)], yall.at[a, part], LINE_PAIR, LINE_PAIR, (a, base + member(turn)))
    for i in range(KX):
        yall[a, part, i] = lines[part, i]
    near_send(yall, LINE, 0)

    def modes(value, rows_each):
        groups = rows_each // 8
        turned = rot_i(value)
        parts = []
        for g in range(groups):
            parts.append(jnp.concatenate([
                v[i * rows_each + g * 8:i * rows_each + g * 8 + 8] for v in (value, turned) for i in range(KX)
            ], axis=0))
        return parts

    l_xi.wait()
    table = tuple(jnp.concatenate([xi[q, k] for q in range(A)], axis=0) for k in range(2))
    halves_y = []
    for n in range(S):
        halves_y += modes(y[:, n * LB:(n + 1) * LB], CQ)
    v = left3(table, split(jnp.concatenate(halves_y, axis=1)))
    steps = HX // G1
    for n in range(S):
        for s in range(steps):
            vx[n * steps + s] = jnp.concatenate([
                v[(s * G1 + xx) * 8:(s * G1 + xx) * 8 + 8, (n * CG + g) * LB:(n * CG + g + 1) * LB]
                for xx in range(G1) for g in range(CG)
            ], axis=0)

    def coarse_step(s, carry):
        v = mul(tall(split(vx[s])), tzi_ref[...])
        count = min(G1, 16)
        near = jnp.concatenate([
            mul(bq_bd, jnp.concatenate([pk_ref[s * G1 + g + xx] for xx in range(count)], axis=0))
            for g in range(0, G1, count)
        ], axis=0)
        g = split(bend(v + near))
        zc[s] = wave(g)
        return carry

    if square:
        arrive(pg.at[lax.rem(sib + 2, A) * S + other], POOL_LAST)
        fill_pooled(lax.rem(sib + 2, A), other)
    else:
        share_finish(pg)
        for ia in range(A):
            for ip in range(S):
                fill_pooled(ia, ip)
    l_tzi.wait()
    lax.fori_loop(0, S * steps, coarse_step, 0, unroll=True)

    l_xf.wait()
    for load in loads[18 + S:]:
        load.wait()
    z = jnp.concatenate([
        jnp.concatenate([
            zc[n * steps + s, xx * CQ + g * 8:xx * CQ + g * 8 + 8] for s in range(steps) for xx in range(G1)
        ], axis=0) for n in range(S) for g in range(CG)
    ], axis=1)
    z = mul(wide((xf[0], xf[1])), deep(split(z)))

    def spectrum(first, n):
        return jnp.concatenate([
            z[(first + i) * 8:(first + i + 1) * 8, (n * CG + g) * LB:(n * CG + g + 1) * LB]
            for i in range(KX) for g in range(CG)
        ], axis=0)

    value = jnp.concatenate([spectrum(0, n) + rot_f(spectrum(KX, n)) for n in range(S)], axis=1)
    tables = tuple(jnp.concatenate([yfc[n, k] for n in range(S)], axis=0) for k in range(2))
    out = mul3(split(value), tables)
    for i in range(KX):
        for h in range(H):
            buf2[i * H + h] = out[i * CQ:(i + 1) * CQ, h * LB:(h + 1) * LB]
    for pa, pb in peers:
        remote(buf2.at[pa * B + pb], r3.at[me], RED, RED, (pa, pb))
    r3[me] = buf2[me]

    pair_finish(yall, LINE_PAIR)
    for turn in range(1, S):
        near_send(yall, LINE, turn)
    near_forward(yall, LINE, 0)
    l_w2.wait()
    arrive(r3.at[pl.ds(0, N - 1)], RED)
    for turn in range(1, S):
        near_forward(yall, LINE, turn)
    sums = []
    for q in range(A):
        for n in range(S):
            total = r3[q * B + n]
            for t in range(S + n, B, S):
                total = total + r3[q * B + t]
            sums.append(total)
    st = (jnp.concatenate(sums, axis=0) * scale2).T
    mixed = jnp.zeros((C1, LB), F32)
    for j in range(J):
        for k in range(KZ):
            q = j * KZ + k
            re = st[q:q + 1]
            im = st[Q + q:Q + q + 1]
            wr = w2[j, 0, k]
            wi = w2[j, 1, k]
            real = jnp.sum(re * wr - im * wi, axis=1, keepdims=True)
            imag = jnp.sum(re * wi + im * wr, axis=1, keepdims=True)
            mixed = jnp.where(lane == q, real, jnp.where(lane == Q + q, imag, mixed))
    ag2[me] = mixed

    NEARBY = 3 * B // 4

    def spread(t):
        source = a * B + flip(t)
        for step in range(1, X):
            remote(
                ag2.at[source], ag2.at[source], EXP2, SPREAD + step * B + t, (lax.rem(a + 2 * step, A), b)
            )
            if t >= NEARBY:
                remote(ag2.at[source], ag2.at[source], EXP2, EXP2, (lax.rem(sib + 2 * step, A), b))
        remote(ag2.at[source], ag2.at[source], EXP2, EXP2, (sib, b))

    for t in range(B - 1, 0, -1):
        remote(ag2.at[me], ag2.at[me], EXP2, SPREAD + t, (a, flip(t)))
    spread(0)
    for t in range(1, B):
        source = a * B + flip(t)
        arrive(ag2.at[source], SPREAD + t)
        spread(t)
    for turn in range(S):
        near_finish(yall, LINE, turn)
    parts = []
    for q in range(A):
        for n in range(S):
            parts += modes(jnp.concatenate([yall[q, n, i] for i in range(KX)], axis=0), CQ)
    v = left3((xi[a, 0], xi[a, 1]), split(jnp.concatenate(parts, axis=1)))
    for s in range(hx // GROUP):
        vn[s] = jnp.concatenate([
            v[(s * GROUP + xx) * 8:(s * GROUP + xx) * 8 + 8, g * LB:(g + 1) * LB]
            for xx in range(GROUP) for g in range(C2 // 8)
        ], axis=0)

    def narrow_step(s, carry):
        v = mul(tall(split(vn[s])), tzi_ref[...])
        near = jnp.concatenate([pk_ref[part * HX + a * hx + s * GROUP + xx] for xx in range(GROUP)], axis=0)
        g = split(bend(v + mul(bp_bd, near)))
        narrow = mul(wo_bd, deep(g))
        for xx in range(GROUP):
            nar[s * GROUP + xx] = narrow[xx * C1:(xx + 1) * C1] + bo_col
        return carry

    lax.fori_loop(0, hx // GROUP, narrow_step, 0, unroll=True)

    def expand(ia):
        rows = jnp.concatenate([
            jnp.concatenate([ag2[(ia * IL + g) * H + h] for h in range(H)], axis=1) for g in range(IL)
        ], axis=0)
        ye[ia] = mul3(split(rows), (yi2[0], yi2[1]))

    l_yi2.wait()
    expand(a)
    for t in range(B):
        for step in range(1, X):
            source = lax.rem(a + A - 2 * step, A) * B + flip(t)
            arrive(ag2.at[source], SPREAD + step * B + t)
            if t < NEARBY:
                remote(ag2.at[source], ag2.at[source], EXP2, EXP2, (sib, b))
    for step in range(1, X):
        expand(lax.rem(a + 2 * step, A))
    arrive(ag2.at[pl.ds(0, X * B)], EXP2)

    for ia in [sib] + [lax.rem(sib + 2 * step, A) for step in range(1, X)]:
        expand(ia)
    l_xo.wait()
    y = jnp.concatenate([ye[ia] for ia in range(A)], axis=0)
    halves_y = [modes(y[:, ch * LB:(ch + 1) * LB], C1) for ch in range(2)]
    v = left3((xo[0], xo[1]), split(jnp.concatenate(halves_y[0] + halves_y[1], axis=1)))
    CF = C1 // 8
    for s in range(cells_x // FINE):
        for ch in range(2):
            vf[s, ch] = jnp.concatenate([
                v[(s * FINE + xx) * 8:(s * FINE + xx) * 8 + 8, (ch * CF + g) * LB:(ch * CF + g + 1) * LB]
                for xx in range(FINE) for g in range(CF)
            ], axis=0)

    def fine_step(group, carry):
        near = jnp.concatenate([fk_ref[group * FINE + xx] for xx in range(FINE)], axis=0)
        for ch in range(2):
            v = mul(tall(split(vf[group, ch])), tzi_ref[...])
            rows = []
            for xx in range(0, FINE, 2):
                half = nar.at[group * (FINE // 2) + xx // 2]
                pieces = []
                for yy in range(YB):
                    at_y = (ch * YB + yy) // 2 * zn
                    pieces.append(half[:, at_y:at_y + zn])
                rows += [jnp.concatenate(pieces, axis=1)] * 2
            g = split(bend(v + jnp.concatenate(rows, axis=0)))
            cols = slice(ch * width, (ch + 1) * width)
            res = left3(pr_bd, g) + mul(pl_bd, near[:, cols])
            for yy in range(YB):
                os_ref[ch, yy * FINE * CIN:(yy + 1) * FINE * CIN] = res[:, yy * zn:(yy + 1) * zn]
            for xx in range(FINE):
                for c in range(CIN):
                    o_ref[c, group * FINE + xx, ch * YB:(ch + 1) * YB] = os_ref[
                        ch, pl.ds(xx * CIN + c, YB, stride=FINE * CIN), :
                    ]
        return carry

    lax.fori_loop(0, cells_x // FINE, fine_step, 0, unroll=True)
    waits = [
        (A2A, buf1.at[pl.ds(0, N - 1)]), (EXP1, g1.at[pl.ds(0, N - 1)]), (RED, buf2.at[pl.ds(0, N - 1)]),
        (EXP2, ag2.at[pl.ds(0, N - 1)]),
    ]
    if S > 1:
        waits.append((LINE_PAIR, yall.at[0, pl.ds(0, S - 1)]))
    waits.append((POOL, pg.at[pl.ds(0, A * S - 1)]))
    for turn in range(S):
        waits.append((LINE + turn, yall.at[pl.ds(0, A - 1), 0]))
    for phase, target in waits:
        whole(target, phase, phase).wait_send()


def on_device(
    A, B, fields, lift, lift_bias, spectral_in, bypass_in, bias_in, spectral_out, bypass_out,
    bias_out, proj, proj_bias,
):
    cin, xc, yc, zc = fields.shape
    C1 = lift.shape[0]
    C2 = bypass_in.shape[0]
    NX = xc * A
    NY = yc * B
    IL = KX // A
    H = B // IL
    J = KY // H
    N = A * B
    width = YB * zc
    S = parts_of(A, H, C2)
    CQ = C2 // (A * S)
    hx = xc // 2
    HX = hx * A
    G1 = GROUP * C2 // CQ
    cells = float(NX * NY * zc)
    back = math.sqrt(2.0 / (KX * KY * KZ))

    tz = z_table(zc)
    tzf = np.concatenate(list(halves(tz)), axis=1)
    tzi = stacked(np.ascontiguousarray(tz.T) * (back * ROOT))
    fine_x = x_angles(A, xc, NX)
    half_x = x_angles(A, xc // 2, NX // 2)
    eye = np.eye(cin)
    tx = np.stack([
        np.concatenate([np.kron(np.cos(fine_x[i].T), eye), np.kron(np.sin(fine_x[i].T), eye)], axis=1)
        for i in range(A)
    ])
    eye8 = np.eye(8)

    def lines(ang):
        return np.concatenate([np.kron(np.cos(ang), eye8), np.kron(np.sin(ang), eye8)], axis=1)

    xi = np.stack([lines(half_x[i]) for i in range(A)])
    xf = np.ascontiguousarray(xi.reshape(-1, xi.shape[2]).T)
    xo = np.stack([lines(fine_x[i]) for i in range(A)])
    yf1 = y_table(B, yc, NY, H)
    yfc = y_table(B, yc // 2, NY // 2, H)

    def per_device(table):
        return jnp.asarray(np.ascontiguousarray(np.swapaxes(halves(table), 0, 1)))

    tx_t = per_device(tx)
    yf1_t = per_device(yf1)
    yfc_t = per_device(yfc)
    yic_t = per_device(np.swapaxes(yfc, 1, 2))
    yi2_t = per_device(np.swapaxes(yf1, 1, 2))
    xi_t = per_device(xi)
    xo_t = per_device(xo)
    xf_t = jnp.asarray(halves(xf))

    weights2 = jnp.swapaxes(spectral_out, 3, 4)

    operands = [
        fields, lift.T, lift_bias[None], bypass_in.T, bias_in[None], bypass_out, bias_out[None], proj,
        proj_bias[None], jnp.asarray(tzf),
        jnp.asarray(tzi), spectral_in, weights2, tx_t, yf1_t, yfc_t, yic_t, yi2_t, xf_t, xi_t, xo_t,
    ]
    anywhere = pl.BlockSpec(memory_space=pl.ANY)
    V = pltpu.VMEM
    return pl.pallas_call(
        functools.partial(
            kernel, A, B, xc, yc, 1.0 / math.sqrt(cells), ROOT / math.sqrt(cells / 4.0), math.sqrt(cells)
        ),
        out_shape=pltpu.VMEM((cin, xc, yc, zc), F32),
        in_specs=[anywhere] * len(operands),
        out_specs=pl.BlockSpec(memory_space=pltpu.VMEM),
        scratch_shapes=[
            V((xc, cin, yc, zc), F32), V((xc * cin, yc * zc), F32),
        ] + [V(v.shape, v.dtype) for v in operands[1:10]] + [
            V((2, YB * FINE * cin, zc), F32),
            V(tzi.shape, BF16), V(spectral_in.shape, F32), V(weights2.shape, F32),
            V(tx_t.shape[1:], BF16), V(yf1_t.shape[1:], BF16), V((S,) + yfc_t.shape[1:], BF16),
            V((S,) + yic_t.shape[1:], BF16), V(yi2_t.shape[1:], BF16), V(xf_t.shape, BF16), V(xi_t.shape, BF16),
            V(xo_t.shape[1:], BF16),
            V((N, cin, LB), F32), V((N, cin, LB), F32), V((LB, LB), F32),
            V((A * S, CQ, LB), F32), V((N, CQ, LB), F32), V((S, KX, CQ, LB), F32), V((A, S, KX, CQ, LB), F32),
            V((A * S, hx * cin, width), F32), V((S * HX, 16, width), BF16),
            V((2, J * KZ, 8, 2 * C2), F32), V((J * KZ, J * KZ * 8), F32), V((A, IL * C1, 2 * LB), F32),
            V((S * HX // G1, G1 * CQ, LB), F32), V((S * HX // G1, G1 * CQ, LB), F32), V((hx // GROUP, GROUP * C2, LB), F32),
            V((N, CQ, LB), F32), V((N, CQ, LB), F32), V((N, C1, LB), F32),
            V((xc // FINE, 2, FINE * C1, LB), F32),
            V((hx, C1, width), F32), V((xc, 16, yc * zc), BF16), V((16, yc * zc), F32),
            V((GROUP * C2, max(GROUP * C2, FINE * C1)), F32), V((A * S, CQ, 16), F32),
            pltpu.SemaphoreType.DMA((cin,)),
            pltpu.SemaphoreType.DMA((18 + 2 * S,)),
            pltpu.SemaphoreType.DMA((10 + S,)), pltpu.SemaphoreType.DMA((10 + S + A * B // 2 + A * S // 2,)),
        ],
        compiler_params=pltpu.CompilerParams(
            collective_id=0, has_side_effects=True, vmem_limit_bytes=60 * 1024 * 1024
        ),
    )(*operands)


def solution(mesh):
    A = mesh.shape["gx"]
    B = mesh.shape["gy"]
    in_specs = (
        P(None, "gx", "gy", None), P(), P(), P(("gx", "gy"), None, None, None, None), P(), P(),
        P(("gx", "gy"), None, None, None, None), P(), P(), P(), P(),
    )
    return jax.shard_map(
        functools.partial(on_device, A, B), mesh=mesh, in_specs=in_specs,
        out_specs=P(None, "gx", "gy", None), check_vma=False,
    )
```
